32 devices in a mesh: dp: 8 (over y, x, core), mp: 4 (over z).
Axes of the slice: x: 2, y: 2, z: 4, core: 2. Of those that a mesh axis runs over, the one named last changes fastest.
Arguments:
- tokens: bfloat16 [16, 128, 4, 2048], P('dp', None, 'mp'), may hold values from -6 to 6
- segment_ids: int32 [16, 512], P('dp'), may hold values from 0 to 5, never falling along the last dimension, each value on 1 to 256 neighbouring positions
- image_blocks: int32 [16, 8], replicated, may hold values from 0 to 8, as said below
- features: bfloat16 [8, 256, 1024], P('dp'), may hold values from -6 to 6
- latent_queries: bfloat16 [64, 1024], P('dp', 'mp'), may hold values from -6 to 6
- image_kv_weight: bfloat16 [1024, 2, 1024], P('dp', None, 'mp'), may hold values from -0.1875 to 0.1875
- image_out_weight: bfloat16 [1024, 2048], P(('mp', 'dp')), may hold values from -1 to 1
- norm1_gain: bfloat16 [2048], replicated, may hold values from 0.5 to 1.5
- attn_in_weight: bfloat16 [2048, 3, 2048], P('dp', None, 'mp'), may hold values from -0.125 to 0.125
- attn_norm_gain: bfloat16 [2048], P(('mp', 'dp')), may hold values from 0.5 to 1.5
- attn_out_weight: bfloat16 [2048, 2048], P(('mp', 'dp')), may hold values from -0.125 to 0.125
- norm2_gain: bfloat16 [2048], replicated, may hold values from 0.5 to 1.5
- ffn_up_weight: bfloat16 [2048, 8192], P('dp', 'mp'), may hold values from -0.125 to 0.125
- ffn_norm_gain: bfloat16 [8192], P(('mp', 'dp')), may hold values from 0.5 to 1.5
- ffn_down_weight: bfloat16 [8192, 2048], P(('mp', 'dp')), may hold values from -0.0625 to 0.0625
- cotangent: bfloat16 [16, 128, 4, 2048], P('dp', None, 'mp'), may hold values from -6 to 6
Outputs:
- output: bfloat16 [16, 128, 4, 2048], P('dp', None, 'mp')
- tokens_grad: float32 [16, 128, 4, 2048], P('dp', None, 'mp')
- queries_grad: float32 [64, 1024], P('dp', 'mp')
- image_kv_grad: float32 [1024, 2, 1024], P('dp', None, 'mp')
- image_out_grad: float32 [1024, 2048], P(('mp', 'dp'))
- norm1_grad: float32 [2048], P(('mp', 'dp'))
- attn_in_grad: float32 [2048, 3, 2048], P('dp', None, 'mp')
- attn_norm_grad: float32 [2048], P(('mp', 'dp'))
- attn_out_grad: float32 [2048, 2048], P(('mp', 'dp'))
- norm2_grad: float32 [2048], P(('mp', 'dp'))
- ffn_up_grad: float32 [2048, 8192], P('dp', 'mp')
- ffn_norm_grad: float32 [8192], P(('mp', 'dp'))
- ffn_down_grad: float32 [8192, 2048], P(('mp', 'dp'))
The draws below stay inside these ranges and needn't reach their ends.
Inputs may be any that keep to these rules, and one draw needn't show every extreme that they name: `image_blocks`: each of the 8 images fills exactly one block of one row; every other block holds 8, meaning text. `segment_ids`: positions of a row with equal numbers form one document; numbers never fall along a row; a document has at most half of 512 positions.
All inputs are finite; a program needn't handle non-finite values.
Results may differ from the reference program's by a relative error of at most 0.03.
Values may be sent and summed in bfloat16 or wider, within the bound.
No kernel may reach another device: no remote copies, remote signals or barrier semaphores. Data moves between devices by JAX's collectives and lax.ppermute only.
A program may use at most 320 MiB of HBM per device.

```python
import math
import jax
import jax.numpy as jnp
import numpy as np
from jax import lax

D = 2048
HEADS = 32
HD = 64
FF = 8192
VD = 1024
LAT = 64
RHEADS = 16
PATCH = 256
L = 512
ROWS = 16
IMAGES = 8
NB = 8
LB = 128
N_MP = 4


def draw_image_blocks(key, part):
    order = jax.random.permutation(key, ROWS * NB)
    table = jnp.full((ROWS * NB,), IMAGES, dtype=jnp.int32)
    table = table.at[order[:IMAGES]].set(jnp.arange(IMAGES, dtype=jnp.int32))
    return table.reshape(ROWS, NB)


def levels(own_key, dims, cuts, low, largest):
    level = 1.0
    for axis_at, parts in cuts:
        draws = jax.random.uniform(jax.random.fold_in(jax.random.fold_in(own_key, 6), axis_at), (parts,), jnp.float32, low / len(cuts), largest / len(cuts))
        level = level * jnp.repeat(jnp.exp(draws), dims[axis_at] // parts).reshape((-1,) + (1,) * (len(dims) - 1 - axis_at))
    return level


def length_profile(amount, total, reach, slope):
    weights = [(1 << 20) // math.isqrt(grade ** slope) + 1 for grade in range(2, amount + 1)]
    surplus, holding = total - reach - (amount - 1), [1] * (amount - 1)
    while surplus > 0:
        movable = [i for i in range(amount - 1) if holding[i] < reach]
        whole, left = sum([weights[i] for i in movable]), surplus
        for i in movable:
            extra = min(reach - holding[i], max(1, left * weights[i] // whole), surplus)
            holding[i] = holding[i] + extra
            surplus = surplus - extra
    return np.array([reach] + holding)


def ragged(rng, number_of, total, limit, skew):
    if number_of == 2:
        one = jax.random.randint(rng, (), max(1, total - limit), min(limit, total - 1) + 1)
        return jnp.stack([one, total - one])
    tallies = jnp.asarray(length_profile(number_of, total, limit, skew), jnp.int32)
    pairs = (number_of - 1) // 2
    source_of, sink = tallies[1:1 + 2 * pairs:2], tallies[2:2 + 2 * pairs:2]
    room = jnp.minimum(source_of - 1, limit - sink)
    shifted = jax.random.randint(jax.random.fold_in(rng, 1), (pairs,), 0, 1 << 20) % (room + 1)
    tallies = tallies.at[1:1 + 2 * pairs:2].set(source_of - shifted).at[2:2 + 2 * pairs:2].set(sink + shifted)
    return tallies[jax.random.permutation(jax.random.fold_in(rng, 2), number_of)]


def noise(key, shape, deviation, reach, split=(), held_as=jnp.bfloat16):
    values = jax.random.normal(key, shape, jnp.float32) * deviation
    if len(split) > 0:
        values = levels(key, shape, split, -0.22, 0.18) * values
    return jnp.clip(values, min=-reach, max=reach).astype(held_as)


def setup_inputs(seed: int = 0) -> dict:
    key_of = jax.random.split(jax.random.key(seed), 17)
    tokens = noise(key_of[0], (ROWS, LB, N_MP, D), 1.0, 6.0, ((0, 8), (2, 4)))
    segment_ids = jax.vmap(lambda own: jnp.searchsorted(jnp.cumsum(ragged(own, 6, L, L // 2, 0)), jnp.arange(L), side="right"))(jax.random.split(key_of[1], ROWS)).reshape((ROWS, L)).astype(jnp.int32)
    image_blocks = draw_image_blocks(jax.random.fold_in(key_of[16], 71), 0)
    features = noise(key_of[3], (IMAGES, PATCH, VD), 1.0, 6.0, ((0, 8),))
    latent_queries = noise(key_of[4], (LAT, VD), 1.0, 6.0, ((0, 8), (1, 4)))
    image_kv_weight = noise(key_of[5], (VD, 2, VD), VD ** -0.5, 0.1875, ((0, 8), (2, 4)))
    image_out_weight = noise(key_of[6], (VD, D), (VD // 32) ** -0.5, 1.0, ((0, 32),))
    norm1_gain = jnp.clip(1.0 + 0.1 * jax.random.normal(key_of[7], (D,), jnp.float32), 0.5, 1.5).astype(jnp.bfloat16)
    attn_in_weight = noise(key_of[8], (D, 3, D), D ** -0.5, 0.125, ((0, 8), (2, 4)))
    attn_norm_gain = jnp.clip(1.0 + 0.1 * jax.random.normal(key_of[9], (D,), jnp.float32), 0.5, 1.5).astype(jnp.bfloat16)
    attn_out_weight = noise(key_of[10], (D, D), D ** -0.5, 0.125, ((0, 32),))
    norm2_gain = jnp.clip(1.0 + 0.1 * jax.random.normal(key_of[11], (D,), jnp.float32), 0.5, 1.5).astype(jnp.bfloat16)
    ffn_up_weight = noise(key_of[12], (D, FF), D ** -0.5, 0.125, ((0, 8), (1, 4)))
    ffn_norm_gain = jnp.clip(1.0 + 0.1 * jax.random.normal(key_of[13], (FF,), jnp.float32), 0.5, 1.5).astype(jnp.bfloat16)
    ffn_down_weight = noise(key_of[14], (FF, D), FF ** -0.5, 0.0625, ((0, 32),))
    cotangent = noise(key_of[15], (ROWS, LB, N_MP, D), 1.0, 6.0, ((0, 8), (2, 4)))
    return dict(tokens=tokens, segment_ids=segment_ids, image_blocks=image_blocks, features=features, latent_queries=latent_queries, image_kv_weight=image_kv_weight, image_out_weight=image_out_weight, norm1_gain=norm1_gain, attn_in_weight=attn_in_weight, attn_norm_gain=attn_norm_gain, attn_out_weight=attn_out_weight, norm2_gain=norm2_gain, ffn_up_weight=ffn_up_weight, ffn_norm_gain=ffn_norm_gain, ffn_down_weight=ffn_down_weight, cotangent=cotangent)


EPS = 1e-05
GAMMA = 0.4
SCALE_BASE = 512.0
NEG = -1e+30
HIGHEST = lax.Precision.HIGHEST

@jax.custom_vjp
def low(v):
    return lax.optimization_barrier(v.astype(jnp.bfloat16)).astype(jnp.float32)

@jax.custom_vjp
def low_back(v):
    return v

def low_keep(v):
    return (low(v), None)

def low_pass(kept, grad):
    return (grad,)

def back_keep(v):
    return (v, None)

def back_low(kept, grad):
    return (low(grad),)
low.defvjp(low_keep, low_pass)
low_back.defvjp(back_keep, back_low)

def norm_rows(values, gain):
    centre = values - lax.optimization_barrier(jnp.mean(values, axis=-1, keepdims=True))
    spread = lax.optimization_barrier(jnp.mean(centre * centre, axis=-1, keepdims=True))
    return centre * lax.rsqrt(spread + EPS) * gain

def doc_positions(segments):
    index = jnp.arange(segments.shape[0], dtype=jnp.int32)
    starts = jnp.concatenate([jnp.ones((1,), dtype=bool), segments[1:] != segments[:-1]])
    first = lax.cummax(jnp.where(starts, index, 0), axis=0)
    return (index - first).astype(jnp.float32)

def rotary_tables(places, head_size):
    half = head_size // 2
    steps = jnp.arange(half, dtype=jnp.float32)
    freqs = 10000.0 ** (-2.0 * steps / head_size)
    angles = places[:, None] * freqs[None, :]
    zeta = (2.0 * steps / head_size + GAMMA) / (1.0 + GAMMA)
    decay = jnp.exp(jnp.log(zeta)[None, :] * places[:, None] / SCALE_BASE)
    return (jnp.cos(angles), jnp.sin(angles), jnp.concatenate([decay, decay], axis=-1))

def rotate(values, cosine, sine):
    half = values.shape[-1] // 2
    first = values[..., :half]
    second = values[..., half:]
    cosine = cosine[:, None, :]
    sine = sine[:, None, :]
    return jnp.concatenate([first * cosine - second * sine, second * cosine + first * sine], axis=-1)

def text_row(start, segments, weights):
    norm1, attn_in, attn_gain, attn_out, norm2, ffn_up, ffn_gain, ffn_down = weights
    length = start.shape[0]
    ahead = low(start)
    normed1 = low(norm_rows(ahead, norm1))
    mixed = low_back(jnp.einsum('lc,ckd->lkd', normed1, attn_in, precision=HIGHEST))
    cosine, sine, decay = rotary_tables(doc_positions(segments), HD)
    decay = decay[:, None, :]
    query = low(rotate(mixed[:, 0].reshape(length, HEADS, HD), cosine, sine) * decay)
    key = low(rotate(mixed[:, 1].reshape(length, HEADS, HD), cosine, sine) / decay)
    value = low(mixed[:, 2].reshape(length, HEADS, HD))
    scores = low_back(jnp.einsum('qhd,khd->hqk', query, key, precision=HIGHEST) * HD ** (-0.5))
    index = jnp.arange(length, dtype=jnp.int32)
    allowed = (index[:, None] >= index[None, :]) & (segments[:, None] == segments[None, :])
    probs = low(jax.nn.softmax(jnp.where(allowed[None], scores, NEG), axis=-1))
    attended = low_back(jnp.einsum('hqk,khd->qhd', probs, value, precision=HIGHEST).reshape(length, D))
    sub_attn = low(norm_rows(attended, attn_gain))
    middle = start + low_back(jnp.dot(sub_attn, attn_out, precision=HIGHEST))
    second = low(middle)
    normed2 = low(norm_rows(second, norm2))
    hidden = low_back(jnp.dot(normed2, ffn_up, precision=HIGHEST))
    sub_ffn = low(norm_rows(jax.nn.gelu(hidden, approximate=False), ffn_gain))
    return middle + low_back(jnp.dot(sub_ffn, ffn_down, precision=HIGHEST))

def resample(features, queries, kv_weight, out_weight):
    images = features.shape[0]
    keyvals = low_back(low(jnp.einsum('ipc,ckd->ipkd', features, kv_weight, precision=HIGHEST)))
    keys = keyvals[:, :, 0].reshape(images, PATCH, RHEADS, HD)
    values = keyvals[:, :, 1].reshape(images, PATCH, RHEADS, HD)
    scores = low_back(jnp.einsum('lhd,iphd->ihlp', queries.reshape(LAT, RHEADS, HD), keys, precision=HIGHEST) * HD ** (-0.5))
    probs = low(jax.nn.softmax(scores, axis=-1))
    pooled = low_back(low(jnp.einsum('ihlp,iphd->ilhd', probs, values, precision=HIGHEST).reshape(images, LAT, VD)))
    return low_back(low(jnp.einsum('ilc,cd->ild', pooled, out_weight, precision=HIGHEST)))

def reference(tokens, segment_ids, image_blocks, features, latent_queries, image_kv_weight, image_out_weight, norm1_gain, attn_in_weight, attn_norm_gain, attn_out_weight, norm2_gain, ffn_up_weight, ffn_norm_gain, ffn_down_weight, cotangent):
    floats = tuple((array.astype(jnp.float32) for array in (tokens, features, latent_queries, image_kv_weight, image_out_weight, norm1_gain, attn_in_weight, attn_norm_gain, attn_out_weight, norm2_gain, ffn_up_weight, ffn_norm_gain, ffn_down_weight)))
    is_text = (image_blocks == IMAGES)[:, :, None, None]
    chosen = jnp.minimum(image_blocks, IMAGES - 1).astype(jnp.int32)

    def forward(tokens_f, features_f, queries, kv_weight, out_weight, norm1, attn_in, attn_gain, attn_out, norm2, ffn_up, ffn_gain, ffn_down):
        embeds = resample(features_f, queries, kv_weight, out_weight)
        picked = jnp.take(embeds, chosen, axis=0)
        flat = tokens_f.reshape(ROWS, NB, LAT, D)
        start = jnp.where(is_text, flat, picked).reshape(ROWS, L, D)
        weights = (norm1, attn_in, attn_gain, attn_out, norm2, ffn_up, ffn_gain, ffn_down)
        row_step = jax.checkpoint(lambda row, segs: text_row(row, segs, weights))
        return lax.map(lambda item: row_step(item[0], item[1]), (start, segment_ids))
    result, pullback = jax.vjp(forward, *floats)
    grads = pullback(cotangent.astype(jnp.float32).reshape(ROWS, L, D))
    output = result.reshape(ROWS, L // N_MP, N_MP, D).astype(jnp.bfloat16)
    tokens_grad = grads[0].reshape(ROWS, L // N_MP, N_MP, D)
    return (output, tokens_grad, grads[2], grads[3], grads[4], grads[5], grads[6], grads[7], grads[8], grads[9], grads[10], grads[11], grads[12])
```

```python
import jax
import jax.numpy as jnp
from jax import lax
from jax.sharding import PartitionSpec as P

D = 2048
HD = 64
FF = 8192


EPS = 1e-05
GAMMA = 0.4
SCALE_BASE = 512.0
NEG = -1e30
HIGHEST = lax.Precision.HIGHEST
ROOT_HALF = 0.7071067811865476
INV_ROOT_TAU = 0.3989422804014327


def doc_positions(segments):
    index = jnp.arange(segments.shape[0], dtype=jnp.int32)
    starts = jnp.concatenate([jnp.ones((1,), dtype=bool), segments[1:] != segments[:-1]])
    first = lax.cummax(jnp.where(starts, index, 0), axis=0)
    return (index - first).astype(jnp.float32)


def rotary_tables(places, head_size):
    half = head_size // 2
    steps = jnp.arange(half, dtype=jnp.float32)
    freqs = 10000.0 ** (-2.0 * steps / head_size)
    angles = places[:, None] * freqs[None, :]
    zeta = (2.0 * steps / head_size + GAMMA) / (1.0 + GAMMA)
    decay = jnp.exp(jnp.log(zeta)[None, :] * places[:, None] / SCALE_BASE)
    return (jnp.cos(angles), jnp.sin(angles), jnp.concatenate([decay, decay], axis=-1))


def rotate(values, cosine, sine):
    half = values.shape[-1] // 2
    first = values[..., :half]
    second = values[..., half:]
    cosine = cosine[:, None, :]
    sine = sine[:, None, :]
    return jnp.concatenate(
        [first * cosine - second * sine, second * cosine + first * sine], axis=-1
    )


def gelu_slope(values):
    return (
        0.5 * (1.0 + lax.erf(values * ROOT_HALF))
        + values * jnp.exp(-0.5 * values * values) * INV_ROOT_TAU
    )


def row_norm(values):
    centre = values - jnp.mean(values, axis=-1, keepdims=True)
    scale_back = lax.rsqrt(jnp.mean(centre * centre, axis=-1, keepdims=True) + EPS)
    return (centre * scale_back, scale_back)


def row_norm_back(grad_out, normed, scale_back, gain):
    scaled = grad_out * gain
    gain_grad = jnp.sum(grad_out * normed, axis=0)
    grad_in = scale_back * (
        scaled
        - jnp.mean(scaled, axis=-1, keepdims=True)
        - normed * jnp.mean(scaled * normed, axis=-1, keepdims=True)
    )
    return (grad_in, gain_grad)


def shift(values, step, size):
    return lax.ppermute(values, "mp", [(i, (i + step) % size) for i in range(size)])


def sum_slots(values, size):
    total = values
    for step in range(1, size):
        total = total + jnp.roll(shift(values, step, size), step, axis=-2)
    return total


def gather_slots(shard, size):
    if size != 4:
        return jnp.concatenate(
            [shard] + [shift(shard, step, size) for step in range(1, size)], axis=0
        )
    place = lax.axis_index("mp")
    across = lax.ppermute(shard, "mp", [(0, 2), (1, 3), (2, 0), (3, 1)])
    up = lax.ppermute(shard, "mp", [(0, 1), (1, 2), (2, 3)])
    down = lax.ppermute(shard, "mp", [(1, 0), (2, 1), (3, 2)])
    ends = lax.ppermute(across, "mp", [(2, 3), (1, 0)])
    first = jnp.where(place == 0, ends, up)
    third = jnp.where(place == 3, ends, down)
    return jnp.concatenate([shard, first, across, third], axis=0)


def scatter_slots(partial, size):
    rows = partial.shape[0] // size
    parts = [partial[k * rows : (k + 1) * rows] for k in range(size)]
    low = [part.astype(jnp.bfloat16) for part in parts]
    if size != 4:
        total = parts[0]
        for step in range(1, size):
            total = total + shift(low[step], size - step, size).astype(jnp.float32)
        return total
    place = lax.axis_index("mp")
    ends = lax.ppermute(jnp.where(place == 0, low[1], low[3]), "mp", [(0, 1), (3, 2)])
    down = lax.ppermute(low[1], "mp", [(1, 0), (2, 1), (3, 2)])
    up = lax.ppermute(low[3], "mp", [(0, 1), (1, 2), (2, 3)])
    across = lax.ppermute(
        (parts[2] + ends.astype(jnp.float32)).astype(jnp.bfloat16),
        "mp",
        [(0, 2), (1, 3), (2, 0), (3, 1)],
    )
    return (
        parts[0]
        + down.astype(jnp.float32)
        + up.astype(jnp.float32)
        + across.astype(jnp.float32)
    )


def split_norm(values, width, size):
    rows = values.shape[0]
    sums = jnp.stack([jnp.sum(values, axis=-1), jnp.sum(values * values, axis=-1)])
    sums = sum_slots(sums.reshape(2, size, rows // size), size).reshape(2, rows)
    mean = sums[0] / width
    scale_back = lax.rsqrt(sums[1] / width - mean * mean + EPS)
    return ((values - mean[:, None]) * scale_back[:, None], scale_back[:, None])


def split_norm_back(grad_out, normed, scale_back, gain, width, size):
    rows = grad_out.shape[0]
    scaled = grad_out * gain
    gain_grad = jnp.sum(grad_out * normed, axis=0)
    sums = jnp.stack([jnp.sum(scaled, axis=-1), jnp.sum(scaled * normed, axis=-1)])
    sums = sum_slots(sums.reshape(2, size, rows // size), size).reshape(2, rows) / width
    grad_in = scale_back * (scaled - sums[0][:, None] - normed * sums[1][:, None])
    return (grad_in, gain_grad)


def score_block(query, key, allowed, factor):
    scores = jnp.einsum("qhd,khd->hqk", query, key, preferred_element_type=jnp.float32) * factor
    return jnp.where(allowed[None], scores, NEG)


def attend_forward(query, key, value, allowed):
    factor = query.shape[2] ** (-0.5)
    scores = score_block(query, key, allowed, factor)
    peak = jnp.max(scores, axis=-1, keepdims=True)
    expo = jnp.exp(scores - peak)
    denom = jnp.sum(expo, axis=-1, keepdims=True)
    probs = (expo / denom).astype(jnp.bfloat16)
    outputs = jnp.einsum("hqk,khd->qhd", probs, value, preferred_element_type=jnp.float32)
    return (outputs, peak + jnp.log(denom))


def attend_backward(query, key, value, allowed, totals, grad_out):
    factor = query.shape[2] ** (-0.5)
    scores = score_block(query, key, allowed, factor)
    probs = jnp.where(allowed[None], jnp.exp(scores - totals), 0.0)
    grad_value = jnp.einsum(
        "hqk,qhd->khd", probs.astype(jnp.bfloat16), grad_out, preferred_element_type=jnp.float32
    )
    grad_probs = jnp.einsum("qhd,khd->hqk", grad_out, value, preferred_element_type=jnp.float32)
    delta = jnp.sum(probs * grad_probs, axis=-1, keepdims=True)
    grad_scores = (probs * (grad_probs - delta)).astype(jnp.bfloat16)
    grad_query = (
        jnp.einsum("hqk,khd->qhd", grad_scores, key, preferred_element_type=jnp.float32) * factor
    )
    grad_key = (
        jnp.einsum("hqk,qhd->khd", grad_scores, query, preferred_element_type=jnp.float32) * factor
    )
    return (grad_query, grad_key, grad_value)


def to_slots(values, place, size):
    columns = values.reshape(-1, size).T
    return jnp.concatenate(
        [
            lax.dynamic_index_in_dim(columns, (place - k) % size, 0, keepdims=False)
            for k in range(size)
        ]
    )


def gather_rows(values):
    return lax.all_gather(values, "dp", axis=0, tiled=True)


def scatter_rows(values):
    return lax.psum_scatter(
        values.astype(jnp.bfloat16), "dp", scatter_dimension=0, tiled=True
    ).astype(jnp.float32)


def per_device(
    tokens,
    segment_ids,
    image_blocks,
    features,
    latent_queries,
    image_kv_weight,
    image_out_weight,
    norm1_gain,
    attn_in_weight,
    attn_norm_gain,
    attn_out_weight,
    norm2_gain,
    ffn_up_weight,
    ffn_norm_gain,
    ffn_down_weight,
    cotangent,
):
    n_model = lax.axis_size("mp")
    n_data = lax.axis_size("dp")
    place = lax.axis_index("mp")
    data_index = lax.axis_index("dp")
    micro, shard_rows, _, width = tokens.shape
    row_length = shard_rows * n_model
    gain_one = norm1_gain.astype(jnp.float32)
    gain_two = norm2_gain.astype(jnp.float32)
    local_attn = attn_norm_gain.shape[0] * n_data
    local_ffn = ffn_norm_gain.shape[0] * n_data
    n_query = latent_queries.shape[0]

    small = gather_rows(
        jnp.concatenate(
            [latent_queries.reshape(-1), attn_norm_gain, ffn_norm_gain]
        )[None, :]
    )
    query_size = n_query * latent_queries.shape[1]
    queries = small[:, :query_size].reshape(n_data * n_query, -1)
    attn_gain = small[:, query_size : query_size + attn_norm_gain.shape[0]].reshape(-1)
    attn_gain = attn_gain.astype(jnp.float32)
    ffn_gain = small[:, query_size + attn_norm_gain.shape[0] :].reshape(-1).astype(jnp.float32)
    kv_weight = gather_rows(image_kv_weight)
    out_weight = gather_rows(image_out_weight)
    attn_in = gather_rows(attn_in_weight)
    attn_out = gather_rows(attn_out_weight)
    ffn_up = gather_rows(ffn_up_weight)
    ffn_down = gather_rows(ffn_down_weight)

    text = [tokens[r, :, 0, :] for r in range(micro)]
    text_in = [
        gather_slots(
            (row_norm(text[r].astype(jnp.float32))[0] * gain_one).astype(jnp.bfloat16), n_model
        )
        for r in range(micro)
    ]
    branch = [gather_slots(cotangent[r, :, 0, :], n_model) for r in range(micro)]

    latents = queries.shape[0]
    per_model = latents // n_model
    images, patches = features.shape[:2]
    image_heads = queries.shape[1] // HD
    factor = HD ** (-0.5)
    slotted = jnp.concatenate(
        [
            lax.dynamic_index_in_dim(
                queries.reshape(per_model, n_model, -1), (place - k) % n_model, 1, keepdims=False
            )
            for k in range(n_model)
        ],
        axis=0,
    ).reshape(latents, image_heads, HD)
    keyvals = jnp.einsum(
        "ipc,ckd->ipkd", features, kv_weight, preferred_element_type=jnp.float32
    ).astype(jnp.bfloat16)
    image_keys = keyvals[:, :, 0].reshape(images, patches, image_heads, HD)
    image_values = keyvals[:, :, 1].reshape(images, patches, image_heads, HD)
    image_scores = (
        jnp.einsum("lhd,iphd->ihlp", slotted, image_keys, preferred_element_type=jnp.float32)
        * factor
    )
    image_expo = jnp.exp(image_scores - jnp.max(image_scores, axis=-1, keepdims=True))
    image_probs = image_expo / jnp.sum(image_expo, axis=-1, keepdims=True)
    image_low = image_probs.astype(jnp.bfloat16)
    pooled = (
        jnp.einsum("ihlp,iphd->ilhd", image_low, image_values, preferred_element_type=jnp.float32)
        .reshape(images, latents, -1)
        .astype(jnp.bfloat16)
    )
    embed_part = jnp.einsum(
        "ilc,cd->lid", pooled, out_weight, preferred_element_type=jnp.float32
    ).reshape(latents, images * width)
    own_embeds = scatter_slots(embed_part, n_model).astype(jnp.bfloat16)
    slot_embeds = gather_slots(own_embeds, n_model).reshape(latents, images, width)
    all_embeds = lax.all_gather(slot_embeds, "dp", axis=0, tiled=False)
    total_images = n_data * images
    all_embeds = all_embeds.transpose(0, 2, 1, 3).reshape(total_images, latents, width)
    embeds_in = (row_norm(all_embeds.astype(jnp.float32))[0] * gain_one).astype(jnp.bfloat16)
    image_index = jnp.arange(total_images, dtype=jnp.int32)
    blocks_row = shard_rows // per_model

    index = jnp.arange(row_length, dtype=jnp.int32)
    position = to_slots(index, place, n_model)
    rows = []
    for r in range(micro):
        row = {}
        blocks = lax.dynamic_index_in_dim(
            image_blocks, data_index * micro + r, 0, keepdims=False
        )
        selector = (blocks[:, None] == image_index[None, :]).astype(jnp.bfloat16)
        row["selector"] = selector
        is_text = jnp.repeat(blocks == total_images, per_model)[:, None]
        row["is_text"] = is_text
        placed = jnp.einsum(
            "bi,isd->bsd",
            selector,
            embeds_in.reshape(total_images, n_model * per_model, width),
            preferred_element_type=jnp.float32,
        ).astype(jnp.bfloat16)
        placed = (
            placed.reshape(blocks_row, n_model, per_model, width)
            .swapaxes(0, 1)
            .reshape(row_length, width)
        )
        own_placed = jnp.einsum(
            "bi,isd->bsd",
            selector,
            all_embeds[:, :per_model],
            preferred_element_type=jnp.float32,
        ).reshape(shard_rows, width)
        start = jnp.where(is_text, text[r].astype(jnp.float32), own_placed)
        row["start"] = start
        row["input1"] = jnp.where(jnp.tile(is_text, (n_model, 1)), text_in[r], placed)
        segments = to_slots(segment_ids[r], place, n_model)
        places = to_slots(doc_positions(segment_ids[r]), place, n_model)
        row["allowed"] = (position[:, None] >= position[None, :]) & (
            segments[:, None] == segments[None, :]
        )
        cosine, sine, decay = rotary_tables(places, HD)
        row["tables"] = (cosine, sine, decay[:, None, :])
        rows.append(row)

    local_heads = attn_in.shape[2] // HD
    outputs = []
    for r in range(micro):
        row = rows[r]
        cosine, sine, decay = row["tables"]
        mixed = jnp.einsum(
            "lc,ckd->lkd", row["input1"], attn_in, preferred_element_type=jnp.float32
        )
        row["query"] = (
            rotate(mixed[:, 0].reshape(row_length, local_heads, HD), cosine, sine) * decay
        ).astype(jnp.bfloat16)
        row["key"] = (
            rotate(mixed[:, 1].reshape(row_length, local_heads, HD), cosine, sine) / decay
        ).astype(jnp.bfloat16)
        row["value"] = mixed[:, 2].reshape(row_length, local_heads, HD).astype(jnp.bfloat16)
        attended, row["totals"] = attend_forward(
            row["query"], row["key"], row["value"], row["allowed"]
        )
        row["normed_a"], row["back_a"] = split_norm(
            attended.reshape(row_length, -1), D, n_model
        )
        row["sub_attn"] = (row["normed_a"] * attn_gain).astype(jnp.bfloat16)
        part = jnp.dot(row["sub_attn"], attn_out, preferred_element_type=jnp.float32)
        row["middle"] = row["start"] + scatter_slots(part, n_model)
        second = row["middle"].astype(jnp.bfloat16).astype(jnp.float32)
        row["normed2"], row["back2"] = row_norm(second)
        row["input2"] = gather_slots(
            (row["normed2"] * gain_two).astype(jnp.bfloat16), n_model
        )
    for r in range(micro):
        row = rows[r]
        row["hidden"] = jnp.dot(row["input2"], ffn_up, preferred_element_type=jnp.float32)
        row["normed_f"], row["back_f"] = split_norm(
            jax.nn.gelu(row["hidden"], approximate=False), FF, n_model
        )
        row["sub_ffn"] = (row["normed_f"] * ffn_gain).astype(jnp.bfloat16)
        part = jnp.dot(row["sub_ffn"], ffn_down, preferred_element_type=jnp.float32)
        outputs.append((row["middle"] + scatter_slots(part, n_model)).astype(jnp.bfloat16))
    ffn_gain_grad = 0.0
    attn_gain_grad = 0.0
    norm2_gain_grad = 0.0
    norm1_gain_grad = 0.0
    for r in range(micro):
        row = rows[r]
        grad_sub = jnp.einsum(
            "ld,fd->lf", branch[r], ffn_down, preferred_element_type=jnp.float32
        )
        grad_active, gain_part = split_norm_back(
            grad_sub, row["normed_f"], row["back_f"], ffn_gain, FF, n_model
        )
        ffn_gain_grad = ffn_gain_grad + gain_part
        row["grad_hidden"] = (grad_active * gelu_slope(row["hidden"])).astype(jnp.bfloat16)
        grad_input2 = jnp.einsum(
            "lf,cf->lc", row["grad_hidden"], ffn_up, preferred_element_type=jnp.float32
        )
        share, gain_part = row_norm_back(
            scatter_slots(grad_input2, n_model), row["normed2"], row["back2"], gain_two
        )
        norm2_gain_grad = norm2_gain_grad + gain_part
        row["grad_middle"] = cotangent[r, :, 0, :].astype(jnp.float32) + share
        row["grad_out"] = gather_slots(row["grad_middle"].astype(jnp.bfloat16), n_model)

    def both(name):
        return jnp.concatenate([row[name] for row in rows], axis=0)

    ffn_down_grad = scatter_rows(
        jnp.einsum(
            "lf,ld->fd",
            both("sub_ffn"),
            jnp.concatenate(branch, axis=0),
            preferred_element_type=jnp.float32,
        )
    )
    ffn_up_grad = scatter_rows(
        jnp.einsum(
            "lc,lf->cf", both("input2"), both("grad_hidden"), preferred_element_type=jnp.float32
        )
    )
    token_grads = []
    grad_table = jnp.zeros((per_model, total_images, width), jnp.float32)
    for r in range(micro):
        row = rows[r]
        cosine, sine, decay = row["tables"]
        grad_sub_attn = jnp.einsum(
            "ld,cd->lc", row["grad_out"], attn_out, preferred_element_type=jnp.float32
        )
        grad_attended, gain_part = split_norm_back(
            grad_sub_attn, row["normed_a"], row["back_a"], attn_gain, D, n_model
        )
        attn_gain_grad = attn_gain_grad + gain_part
        grad_query, grad_key, grad_value = attend_backward(
            row["query"],
            row["key"],
            row["value"],
            row["allowed"],
            row["totals"],
            grad_attended.astype(jnp.bfloat16).reshape(row_length, local_heads, HD),
        )
        row["grad_mixed"] = (
            jnp.stack(
                [
                    rotate(grad_query * decay, cosine, -sine),
                    rotate(grad_key / decay, cosine, -sine),
                    grad_value,
                ],
                axis=1,
            )
            .reshape(row_length, 3, -1)
            .astype(jnp.bfloat16)
        )
        grad_input1 = jnp.einsum(
            "lkd,ckd->lc", row["grad_mixed"], attn_in, preferred_element_type=jnp.float32
        )
        normed1, back1 = row_norm(row["start"])
        share, gain_part = row_norm_back(
            scatter_slots(grad_input1, n_model), normed1, back1, gain_one
        )
        norm1_gain_grad = norm1_gain_grad + gain_part
        grad_start = row["grad_middle"] + share
        token_grads.append(jnp.where(row["is_text"], grad_start, 0.0))
        grad_table = grad_table + jnp.einsum(
            "bi,bsd->sid",
            row["selector"],
            grad_start.astype(jnp.bfloat16).reshape(blocks_row, per_model, width),
            preferred_element_type=jnp.float32,
        )
    attn_out_grad = scatter_rows(
        jnp.einsum(
            "lc,ld->cd", both("sub_attn"), both("grad_out"), preferred_element_type=jnp.float32
        )
    )
    attn_in_grad = scatter_rows(
        jnp.einsum(
            "lc,lkd->ckd", both("input1"), both("grad_mixed"), preferred_element_type=jnp.float32
        )
    )

    share_grad = lax.psum_scatter(
        grad_table.astype(jnp.bfloat16), "dp", scatter_dimension=1, tiled=True
    )
    embed_grad = gather_slots(share_grad.reshape(per_model, images * width), n_model).reshape(
        latents, images, width
    )
    out_grad = jnp.einsum("ilc,lid->cd", pooled, embed_grad, preferred_element_type=jnp.float32)
    grad_pooled = (
        jnp.einsum("lid,cd->ilc", embed_grad, out_weight, preferred_element_type=jnp.float32)
        .astype(jnp.bfloat16)
        .reshape(images, latents, image_heads, HD)
    )
    grad_values = jnp.einsum(
        "ihlp,ilhd->iphd", image_low, grad_pooled, preferred_element_type=jnp.float32
    )
    grad_probs = jnp.einsum(
        "ilhd,iphd->ihlp", grad_pooled, image_values, preferred_element_type=jnp.float32
    )
    delta = jnp.sum(image_probs * grad_probs, axis=-1, keepdims=True)
    grad_scores = (image_probs * (grad_probs - delta)).astype(jnp.bfloat16)
    grad_latent = (
        jnp.einsum("ihlp,iphd->lhd", grad_scores, image_keys, preferred_element_type=jnp.float32)
        * factor
    )
    grad_keys = (
        jnp.einsum("ihlp,lhd->iphd", grad_scores, slotted, preferred_element_type=jnp.float32)
        * factor
    )
    grad_keyvals = jnp.stack(
        [grad_keys.reshape(images, patches, -1), grad_values.reshape(images, patches, -1)], axis=2
    ).astype(jnp.bfloat16)
    kv_grad = jnp.einsum(
        "ipc,ipkd->ckd", features, grad_keyvals, preferred_element_type=jnp.float32
    )
    slot_grad = grad_latent.reshape(n_model, per_model, -1)
    query_grad = jnp.stack(
        [
            lax.dynamic_index_in_dim(slot_grad, (place - m) % n_model, 0, keepdims=False)
            for m in range(n_model)
        ],
        axis=1,
    ).reshape(latents, -1)
    packed = jnp.concatenate(
        [
            kv_grad.astype(jnp.bfloat16).reshape(n_data, -1),
            out_grad.astype(jnp.bfloat16).reshape(n_data, -1),
            query_grad.astype(jnp.bfloat16).reshape(n_data, -1),
        ],
        axis=1,
    ).reshape(n_data, -1, 128)
    packed = lax.psum_scatter(packed, "dp", scatter_dimension=0, tiled=True)
    packed = packed.reshape(-1).astype(jnp.float32)
    kv_size = kv_grad.size // n_data
    out_size = out_grad.size // n_data
    image_kv_grad = packed[:kv_size].reshape(image_kv_weight.shape)
    image_out_grad = packed[kv_size : kv_size + out_size].reshape(image_out_weight.shape)
    queries_grad = packed[kv_size + out_size :].reshape(latent_queries.shape)

    gains = jnp.stack([norm1_gain_grad, norm2_gain_grad]).reshape(2, n_model, -1)
    own = 0.0
    for step in range(n_model):
        chunk = lax.dynamic_index_in_dim(gains, (place + step) % n_model, 1, keepdims=False)
        own = own + (chunk if step == 0 else shift(chunk, step, n_model))
    gain_pack = jnp.concatenate(
        [
            own[0].reshape(n_data, -1),
            own[1].reshape(n_data, -1),
            attn_gain_grad.reshape(n_data, -1),
            ffn_gain_grad.reshape(n_data, -1),
        ],
        axis=1,
    )
    gain_pack = lax.psum_scatter(gain_pack, "dp", scatter_dimension=0, tiled=True)[0]
    part = own.shape[1] // n_data
    attn_part = attn_norm_gain.shape[0]
    return (
        jnp.stack(outputs)[:, :, None, :],
        jnp.stack(token_grads)[:, :, None, :],
        queries_grad,
        image_kv_grad,
        image_out_grad,
        gain_pack[:part],
        attn_in_grad,
        gain_pack[2 * part : 2 * part + attn_part],
        attn_out_grad,
        gain_pack[part : 2 * part],
        ffn_up_grad,
        gain_pack[2 * part + attn_part :],
        ffn_down_grad,
    )


def solution(mesh):
    placed = (
        P("dp", None, "mp", None),
        P("dp", None),
        P(),
        P("dp", None, None),
        P("dp", "mp"),
        P("dp", None, "mp"),
        P(("mp", "dp"), None),
        P(),
        P("dp", None, "mp"),
        P(("mp", "dp")),
        P(("mp", "dp"), None),
        P(),
        P("dp", "mp"),
        P(("mp", "dp")),
        P(("mp", "dp"), None),
        P("dp", None, "mp", None),
    )
    return jax.shard_map(
        per_device,
        mesh=mesh,
        in_specs=placed,
        out_specs=(
            P("dp", None, "mp", None),
            P("dp", None, "mp", None),
            P("dp", "mp"),
            P("dp", None, "mp"),
            P(("mp", "dp"), None),
            P(("mp", "dp")),
            P("dp", None, "mp"),
            P(("mp", "dp")),
            P(("mp", "dp"), None),
            P(("mp", "dp")),
            P("dp", "mp"),
            P(("mp", "dp")),
            P(("mp", "dp"), None),
        ),
        check_vma=False,
    )
```

```python
import jax
import jax.numpy as jnp
from jax import lax
from jax.sharding import PartitionSpec as P

D = 2048
HD = 64
FF = 8192


EPS = 1e-05
GAMMA = 0.4
SCALE_BASE = 512.0
NEG = -1e30
HIGHEST = lax.Precision.HIGHEST
ROOT_HALF = 0.7071067811865476
INV_ROOT_TAU = 0.3989422804014327


def doc_positions(segments):
    index = jnp.arange(segments.shape[0], dtype=jnp.int32)
    starts = jnp.concatenate([jnp.ones((1,), dtype=bool), segments[1:] != segments[:-1]])
    first = lax.cummax(jnp.where(starts, index, 0), axis=0)
    return (index - first).astype(jnp.float32)


def rotary_tables(places, head_size):
    half = head_size // 2
    steps = jnp.arange(half, dtype=jnp.float32)
    freqs = 10000.0 ** (-2.0 * steps / head_size)
    angles = places[:, None] * freqs[None, :]
    zeta = (2.0 * steps / head_size + GAMMA) / (1.0 + GAMMA)
    decay = jnp.exp(jnp.log(zeta)[None, :] * places[:, None] / SCALE_BASE)
    return (jnp.cos(angles), jnp.sin(angles), jnp.concatenate([decay, decay], axis=-1))


def rotate(values, cosine, sine):
    half = values.shape[-1] // 2
    first = values[..., :half]
    second = values[..., half:]
    cosine = cosine[:, None, :]
    sine = sine[:, None, :]
    return jnp.concatenate(
        [first * cosine - second * sine, second * cosine + first * sine], axis=-1
    )


def gelu_slope(values):
    return (
        0.5 * (1.0 + lax.erf(values * ROOT_HALF))
        + values * jnp.exp(-0.5 * values * values) * INV_ROOT_TAU
    )


def row_norm(values):
    centre = values - jnp.mean(values, axis=-1, keepdims=True)
    scale_back = lax.rsqrt(jnp.mean(centre * centre, axis=-1, keepdims=True) + EPS)
    return (centre * scale_back, scale_back)


def row_norm_back(grad_out, normed, scale_back, gain):
    scaled = grad_out * gain
    gain_grad = jnp.sum(grad_out * normed, axis=0)
    grad_in = scale_back * (
        scaled
        - jnp.mean(scaled, axis=-1, keepdims=True)
        - normed * jnp.mean(scaled * normed, axis=-1, keepdims=True)
    )
    return (grad_in, gain_grad)


def shift(values, step, size):
    return lax.ppermute(values, "mp", [(i, (i + step) % size) for i in range(size)])


def sum_slots(values, size):
    total = values
    for step in range(1, size):
        total = total + jnp.roll(shift(values, step, size), step, axis=-2)
    return total


def gather_slots(shard, size):
    if size != 4:
        return jnp.concatenate(
            [shard] + [shift(shard, step, size) for step in range(1, size)], axis=0
        )
    place = lax.axis_index("mp")
    across = lax.ppermute(shard, "mp", [(0, 2), (1, 3), (2, 0), (3, 1)])
    up = lax.ppermute(shard, "mp", [(0, 1), (1, 2), (2, 3)])
    down = lax.ppermute(shard, "mp", [(1, 0), (2, 1), (3, 2)])
    ends = lax.ppermute(across, "mp", [(2, 3), (1, 0)])
    first = jnp.where(place == 0, ends, up)
    third = jnp.where(place == 3, ends, down)
    return jnp.concatenate([shard, first, across, third], axis=0)


def scatter_slots(partial, size):
    rows = partial.shape[0] // size
    parts = [partial[k * rows : (k + 1) * rows] for k in range(size)]
    low = [part.astype(jnp.bfloat16) for part in parts]
    if size != 4:
        total = parts[0]
        for step in range(1, size):
            total = total + shift(low[step], size - step, size).astype(jnp.float32)
        return total
    place = lax.axis_index("mp")
    ends = lax.ppermute(jnp.where(place == 0, low[1], low[3]), "mp", [(0, 1), (3, 2)])
    down = lax.ppermute(low[1], "mp", [(1, 0), (2, 1), (3, 2)])
    up = lax.ppermute(low[3], "mp", [(0, 1), (1, 2), (2, 3)])
    across = lax.ppermute(
        (parts[2] + ends.astype(jnp.float32)).astype(jnp.bfloat16),
        "mp",
        [(0, 2), (1, 3), (2, 0), (3, 1)],
    )
    return (
        parts[0]
        + down.astype(jnp.float32)
        + up.astype(jnp.float32)
        + across.astype(jnp.float32)
    )


def split_norm(values, width, size):
    rows = values.shape[0]
    sums = jnp.stack([jnp.sum(values, axis=-1), jnp.sum(values * values, axis=-1)])
    sums = sum_slots(sums.reshape(2, size, rows // size), size).reshape(2, rows)
    mean = sums[0] / width
    scale_back = lax.rsqrt(sums[1] / width - mean * mean + EPS)
    return ((values - mean[:, None]) * scale_back[:, None], scale_back[:, None])


def split_norm_back(grad_out, normed, scale_back, gain, width, size):
    rows = grad_out.shape[0]
    scaled = grad_out * gain
    gain_grad = jnp.sum(grad_out * normed, axis=0)
    sums = jnp.stack([jnp.sum(scaled, axis=-1), jnp.sum(scaled * normed, axis=-1)])
    sums = sum_slots(sums.reshape(2, size, rows // size), size).reshape(2, rows) / width
    grad_in = scale_back * (scaled - sums[0][:, None] - normed * sums[1][:, None])
    return (grad_in, gain_grad)


def score_block(query, key, allowed, factor):
    scores = jnp.einsum("qhd,khd->hqk", query, key, preferred_element_type=jnp.float32) * factor
    return jnp.where(allowed[None], scores, NEG)


def attend_forward(query, key, value, allowed):
    factor = query.shape[2] ** (-0.5)
    scores = score_block(query, key, allowed, factor)
    peak = jnp.max(scores, axis=-1, keepdims=True)
    expo = jnp.exp(scores - peak)
    denom = jnp.sum(expo, axis=-1, keepdims=True)
    probs = (expo / denom).astype(jnp.bfloat16)
    outputs = jnp.einsum("hqk,khd->qhd", probs, value, preferred_element_type=jnp.float32)
    return (outputs, peak + jnp.log(denom))


def attend_backward(query, key, value, allowed, totals, grad_out):
    factor = query.shape[2] ** (-0.5)
    scores = score_block(query, key, allowed, factor)
    probs = jnp.where(allowed[None], jnp.exp(scores - totals), 0.0)
    grad_value = jnp.einsum(
        "hqk,qhd->khd", probs.astype(jnp.bfloat16), grad_out, preferred_element_type=jnp.float32
    )
    grad_probs = jnp.einsum("qhd,khd->hqk", grad_out, value, preferred_element_type=jnp.float32)
    delta = jnp.sum(probs * grad_probs, axis=-1, keepdims=True)
    grad_scores = (probs * (grad_probs - delta)).astype(jnp.bfloat16)
    grad_query = (
        jnp.einsum("hqk,khd->qhd", grad_scores, key, preferred_element_type=jnp.float32) * factor
    )
    grad_key = (
        jnp.einsum("hqk,qhd->khd", grad_scores, query, preferred_element_type=jnp.float32) * factor
    )
    return (grad_query, grad_key, grad_value)


def to_slots(values, place, size):
    columns = values.reshape(-1, size).T
    return jnp.concatenate(
        [
            lax.dynamic_index_in_dim(columns, (place - k) % size, 0, keepdims=False)
            for k in range(size)
        ]
    )


def gather_rows(values):
    return lax.all_gather(values, "dp", axis=0, tiled=True)


def scatter_rows(values):
    return lax.psum_scatter(
        values.astype(jnp.bfloat16), "dp", scatter_dimension=0, tiled=True
    ).astype(jnp.float32)


def per_device(
    tokens,
    segment_ids,
    image_blocks,
    features,
    latent_queries,
    image_kv_weight,
    image_out_weight,
    norm1_gain,
    attn_in_weight,
    attn_norm_gain,
    attn_out_weight,
    norm2_gain,
    ffn_up_weight,
    ffn_norm_gain,
    ffn_down_weight,
    cotangent,
):
    n_model = lax.axis_size("mp")
    n_data = lax.axis_size("dp")
    place = lax.axis_index("mp")
    data_index = lax.axis_index("dp")
    micro, shard_rows, _, width = tokens.shape
    row_length = shard_rows * n_model
    gain_one = norm1_gain.astype(jnp.float32)
    gain_two = norm2_gain.astype(jnp.float32)
    local_attn = attn_norm_gain.shape[0] * n_data
    local_ffn = ffn_norm_gain.shape[0] * n_data
    n_query = latent_queries.shape[0]

    columns = latent_queries.shape[1]
    query_size = n_query * columns
    small = jnp.concatenate([latent_queries.reshape(-1), attn_norm_gain, ffn_norm_gain])
    small = jnp.pad(small, (0, -small.shape[0] % (16 * columns))).reshape(-1, columns)
    kv_rows = image_kv_weight.size // columns
    out_rows = image_out_weight.size // columns
    pack = lax.all_gather(
        jnp.concatenate(
            [image_kv_weight.reshape(-1, columns), image_out_weight.reshape(-1, columns), small]
        ),
        "dp",
        axis=0,
        tiled=True,
    ).reshape(n_data, -1, columns)
    kv_weight = pack[:, :kv_rows].reshape(-1, 2, columns)
    out_weight = pack[:, kv_rows : kv_rows + out_rows].reshape(-1, width)
    small = pack[:, kv_rows + out_rows :].reshape(n_data, -1)
    queries = small[:, :query_size].reshape(n_data * n_query, -1)
    attn_end = query_size + attn_norm_gain.shape[0]
    attn_gain = small[:, query_size:attn_end].reshape(-1).astype(jnp.float32)
    ffn_gain = small[:, attn_end : attn_end + ffn_norm_gain.shape[0]].reshape(-1)
    ffn_gain = ffn_gain.astype(jnp.float32)
    attn_in = gather_rows(attn_in_weight)
    attn_out = gather_rows(attn_out_weight)
    ffn_up = gather_rows(ffn_up_weight)
    ffn_down = gather_rows(ffn_down_weight)

    text = [tokens[r, :, 0, :] for r in range(micro)]
    text_in = [
        gather_slots(
            (row_norm(text[r].astype(jnp.float32))[0] * gain_one).astype(jnp.bfloat16), n_model
        )
        for r in range(micro)
    ]
    branch = [gather_slots(cotangent[r, :, 0, :], n_model) for r in range(micro)]

    latents = queries.shape[0]
    per_model = latents // n_model
    images, patches = features.shape[:2]
    image_heads = queries.shape[1] // HD
    factor = HD ** (-0.5)
    slotted = jnp.concatenate(
        [
            lax.dynamic_index_in_dim(
                queries.reshape(per_model, n_model, -1), (place - k) % n_model, 1, keepdims=False
            )
            for k in range(n_model)
        ],
        axis=0,
    ).reshape(latents, image_heads, HD)
    keyvals = jnp.einsum(
        "ipc,ckd->ipkd", features, kv_weight, preferred_element_type=jnp.float32
    ).astype(jnp.bfloat16)
    image_keys = keyvals[:, :, 0].reshape(images, patches, image_heads, HD)
    image_values = keyvals[:, :, 1].reshape(images, patches, image_heads, HD)
    image_scores = (
        jnp.einsum("lhd,iphd->ihlp", slotted, image_keys, preferred_element_type=jnp.float32)
        * factor
    )
    image_expo = jnp.exp(image_scores - jnp.max(image_scores, axis=-1, keepdims=True))
    image_probs = image_expo / jnp.sum(image_expo, axis=-1, keepdims=True)
    image_low = image_probs.astype(jnp.bfloat16)
    pooled = (
        jnp.einsum("ihlp,iphd->ilhd", image_low, image_values, preferred_element_type=jnp.float32)
        .reshape(images, latents, -1)
        .astype(jnp.bfloat16)
    )
    pooled_late, text_in[0] = lax.optimization_barrier((pooled, text_in[0]))
    embed_part = jnp.einsum(
        "ilc,cd->lid", pooled_late, out_weight, preferred_element_type=jnp.float32
    ).reshape(latents, images * width)
    own_embeds = scatter_slots(embed_part, n_model).astype(jnp.bfloat16)
    slot_embeds = gather_slots(own_embeds, n_model)
    slot_embeds, text_in[1:] = lax.optimization_barrier((slot_embeds, text_in[1:]))
    slot_embeds, attn_in = lax.optimization_barrier((slot_embeds, attn_in))
    slot_embeds = slot_embeds.reshape(latents, images, width)
    all_embeds = lax.all_gather(slot_embeds, "dp", axis=0, tiled=False)
    total_images = n_data * images
    all_embeds = all_embeds.transpose(0, 2, 1, 3).reshape(total_images, latents, width)
    embeds_in = (row_norm(all_embeds.astype(jnp.float32))[0] * gain_one).astype(jnp.bfloat16)
    image_index = jnp.arange(total_images, dtype=jnp.int32)
    blocks_row = shard_rows // per_model

    index = jnp.arange(row_length, dtype=jnp.int32)
    position = to_slots(index, place, n_model)
    rows = []
    for r in range(micro):
        row = {}
        blocks = lax.dynamic_index_in_dim(
            image_blocks, data_index * micro + r, 0, keepdims=False
        )
        selector = (blocks[:, None] == image_index[None, :]).astype(jnp.bfloat16)
        row["selector"] = selector
        is_text = jnp.repeat(blocks == total_images, per_model)[:, None]
        row["is_text"] = is_text
        placed = jnp.einsum(
            "bi,isd->bsd",
            selector,
            embeds_in.reshape(total_images, n_model * per_model, width),
            preferred_element_type=jnp.float32,
        ).astype(jnp.bfloat16)
        placed = (
            placed.reshape(blocks_row, n_model, per_model, width)
            .swapaxes(0, 1)
            .reshape(row_length, width)
        )
        own_placed = jnp.einsum(
            "bi,isd->bsd",
            selector,
            all_embeds[:, :per_model],
            preferred_element_type=jnp.float32,
        ).reshape(shard_rows, width)
        start = jnp.where(is_text, text[r].astype(jnp.float32), own_placed)
        row["start"] = start
        row["input1"] = jnp.where(jnp.tile(is_text, (n_model, 1)), text_in[r], placed)
        segments = to_slots(segment_ids[r], place, n_model)
        places = to_slots(doc_positions(segment_ids[r]), place, n_model)
        row["allowed"] = (position[:, None] >= position[None, :]) & (
            segments[:, None] == segments[None, :]
        )
        cosine, sine, decay = rotary_tables(places, HD)
        row["tables"] = (cosine, sine, decay[:, None, :])
        rows.append(row)

    local_heads = attn_in.shape[2] // HD
    outputs = []
    for r in range(micro):
        row = rows[r]
        cosine, sine, decay = row["tables"]
        mixed = jnp.einsum(
            "lc,ckd->lkd", row["input1"], attn_in, preferred_element_type=jnp.float32
        )
        row["query"] = (
            rotate(mixed[:, 0].reshape(row_length, local_heads, HD), cosine, sine) * decay
        ).astype(jnp.bfloat16)
        row["key"] = (
            rotate(mixed[:, 1].reshape(row_length, local_heads, HD), cosine, sine) / decay
        ).astype(jnp.bfloat16)
        row["value"] = mixed[:, 2].reshape(row_length, local_heads, HD).astype(jnp.bfloat16)
        attended, row["totals"] = attend_forward(
            row["query"], row["key"], row["value"], row["allowed"]
        )
        row["normed_a"], row["back_a"] = split_norm(
            attended.reshape(row_length, -1), D, n_model
        )
        row["sub_attn"] = (row["normed_a"] * attn_gain).astype(jnp.bfloat16)
        part = jnp.dot(row["sub_attn"], attn_out, preferred_element_type=jnp.float32)
        later = [other["input1"] for other in rows[r + 1 :]]
        part, branch[r], later = lax.optimization_barrier((part, branch[r], later))
        for other, value in zip(rows[r + 1 :], later):
            other["input1"] = value
        row["middle"] = row["start"] + scatter_slots(part, n_model)
        second = row["middle"].astype(jnp.bfloat16).astype(jnp.float32)
        row["normed2"], row["back2"] = row_norm(second)
        row["input2"] = gather_slots(
            (row["normed2"] * gain_two).astype(jnp.bfloat16), n_model
        )
    ffn_gain_grad = 0.0
    attn_gain_grad = 0.0
    norm2_gain_grad = 0.0
    norm1_gain_grad = 0.0
    for r in range(micro):
        row = rows[r]
        row["hidden"] = jnp.dot(row["input2"], ffn_up, preferred_element_type=jnp.float32)
        row["normed_f"], row["back_f"] = split_norm(
            jax.nn.gelu(row["hidden"], approximate=False), FF, n_model
        )
        row["sub_ffn"] = (row["normed_f"] * ffn_gain).astype(jnp.bfloat16)
        part = jnp.dot(row["sub_ffn"], ffn_down, preferred_element_type=jnp.float32)
        outputs.append((row["middle"] + scatter_slots(part, n_model)).astype(jnp.bfloat16))
        grad_sub = jnp.einsum(
            "ld,fd->lf", branch[r], ffn_down, preferred_element_type=jnp.float32
        )
        grad_active, gain_part = split_norm_back(
            grad_sub, row["normed_f"], row["back_f"], ffn_gain, FF, n_model
        )
        ffn_gain_grad = ffn_gain_grad + gain_part
        row["grad_hidden"] = (grad_active * gelu_slope(row["hidden"])).astype(jnp.bfloat16)
        grad_input2 = jnp.einsum(
            "lf,cf->lc", row["grad_hidden"], ffn_up, preferred_element_type=jnp.float32
        )
        later = [other["input2"] for other in rows[r + 1 :]]
        grad_input2, later = lax.optimization_barrier((grad_input2, later))
        for other, value in zip(rows[r + 1 :], later):
            other["input2"] = value
        share, gain_part = row_norm_back(
            scatter_slots(grad_input2, n_model), row["normed2"], row["back2"], gain_two
        )
        norm2_gain_grad = norm2_gain_grad + gain_part
        row["grad_middle"] = cotangent[r, :, 0, :].astype(jnp.float32) + share
        row["grad_out"] = gather_slots(row["grad_middle"].astype(jnp.bfloat16), n_model)

    def both(name):
        return jnp.concatenate([row[name] for row in rows], axis=0)

    down_part = jnp.einsum(
        "lf,ld->fd",
        both("sub_ffn"),
        jnp.concatenate(branch, axis=0),
        preferred_element_type=jnp.float32,
    ).astype(jnp.bfloat16)
    up_part = jnp.einsum(
        "lc,lf->cf", both("input2"), both("grad_hidden"), preferred_element_type=jnp.float32
    ).astype(jnp.bfloat16)
    down_part, rows[0]["grad_out"] = lax.optimization_barrier((down_part, rows[0]["grad_out"]))
    up_part, rows[-1]["grad_out"] = lax.optimization_barrier((up_part, rows[-1]["grad_out"]))
    ffn_down_grad = scatter_rows(down_part)
    ffn_up_grad = scatter_rows(up_part)
    attn_out_part = jnp.einsum(
        "lc,ld->cd", both("sub_attn"), both("grad_out"), preferred_element_type=jnp.float32
    ).astype(jnp.bfloat16)
    token_grads = []
    grad_table = jnp.zeros((per_model, total_images, width), jnp.float32)
    for r in range(micro):
        row = rows[r]
        cosine, sine, decay = row["tables"]
        grad_sub_attn = jnp.einsum(
            "ld,cd->lc", row["grad_out"], attn_out, preferred_element_type=jnp.float32
        )
        grad_attended, gain_part = split_norm_back(
            grad_sub_attn, row["normed_a"], row["back_a"], attn_gain, D, n_model
        )
        attn_gain_grad = attn_gain_grad + gain_part
        grad_query, grad_key, grad_value = attend_backward(
            row["query"],
            row["key"],
            row["value"],
            row["allowed"],
            row["totals"],
            grad_attended.astype(jnp.bfloat16).reshape(row_length, local_heads, HD),
        )
        row["grad_mixed"] = (
            jnp.stack(
                [
                    rotate(grad_query * decay, cosine, -sine),
                    rotate(grad_key / decay, cosine, -sine),
                    grad_value,
                ],
                axis=1,
            )
            .reshape(row_length, 3, -1)
            .astype(jnp.bfloat16)
        )
        grad_input1 = jnp.einsum(
            "lkd,ckd->lc", row["grad_mixed"], attn_in, preferred_element_type=jnp.float32
        )
        if r < micro - 1:
            later = [other["grad_out"] for other in rows[r + 1 :]]
            grad_input1, later = lax.optimization_barrier((grad_input1, later))
            for other, value in zip(rows[r + 1 :], later):
                other["grad_out"] = value
        else:
            grad_input1, attn_out_part = lax.optimization_barrier((grad_input1, attn_out_part))
        normed1, back1 = row_norm(row["start"])
        share, gain_part = row_norm_back(
            scatter_slots(grad_input1, n_model), normed1, back1, gain_one
        )
        norm1_gain_grad = norm1_gain_grad + gain_part
        grad_start = row["grad_middle"] + share
        token_grads.append(jnp.where(row["is_text"], grad_start, 0.0))
        grad_table = grad_table + jnp.einsum(
            "bi,bsd->sid",
            row["selector"],
            grad_start.astype(jnp.bfloat16).reshape(blocks_row, per_model, width),
            preferred_element_type=jnp.float32,
        )
    attn_in_grad = scatter_rows(
        jnp.einsum(
            "lc,lkd->ckd", both("input1"), both("grad_mixed"), preferred_element_type=jnp.float32
        )
    )

    attn_out_grad = scatter_rows(attn_out_part)
    grad_table, ffn_down_grad, ffn_up_grad, attn_out_grad = lax.optimization_barrier(
        (grad_table, ffn_down_grad, ffn_up_grad, attn_out_grad)
    )
    share_grad = lax.psum_scatter(
        grad_table.astype(jnp.bfloat16), "dp", scatter_dimension=1, tiled=True
    )
    embed_grad = gather_slots(share_grad.reshape(per_model, images * width), n_model).reshape(
        latents, images, width
    )
    out_grad = jnp.einsum("ilc,lid->cd", pooled, embed_grad, preferred_element_type=jnp.float32)
    grad_pooled = (
        jnp.einsum("lid,cd->ilc", embed_grad, out_weight, preferred_element_type=jnp.float32)
        .astype(jnp.bfloat16)
        .reshape(images, latents, image_heads, HD)
    )
    grad_values = jnp.einsum(
        "ihlp,ilhd->iphd", image_low, grad_pooled, preferred_element_type=jnp.float32
    )
    grad_probs = jnp.einsum(
        "ilhd,iphd->ihlp", grad_pooled, image_values, preferred_element_type=jnp.float32
    )
    delta = jnp.sum(image_probs * grad_probs, axis=-1, keepdims=True)
    grad_scores = (image_probs * (grad_probs - delta)).astype(jnp.bfloat16)
    grad_latent = (
        jnp.einsum("ihlp,iphd->lhd", grad_scores, image_keys, preferred_element_type=jnp.float32)
        * factor
    )
    grad_keys = (
        jnp.einsum("ihlp,lhd->iphd", grad_scores, slotted, preferred_element_type=jnp.float32)
        * factor
    )
    grad_keyvals = jnp.stack(
        [grad_keys.reshape(images, patches, -1), grad_values.reshape(images, patches, -1)], axis=2
    ).astype(jnp.bfloat16)
    kv_grad = jnp.einsum(
        "ipc,ipkd->ckd", features, grad_keyvals, preferred_element_type=jnp.float32
    )
    slot_grad = grad_latent.reshape(n_model, per_model, -1)
    query_grad = jnp.stack(
        [
            lax.dynamic_index_in_dim(slot_grad, (place - m) % n_model, 0, keepdims=False)
            for m in range(n_model)
        ],
        axis=1,
    ).reshape(latents, -1)
    gains = jnp.stack([norm1_gain_grad, norm2_gain_grad]).reshape(2, n_model, -1)
    own = 0.0
    for step in range(n_model):
        chunk = lax.dynamic_index_in_dim(gains, (place + step) % n_model, 1, keepdims=False)
        own = own + (chunk if step == 0 else shift(chunk, step, n_model))
    pieces = [
        piece.astype(jnp.bfloat16).reshape(n_data, -1)
        for piece in (
            kv_grad,
            out_grad,
            query_grad,
            own[0],
            own[1],
            attn_gain_grad,
            ffn_gain_grad,
        )
    ]
    packed = jnp.concatenate(pieces, axis=1)
    packed = jnp.pad(packed, ((0, 0), (0, -packed.shape[1] % 2048))).reshape(n_data, -1, 128)
    packed, attn_in_grad = lax.optimization_barrier((packed, attn_in_grad))
    packed = lax.psum_scatter(packed, "dp", scatter_dimension=0, tiled=True)
    packed = packed.reshape(-1).astype(jnp.float32)
    split = []
    begin = 0
    for piece in pieces:
        split.append(packed[begin : begin + piece.shape[1]])
        begin += piece.shape[1]
    return (
        jnp.stack(outputs)[:, :, None, :],
        jnp.stack(token_grads)[:, :, None, :],
        split[2].reshape(latent_queries.shape),
        split[0].reshape(image_kv_weight.shape),
        split[1].reshape(image_out_weight.shape),
        split[3],
        attn_in_grad,
        split[5],
        attn_out_grad,
        split[4],
        ffn_up_grad,
        split[6],
        ffn_down_grad,
    )


def solution(mesh):
    placed = (
        P("dp", None, "mp", None),
        P("dp", None),
        P(),
        P("dp", None, None),
        P("dp", "mp"),
        P("dp", None, "mp"),
        P(("mp", "dp"), None),
        P(),
        P("dp", None, "mp"),
        P(("mp", "dp")),
        P(("mp", "dp"), None),
        P(),
        P("dp", "mp"),
        P(("mp", "dp")),
        P(("mp", "dp"), None),
        P("dp", None, "mp", None),
    )
    return jax.shard_map(
        per_device,
        mesh=mesh,
        in_specs=placed,
        out_specs=(
            P("dp", None, "mp", None),
            P("dp", None, "mp", None),
            P("dp", "mp"),
            P("dp", None, "mp"),
            P(("mp", "dp"), None),
            P(("mp", "dp")),
            P("dp", None, "mp"),
            P(("mp", "dp")),
            P(("mp", "dp"), None),
            P(("mp", "dp")),
            P("dp", "mp"),
            P(("mp", "dp")),
            P(("mp", "dp"), None),
        ),
        check_vma=False,
    )
```

```python
import jax
import jax.numpy as jnp
from jax import lax
from jax.sharding import PartitionSpec as P

D = 2048
HD = 64
FF = 8192


EPS = 1e-05
GAMMA = 0.4
SCALE_BASE = 512.0
NEG = -1e30
HIGHEST = lax.Precision.HIGHEST
ROOT_HALF = 0.7071067811865476
INV_ROOT_TAU = 0.3989422804014327


def doc_positions(segments):
    index = jnp.arange(segments.shape[0], dtype=jnp.int32)
    starts = jnp.concatenate([jnp.ones((1,), dtype=bool), segments[1:] != segments[:-1]])
    first = lax.cummax(jnp.where(starts, index, 0), axis=0)
    return (index - first).astype(jnp.float32)


def rotary_tables(places, head_size):
    half = head_size // 2
    steps = jnp.arange(half, dtype=jnp.float32)
    freqs = 10000.0 ** (-2.0 * steps / head_size)
    angles = places[:, None] * freqs[None, :]
    zeta = (2.0 * steps / head_size + GAMMA) / (1.0 + GAMMA)
    decay = jnp.exp(jnp.log(zeta)[None, :] * places[:, None] / SCALE_BASE)
    return (jnp.cos(angles), jnp.sin(angles), jnp.concatenate([decay, decay], axis=-1))


def rotate(values, cosine, sine):
    half = values.shape[-1] // 2
    first = values[..., :half]
    second = values[..., half:]
    cosine = cosine[:, None, :]
    sine = sine[:, None, :]
    return jnp.concatenate(
        [first * cosine - second * sine, second * cosine + first * sine], axis=-1
    )


def gelu_slope(values):
    return (
        0.5 * (1.0 + lax.erf(values * ROOT_HALF))
        + values * jnp.exp(-0.5 * values * values) * INV_ROOT_TAU
    )


def row_norm(values):
    centre = values - jnp.mean(values, axis=-1, keepdims=True)
    scale_back = lax.rsqrt(jnp.mean(centre * centre, axis=-1, keepdims=True) + EPS)
    return (centre * scale_back, scale_back)


def row_norm_back(grad_out, normed, scale_back, gain):
    scaled = grad_out * gain
    gain_grad = jnp.sum(grad_out * normed, axis=0)
    grad_in = scale_back * (
        scaled
        - jnp.mean(scaled, axis=-1, keepdims=True)
        - normed * jnp.mean(scaled * normed, axis=-1, keepdims=True)
    )
    return (grad_in, gain_grad)


def shift(values, step, size):
    return lax.ppermute(values, "mp", [(i, (i + step) % size) for i in range(size)])


def sum_slots(values, size):
    total = values
    for step in range(1, size):
        total = total + jnp.roll(shift(values, step, size), step, axis=-2)
    return total


def gather_slots(shard, size):
    if size != 4:
        return jnp.concatenate(
            [shard] + [shift(shard, step, size) for step in range(1, size)], axis=0
        )
    place = lax.axis_index("mp")
    across = lax.ppermute(shard, "mp", [(0, 2), (1, 3), (2, 0), (3, 1)])
    up = lax.ppermute(shard, "mp", [(0, 1), (1, 2), (2, 3)])
    down = lax.ppermute(shard, "mp", [(1, 0), (2, 1), (3, 2)])
    ends = lax.ppermute(across, "mp", [(2, 3), (1, 0)])
    first = jnp.where(place == 0, ends, up)
    third = jnp.where(place == 3, ends, down)
    return jnp.concatenate([shard, first, across, third], axis=0)


def scatter_slots(partial, size):
    rows = partial.shape[0] // size
    parts = [partial[k * rows : (k + 1) * rows] for k in range(size)]
    low = [part.astype(jnp.bfloat16) for part in parts]
    if size != 4:
        total = parts[0]
        for step in range(1, size):
            total = total + shift(low[step], size - step, size).astype(jnp.float32)
        return total
    place = lax.axis_index("mp")
    ends = lax.ppermute(jnp.where(place == 0, low[1], low[3]), "mp", [(0, 1), (3, 2)])
    down = lax.ppermute(low[1], "mp", [(1, 0), (2, 1), (3, 2)])
    up = lax.ppermute(low[3], "mp", [(0, 1), (1, 2), (2, 3)])
    across = lax.ppermute(
        (parts[2] + ends.astype(jnp.float32)).astype(jnp.bfloat16),
        "mp",
        [(0, 2), (1, 3), (2, 0), (3, 1)],
    )
    return (
        parts[0]
        + down.astype(jnp.float32)
        + up.astype(jnp.float32)
        + across.astype(jnp.float32)
    )


def split_norm(values, width, size):
    rows = values.shape[0]
    sums = jnp.stack([jnp.sum(values, axis=-1), jnp.sum(values * values, axis=-1)])
    sums = sum_slots(sums.reshape(2, size, rows // size), size).reshape(2, rows)
    mean = sums[0] / width
    scale_back = lax.rsqrt(sums[1] / width - mean * mean + EPS)
    return ((values - mean[:, None]) * scale_back[:, None], scale_back[:, None])


def split_norm_back(grad_out, normed, scale_back, gain, width, size):
    rows = grad_out.shape[0]
    scaled = grad_out * gain
    gain_grad = jnp.sum(grad_out * normed, axis=0)
    sums = jnp.stack([jnp.sum(scaled, axis=-1), jnp.sum(scaled * normed, axis=-1)])
    sums = sum_slots(sums.reshape(2, size, rows // size), size).reshape(2, rows) / width
    grad_in = scale_back * (scaled - sums[0][:, None] - normed * sums[1][:, None])
    return (grad_in, gain_grad)


def score_block(query, key, allowed, factor):
    scores = jnp.einsum("qhd,khd->hqk", query, key, preferred_element_type=jnp.float32) * factor
    return jnp.where(allowed[None], scores, NEG)


def attend_forward(query, key, value, allowed):
    factor = query.shape[2] ** (-0.5)
    scores = score_block(query, key, allowed, factor)
    peak = jnp.max(scores, axis=-1, keepdims=True)
    expo = jnp.exp(scores - peak)
    denom = jnp.sum(expo, axis=-1, keepdims=True)
    probs = (expo / denom).astype(jnp.bfloat16)
    outputs = jnp.einsum("hqk,khd->qhd", probs, value, preferred_element_type=jnp.float32)
    return (outputs, peak + jnp.log(denom))


def attend_backward(query, key, value, allowed, totals, grad_out):
    factor = query.shape[2] ** (-0.5)
    scores = score_block(query, key, allowed, factor)
    probs = jnp.where(allowed[None], jnp.exp(scores - totals), 0.0)
    grad_value = jnp.einsum(
        "hqk,qhd->khd", probs.astype(jnp.bfloat16), grad_out, preferred_element_type=jnp.float32
    )
    grad_probs = jnp.einsum("qhd,khd->hqk", grad_out, value, preferred_element_type=jnp.float32)
    delta = jnp.sum(probs * grad_probs, axis=-1, keepdims=True)
    grad_scores = (probs * (grad_probs - delta)).astype(jnp.bfloat16)
    grad_query = (
        jnp.einsum("hqk,khd->qhd", grad_scores, key, preferred_element_type=jnp.float32) * factor
    )
    grad_key = (
        jnp.einsum("hqk,qhd->khd", grad_scores, query, preferred_element_type=jnp.float32) * factor
    )
    return (grad_query, grad_key, grad_value)


def to_slots(values, place, size):
    columns = values.reshape(-1, size).T
    return jnp.concatenate(
        [
            lax.dynamic_index_in_dim(columns, (place - k) % size, 0, keepdims=False)
            for k in range(size)
        ]
    )


def gather_rows(values):
    return lax.all_gather(values, "dp", axis=0, tiled=True)


def scatter_rows(values):
    return lax.psum_scatter(
        values.astype(jnp.bfloat16), "dp", scatter_dimension=0, tiled=True
    ).astype(jnp.float32)


class Row:
    pass


def per_device(
    tokens,
    segment_ids,
    image_blocks,
    features,
    latent_queries,
    image_kv_weight,
    image_out_weight,
    norm1_gain,
    attn_in_weight,
    attn_norm_gain,
    attn_out_weight,
    norm2_gain,
    ffn_up_weight,
    ffn_norm_gain,
    ffn_down_weight,
    cotangent,
):
    n_model = lax.axis_size("mp")
    n_data = lax.axis_size("dp")
    place = lax.axis_index("mp")
    data_index = lax.axis_index("dp")
    micro, shard_rows, _, width = tokens.shape
    row_length = shard_rows * n_model
    gain_one = norm1_gain.astype(jnp.float32)
    gain_two = norm2_gain.astype(jnp.float32)
    local_attn = attn_norm_gain.shape[0] * n_data
    local_ffn = ffn_norm_gain.shape[0] * n_data
    n_query = latent_queries.shape[0]

    columns = latent_queries.shape[1]
    query_size = n_query * columns
    small = jnp.concatenate([latent_queries.reshape(-1), attn_norm_gain, ffn_norm_gain])
    small = jnp.pad(small, (0, -small.shape[0] % (16 * columns))).reshape(-1, columns)
    kv_rows = image_kv_weight.size // columns
    out_rows = image_out_weight.size // columns
    pack = lax.all_gather(
        jnp.concatenate(
            [image_kv_weight.reshape(-1, columns), image_out_weight.reshape(-1, columns), small]
        ),
        "dp",
        axis=0,
        tiled=True,
    ).reshape(n_data, -1, columns)
    kv_weight = pack[:, :kv_rows].reshape(-1, 2, columns)
    out_weight = pack[:, kv_rows : kv_rows + out_rows].reshape(-1, width)
    small = pack[:, kv_rows + out_rows :].reshape(n_data, -1)
    queries = small[:, :query_size].reshape(n_data * n_query, -1)
    attn_end = query_size + attn_norm_gain.shape[0]
    attn_gain = small[:, query_size:attn_end].reshape(-1).astype(jnp.float32)
    ffn_gain = small[:, attn_end : attn_end + ffn_norm_gain.shape[0]].reshape(-1)
    ffn_gain = ffn_gain.astype(jnp.float32)
    attn_in = gather_rows(attn_in_weight)
    attn_out = gather_rows(attn_out_weight)

    text = [tokens[r, :, 0, :] for r in range(micro)]
    text_in = [
        gather_slots(
            (row_norm(text[r].astype(jnp.float32))[0] * gain_one).astype(jnp.bfloat16), n_model
        )
        for r in range(micro)
    ]

    latents = queries.shape[0]
    per_model = latents // n_model
    images, patches = features.shape[:2]
    image_heads = queries.shape[1] // HD
    factor = HD ** (-0.5)
    slotted = jnp.concatenate(
        [
            lax.dynamic_index_in_dim(
                queries.reshape(per_model, n_model, -1), (place - k) % n_model, 1, keepdims=False
            )
            for k in range(n_model)
        ],
        axis=0,
    ).reshape(latents, image_heads, HD)
    keyvals = jnp.einsum(
        "ipc,ckd->ipkd", features, kv_weight, preferred_element_type=jnp.float32
    ).astype(jnp.bfloat16)
    image_keys = keyvals[:, :, 0].reshape(images, patches, image_heads, HD)
    image_values = keyvals[:, :, 1].reshape(images, patches, image_heads, HD)
    image_scores = (
        jnp.einsum("lhd,iphd->ihlp", slotted, image_keys, preferred_element_type=jnp.float32)
        * factor
    )
    image_expo = jnp.exp(image_scores - jnp.max(image_scores, axis=-1, keepdims=True))
    image_probs = image_expo / jnp.sum(image_expo, axis=-1, keepdims=True)
    image_low = image_probs.astype(jnp.bfloat16)
    pooled = (
        jnp.einsum("ihlp,iphd->ilhd", image_low, image_values, preferred_element_type=jnp.float32)
        .reshape(images, latents, -1)
        .astype(jnp.bfloat16)
    )
    pooled_late, text_in[0] = lax.optimization_barrier((pooled, text_in[0]))
    embed_part = jnp.einsum(
        "ilc,cd->lid", pooled_late, out_weight, preferred_element_type=jnp.float32
    ).reshape(latents, images * width)
    own_embeds = scatter_slots(embed_part, n_model).astype(jnp.bfloat16)
    slot_embeds = gather_slots(own_embeds, n_model)
    slot_embeds, text_in[1:] = lax.optimization_barrier((slot_embeds, text_in[1:]))
    slot_embeds, attn_in, attn_out = lax.optimization_barrier((slot_embeds, attn_in, attn_out))
    slot_embeds = slot_embeds.reshape(latents, images, width)
    all_embeds = lax.all_gather(slot_embeds, "dp", axis=0, tiled=False)
    grads_own, all_embeds = lax.optimization_barrier((cotangent[:, :, 0, :], all_embeds))
    grads_all = lax.all_gather(grads_own, "mp", axis=0, tiled=False)
    branch = [
        jnp.concatenate(
            [
                lax.dynamic_index_in_dim(grads_all, (place - k) % n_model, 0, keepdims=False)[r]
                for k in range(n_model)
            ],
            axis=0,
        )
        for r in range(micro)
    ]
    up_late, down_late, _ = lax.optimization_barrier((ffn_up_weight, ffn_down_weight, grads_all))
    ffn_up = gather_rows(up_late)
    ffn_down = gather_rows(down_late)
    total_images = n_data * images
    all_embeds = all_embeds.transpose(0, 2, 1, 3).reshape(total_images, latents, width)
    embeds_in = (row_norm(all_embeds.astype(jnp.float32))[0] * gain_one).astype(jnp.bfloat16)
    image_index = jnp.arange(total_images, dtype=jnp.int32)
    blocks_row = shard_rows // per_model

    index = jnp.arange(row_length, dtype=jnp.int32)
    position = to_slots(index, place, n_model)
    rows = []
    for r in range(micro):
        row = Row()
        blocks = lax.dynamic_index_in_dim(
            image_blocks, data_index * micro + r, 0, keepdims=False
        )
        selector = (blocks[:, None] == image_index[None, :]).astype(jnp.bfloat16)
        row.selector = selector
        is_text = jnp.repeat(blocks == total_images, per_model)[:, None]
        row.is_text = is_text
        placed = jnp.einsum(
            "bi,isd->bsd",
            selector,
            embeds_in.reshape(total_images, n_model * per_model, width),
            preferred_element_type=jnp.float32,
        ).astype(jnp.bfloat16)
        placed = (
            placed.reshape(blocks_row, n_model, per_model, width)
            .swapaxes(0, 1)
            .reshape(row_length, width)
        )
        own_placed = jnp.einsum(
            "bi,isd->bsd",
            selector,
            all_embeds[:, :per_model],
            preferred_element_type=jnp.float32,
        ).reshape(shard_rows, width)
        start = jnp.where(is_text, text[r].astype(jnp.float32), own_placed)
        row.start = start
        row.input1 = jnp.where(jnp.tile(is_text, (n_model, 1)), text_in[r], placed)
        segments = to_slots(segment_ids[r], place, n_model)
        places = to_slots(doc_positions(segment_ids[r]), place, n_model)
        row.allowed = (position[:, None] >= position[None, :]) & (
            segments[:, None] == segments[None, :]
        )
        cosine, sine, decay = rotary_tables(places, HD)
        row.tables = (cosine, sine, decay[:, None, :])
        rows.append(row)

    local_heads = attn_in.shape[2] // HD
    outputs = []
    for r in range(micro):
        row = rows[r]
        cosine, sine, decay = row.tables
        mixed = jnp.einsum(
            "lc,ckd->lkd", row.input1, attn_in, preferred_element_type=jnp.float32
        )
        row.query = (
            rotate(mixed[:, 0].reshape(row_length, local_heads, HD), cosine, sine) * decay
        ).astype(jnp.bfloat16)
        row.key = (
            rotate(mixed[:, 1].reshape(row_length, local_heads, HD), cosine, sine) / decay
        ).astype(jnp.bfloat16)
        row.value = mixed[:, 2].reshape(row_length, local_heads, HD).astype(jnp.bfloat16)
        attended, row.totals = attend_forward(
            row.query, row.key, row.value, row.allowed
        )
        row.normed_a, row.back_a = split_norm(
            attended.reshape(row_length, -1), D, n_model
        )
        row.sub_attn = (row.normed_a * attn_gain).astype(jnp.bfloat16)
        part = jnp.dot(row.sub_attn, attn_out, preferred_element_type=jnp.float32)
        later = [other.input1 for other in rows[r + 1 :]]
        part, later = lax.optimization_barrier((part, later))
        for other, value in zip(rows[r + 1 :], later):
            other.input1 = value
        row.middle = row.start + scatter_slots(part, n_model)
        second = row.middle.astype(jnp.bfloat16).astype(jnp.float32)
        row.normed2, row.back2 = row_norm(second)
        row.input2 = gather_slots(
            (row.normed2 * gain_two).astype(jnp.bfloat16), n_model
        )
    ffn_gain_grad = 0.0
    attn_gain_grad = 0.0
    norm2_gain_grad = 0.0
    norm1_gain_grad = 0.0
    for r in range(micro):
        row = rows[r]
        row.hidden = jnp.dot(row.input2, ffn_up, preferred_element_type=jnp.float32)
        row.normed_f, row.back_f = split_norm(
            jax.nn.gelu(row.hidden, approximate=False), FF, n_model
        )
        row.sub_ffn = (row.normed_f * ffn_gain).astype(jnp.bfloat16)
        part = jnp.dot(row.sub_ffn, ffn_down, preferred_element_type=jnp.float32)
        outputs.append((row.middle + scatter_slots(part, n_model)).astype(jnp.bfloat16))
        grad_sub = jnp.einsum(
            "ld,fd->lf", branch[r], ffn_down, preferred_element_type=jnp.float32
        )
        grad_active, gain_part = split_norm_back(
            grad_sub, row.normed_f, row.back_f, ffn_gain, FF, n_model
        )
        ffn_gain_grad = ffn_gain_grad + gain_part
        row.grad_hidden = (grad_active * gelu_slope(row.hidden)).astype(jnp.bfloat16)
        grad_input2 = jnp.einsum(
            "lf,cf->lc", row.grad_hidden, ffn_up, preferred_element_type=jnp.float32
        )
        later = [other.input2 for other in rows[r + 1 :]]
        grad_input2, later = lax.optimization_barrier((grad_input2, later))
        for other, value in zip(rows[r + 1 :], later):
            other.input2 = value
        share, gain_part = row_norm_back(
            scatter_slots(grad_input2, n_model), row.normed2, row.back2, gain_two
        )
        norm2_gain_grad = norm2_gain_grad + gain_part
        row.grad_middle = cotangent[r, :, 0, :].astype(jnp.float32) + share
        row.grad_out = gather_slots(row.grad_middle.astype(jnp.bfloat16), n_model)

    def both(values):
        return jnp.concatenate(values, axis=0)

    down_part = jnp.einsum(
        "lf,ld->fd",
        both([row.sub_ffn for row in rows]),
        jnp.concatenate(branch, axis=0),
        preferred_element_type=jnp.float32,
    ).astype(jnp.bfloat16)
    up_part = jnp.einsum(
        "lc,lf->cf", both([row.input2 for row in rows]), both([row.grad_hidden for row in rows]), preferred_element_type=jnp.float32
    ).astype(jnp.bfloat16)
    down_part, rows[0].grad_out = lax.optimization_barrier((down_part, rows[0].grad_out))
    up_part, rows[-1].grad_out = lax.optimization_barrier((up_part, rows[-1].grad_out))
    ffn_down_grad = scatter_rows(down_part)
    ffn_up_grad = scatter_rows(up_part)
    attn_out_part = jnp.einsum(
        "lc,ld->cd", both([row.sub_attn for row in rows]), both([row.grad_out for row in rows]), preferred_element_type=jnp.float32
    ).astype(jnp.bfloat16)
    token_grads = []
    grad_table = jnp.zeros((per_model, total_images, width), jnp.float32)
    for r in range(micro):
        row = rows[r]
        cosine, sine, decay = row.tables
        grad_sub_attn = jnp.einsum(
            "ld,cd->lc", row.grad_out, attn_out, preferred_element_type=jnp.float32
        )
        grad_attended, gain_part = split_norm_back(
            grad_sub_attn, row.normed_a, row.back_a, attn_gain, D, n_model
        )
        attn_gain_grad = attn_gain_grad + gain_part
        grad_query, grad_key, grad_value = attend_backward(
            row.query,
            row.key,
            row.value,
            row.allowed,
            row.totals,
            grad_attended.astype(jnp.bfloat16).reshape(row_length, local_heads, HD),
        )
        row.grad_mixed = (
            jnp.stack(
                [
                    rotate(grad_query * decay, cosine, -sine),
                    rotate(grad_key / decay, cosine, -sine),
                    grad_value,
                ],
                axis=1,
            )
            .reshape(row_length, 3, -1)
            .astype(jnp.bfloat16)
        )
        grad_input1 = jnp.einsum(
            "lkd,ckd->lc", row.grad_mixed, attn_in, preferred_element_type=jnp.float32
        )
        if r < micro - 1:
            later = [other.grad_out for other in rows[r + 1 :]]
            grad_input1, ffn_down_grad, later = lax.optimization_barrier(
                (grad_input1, ffn_down_grad, later)
            )
            for other, value in zip(rows[r + 1 :], later):
                other.grad_out = value
        else:
            grad_input1, ffn_up_grad, attn_out_part = lax.optimization_barrier(
                (grad_input1, ffn_up_grad, attn_out_part)
            )
        normed1, back1 = row_norm(row.start)
        share, gain_part = row_norm_back(
            scatter_slots(grad_input1, n_model), normed1, back1, gain_one
        )
        norm1_gain_grad = norm1_gain_grad + gain_part
        grad_start = row.grad_middle + share
        token_grads.append(jnp.where(row.is_text, grad_start, 0.0))
        grad_table = grad_table + jnp.einsum(
            "bi,bsd->sid",
            row.selector,
            grad_start.astype(jnp.bfloat16).reshape(blocks_row, per_model, width),
            preferred_element_type=jnp.float32,
        )
    attn_in_grad = scatter_rows(
        jnp.einsum(
            "lc,lkd->ckd", both([row.input1 for row in rows]), both([row.grad_mixed for row in rows]), preferred_element_type=jnp.float32
        )
    )

    attn_out_grad = scatter_rows(attn_out_part)
    grad_table, attn_out_grad = lax.optimization_barrier((grad_table, attn_out_grad))
    share_grad = lax.psum_scatter(
        grad_table.astype(jnp.bfloat16), "dp", scatter_dimension=1, tiled=True
    )
    embed_grad = gather_slots(share_grad.reshape(per_model, images * width), n_model).reshape(
        latents, images, width
    )
    out_grad = jnp.einsum("ilc,lid->cd", pooled, embed_grad, preferred_element_type=jnp.float32)
    grad_pooled = (
        jnp.einsum("lid,cd->ilc", embed_grad, out_weight, preferred_element_type=jnp.float32)
        .astype(jnp.bfloat16)
        .reshape(images, latents, image_heads, HD)
    )
    grad_values = jnp.einsum(
        "ihlp,ilhd->iphd", image_low, grad_pooled, preferred_element_type=jnp.float32
    )
    grad_probs = jnp.einsum(
        "ilhd,iphd->ihlp", grad_pooled, image_values, preferred_element_type=jnp.float32
    )
    delta = jnp.sum(image_probs * grad_probs, axis=-1, keepdims=True)
    grad_scores = (image_probs * (grad_probs - delta)).astype(jnp.bfloat16)
    grad_latent = (
        jnp.einsum("ihlp,iphd->lhd", grad_scores, image_keys, preferred_element_type=jnp.float32)
        * factor
    )
    grad_keys = (
        jnp.einsum("ihlp,lhd->iphd", grad_scores, slotted, preferred_element_type=jnp.float32)
        * factor
    )
    grad_keyvals = jnp.stack(
        [grad_keys.reshape(images, patches, -1), grad_values.reshape(images, patches, -1)], axis=2
    ).astype(jnp.bfloat16)
    kv_grad = jnp.einsum(
        "ipc,ipkd->ckd", features, grad_keyvals, preferred_element_type=jnp.float32
    )
    slot_grad = grad_latent.reshape(n_model, per_model, -1)
    query_grad = jnp.stack(
        [
            lax.dynamic_index_in_dim(slot_grad, (place - m) % n_model, 0, keepdims=False)
            for m in range(n_model)
        ],
        axis=1,
    ).reshape(latents, -1)
    gains = jnp.stack([norm1_gain_grad, norm2_gain_grad]).reshape(2, n_model, -1)
    own = 0.0
    for step in range(n_model):
        chunk = lax.dynamic_index_in_dim(gains, (place + step) % n_model, 1, keepdims=False)
        own = own + (chunk if step == 0 else shift(chunk, step, n_model))
    pieces = [
        piece.astype(jnp.bfloat16).reshape(n_data, -1)
        for piece in (
            kv_grad,
            out_grad,
            query_grad,
            own[0],
            own[1],
            attn_gain_grad,
            ffn_gain_grad,
        )
    ]
    packed = jnp.concatenate(pieces, axis=1)
    packed = jnp.pad(packed, ((0, 0), (0, -packed.shape[1] % 2048))).reshape(n_data, -1, 128)
    packed, attn_in_grad = lax.optimization_barrier((packed, attn_in_grad))
    packed = lax.psum_scatter(packed, "dp", scatter_dimension=0, tiled=True)
    packed = packed.reshape(-1).astype(jnp.float32)
    split = []
    begin = 0
    for piece in pieces:
        split.append(packed[begin : begin + piece.shape[1]])
        begin += piece.shape[1]
    return (
        jnp.stack(outputs)[:, :, None, :],
        jnp.stack(token_grads)[:, :, None, :],
        split[2].reshape(latent_queries.shape),
        split[0].reshape(image_kv_weight.shape),
        split[1].reshape(image_out_weight.shape),
        split[3],
        attn_in_grad,
        split[5],
        attn_out_grad,
        split[4],
        ffn_up_grad,
        split[6],
        ffn_down_grad,
    )


def solution(mesh):
    placed = (
        P("dp", None, "mp", None),
        P("dp", None),
        P(),
        P("dp", None, None),
        P("dp", "mp"),
        P("dp", None, "mp"),
        P(("mp", "dp"), None),
        P(),
        P("dp", None, "mp"),
        P(("mp", "dp")),
        P(("mp", "dp"), None),
        P(),
        P("dp", "mp"),
        P(("mp", "dp")),
        P(("mp", "dp"), None),
        P("dp", None, "mp", None),
    )
    return jax.shard_map(
        per_device,
        mesh=mesh,
        in_specs=placed,
        out_specs=(
            P("dp", None, "mp", None),
            P("dp", None, "mp", None),
            P("dp", "mp"),
            P("dp", None, "mp"),
            P(("mp", "dp"), None),
            P(("mp", "dp")),
            P("dp", None, "mp"),
            P(("mp", "dp")),
            P(("mp", "dp"), None),
            P(("mp", "dp")),
            P("dp", "mp"),
            P(("mp", "dp")),
            P(("mp", "dp"), None),
        ),
        check_vma=False,
    )
```

```python
import jax
import jax.numpy as jnp
from jax import lax
from jax.sharding import PartitionSpec as P

D = 2048
HD = 64
FF = 8192


EPS = 1e-05
GAMMA = 0.4
SCALE_BASE = 512.0
NEG = -1e30
ROOT_HALF = 0.7071067811865476
INV_ROOT_TAU = 0.3989422804014327


def doc_positions(segments):
    index = jnp.arange(segments.shape[0], dtype=jnp.int32)
    starts = jnp.concatenate([jnp.ones((1,), dtype=bool), segments[1:] != segments[:-1]])
    first = lax.cummax(jnp.where(starts, index, 0), axis=0)
    return (index - first).astype(jnp.float32)


def rotary_tables(places, head_size):
    half = head_size // 2
    steps = jnp.arange(half, dtype=jnp.float32)
    freqs = 10000.0 ** (-2.0 * steps / head_size)
    angles = places[:, None] * freqs[None, :]
    zeta = (2.0 * steps / head_size + GAMMA) / (1.0 + GAMMA)
    decay = jnp.exp(jnp.log(zeta)[None, :] * places[:, None] / SCALE_BASE)
    return (jnp.cos(angles), jnp.sin(angles), jnp.concatenate([decay, decay], axis=-1))


def rotate(values, cosine, sine):
    half = values.shape[-1] // 2
    first = values[..., :half]
    second = values[..., half:]
    cosine = cosine[:, None, :]
    sine = sine[:, None, :]
    return jnp.concatenate(
        [first * cosine - second * sine, second * cosine + first * sine], axis=-1
    )


def gelu_slope(values):
    return (
        0.5 * (1.0 + lax.erf(values * ROOT_HALF))
        + values * jnp.exp(-0.5 * values * values) * INV_ROOT_TAU
    )


def row_norm(values):
    centre = values - jnp.mean(values, axis=-1, keepdims=True)
    scale_back = lax.rsqrt(jnp.mean(centre * centre, axis=-1, keepdims=True) + EPS)
    return (centre * scale_back, scale_back)


def row_norm_back(grad_out, normed, scale_back, gain):
    scaled = grad_out * gain
    gain_grad = jnp.sum(grad_out * normed, axis=0)
    grad_in = scale_back * (
        scaled
        - jnp.mean(scaled, axis=-1, keepdims=True)
        - normed * jnp.mean(scaled * normed, axis=-1, keepdims=True)
    )
    return (grad_in, gain_grad)


def shift(values, step, size):
    return lax.ppermute(values, "mp", [(i, (i + step) % size) for i in range(size)])


def sum_slots(values, size):
    total = values
    for step in range(1, size):
        total = total + jnp.roll(shift(values, step, size), step, axis=-2)
    return total


def gather_slots(shard, size):
    if size != 4:
        return jnp.concatenate(
            [shard] + [shift(shard, step, size) for step in range(1, size)], axis=0
        )
    place = lax.axis_index("mp")
    across = lax.ppermute(shard, "mp", [(0, 2), (1, 3), (2, 0), (3, 1)])
    up = lax.ppermute(shard, "mp", [(0, 1), (1, 2), (2, 3)])
    down = lax.ppermute(shard, "mp", [(1, 0), (2, 1), (3, 2)])
    ends = lax.ppermute(across, "mp", [(2, 3), (1, 0)])
    first = jnp.where(place == 0, ends, up)
    third = jnp.where(place == 3, ends, down)
    return jnp.concatenate([shard, first, across, third], axis=0)


def scatter_slots(partial, size):
    rows = partial.shape[0] // size
    parts = [partial[k * rows : (k + 1) * rows] for k in range(size)]
    low = [part.astype(jnp.bfloat16) for part in parts]
    if size != 4:
        total = parts[0]
        for step in range(1, size):
            total = total + shift(low[step], size - step, size).astype(jnp.float32)
        return total
    place = lax.axis_index("mp")
    ends = lax.ppermute(jnp.where(place == 0, low[1], low[3]), "mp", [(0, 1), (3, 2)])
    down = lax.ppermute(low[1], "mp", [(1, 0), (2, 1), (3, 2)])
    up = lax.ppermute(low[3], "mp", [(0, 1), (1, 2), (2, 3)])
    across = lax.ppermute(
        (parts[2] + ends.astype(jnp.float32)).astype(jnp.bfloat16),
        "mp",
        [(0, 2), (1, 3), (2, 0), (3, 1)],
    )
    return (
        parts[0]
        + down.astype(jnp.float32)
        + up.astype(jnp.float32)
        + across.astype(jnp.float32)
    )


def split_norm(values, width, size):
    rows = values.shape[0]
    sums = jnp.stack([jnp.sum(values, axis=-1), jnp.sum(values * values, axis=-1)])
    sums = sum_slots(sums.reshape(2, size, rows // size), size).reshape(2, rows)
    mean = sums[0] / width
    scale_back = lax.rsqrt(sums[1] / width - mean * mean + EPS)
    return ((values - mean[:, None]) * scale_back[:, None], scale_back[:, None])


def split_norm_back(grad_out, normed, scale_back, gain, width, size):
    rows = grad_out.shape[0]
    scaled = grad_out * gain
    gain_grad = jnp.sum(grad_out * normed, axis=0)
    sums = jnp.stack([jnp.sum(scaled, axis=-1), jnp.sum(scaled * normed, axis=-1)])
    sums = sum_slots(sums.reshape(2, size, rows // size), size).reshape(2, rows) / width
    grad_in = scale_back * (scaled - sums[0][:, None] - normed * sums[1][:, None])
    return (grad_in, gain_grad)


def score_block(query, key, allowed, factor):
    scores = jnp.einsum("qhd,khd->hqk", query, key, preferred_element_type=jnp.float32) * factor
    return jnp.where(allowed[None], scores, NEG)


def attend_forward(query, key, value, allowed):
    factor = query.shape[2] ** (-0.5)
    scores = score_block(query, key, allowed, factor)
    peak = jnp.max(scores, axis=-1, keepdims=True)
    expo = jnp.exp(scores - peak)
    denom = jnp.sum(expo, axis=-1, keepdims=True)
    probs = (expo / denom).astype(jnp.bfloat16)
    outputs = jnp.einsum("hqk,khd->qhd", probs, value, preferred_element_type=jnp.float32)
    return (outputs, peak + jnp.log(denom))


def attend_backward(query, key, value, allowed, totals, grad_out):
    factor = query.shape[2] ** (-0.5)
    scores = score_block(query, key, allowed, factor)
    probs = jnp.where(allowed[None], jnp.exp(scores - totals), 0.0)
    grad_value = jnp.einsum(
        "hqk,qhd->khd", probs.astype(jnp.bfloat16), grad_out, preferred_element_type=jnp.float32
    )
    grad_probs = jnp.einsum("qhd,khd->hqk", grad_out, value, preferred_element_type=jnp.float32)
    delta = jnp.sum(probs * grad_probs, axis=-1, keepdims=True)
    grad_scores = (probs * (grad_probs - delta)).astype(jnp.bfloat16)
    grad_query = (
        jnp.einsum("hqk,khd->qhd", grad_scores, key, preferred_element_type=jnp.float32) * factor
    )
    grad_key = (
        jnp.einsum("hqk,qhd->khd", grad_scores, query, preferred_element_type=jnp.float32) * factor
    )
    return (grad_query, grad_key, grad_value)


def to_slots(values, place, size):
    columns = values.reshape(-1, size).T
    return jnp.concatenate(
        [
            lax.dynamic_index_in_dim(columns, (place - k) % size, 0, keepdims=False)
            for k in range(size)
        ]
    )


def gather_rows(values):
    return lax.all_gather(values, "dp", axis=0, tiled=True)


def scatter_rows(values):
    return lax.psum_scatter(
        values.astype(jnp.bfloat16), "dp", scatter_dimension=0, tiled=True
    ).astype(jnp.float32)


class Row:
    pass


def per_device(
    tokens,
    segment_ids,
    image_blocks,
    features,
    latent_queries,
    image_kv_weight,
    image_out_weight,
    norm1_gain,
    attn_in_weight,
    attn_norm_gain,
    attn_out_weight,
    norm2_gain,
    ffn_up_weight,
    ffn_norm_gain,
    ffn_down_weight,
    cotangent,
):
    n_model = lax.axis_size("mp")
    n_data = lax.axis_size("dp")
    place = lax.axis_index("mp")
    data_index = lax.axis_index("dp")
    micro, shard_rows, _, width = tokens.shape
    row_length = shard_rows * n_model
    gain_one = norm1_gain.astype(jnp.float32)
    gain_two = norm2_gain.astype(jnp.float32)
    n_query = latent_queries.shape[0]

    columns = latent_queries.shape[1]
    query_size = n_query * columns
    small = jnp.concatenate([latent_queries.reshape(-1), attn_norm_gain, ffn_norm_gain])
    small = jnp.pad(small, (0, -small.shape[0] % (16 * columns))).reshape(-1, columns)
    kv_rows = image_kv_weight.size // columns
    out_rows = image_out_weight.size // columns
    pack = lax.all_gather(
        jnp.concatenate(
            [image_kv_weight.reshape(-1, columns), image_out_weight.reshape(-1, columns), small]
        ),
        "dp",
        axis=0,
        tiled=True,
    ).reshape(n_data, -1, columns)
    kv_weight = pack[:, :kv_rows].reshape(-1, 2, columns)
    out_weight = pack[:, kv_rows : kv_rows + out_rows].reshape(-1, width)
    small = pack[:, kv_rows + out_rows :].reshape(n_data, -1)
    queries = small[:, :query_size].reshape(n_data * n_query, -1)
    attn_end = query_size + attn_norm_gain.shape[0]
    attn_gain = small[:, query_size:attn_end].reshape(-1).astype(jnp.float32)
    ffn_gain = small[:, attn_end : attn_end + ffn_norm_gain.shape[0]].reshape(-1)
    ffn_gain = ffn_gain.astype(jnp.float32)
    attn_in = gather_rows(attn_in_weight)
    attn_out = gather_rows(attn_out_weight)

    text = [tokens[r, :, 0, :] for r in range(micro)]
    text_in = [
        gather_slots(
            (row_norm(text[r].astype(jnp.float32))[0] * gain_one).astype(jnp.bfloat16), n_model
        )
        for r in range(micro)
    ]

    latents = queries.shape[0]
    per_model = latents // n_model
    images, patches = features.shape[:2]
    image_heads = queries.shape[1] // HD
    factor = HD ** (-0.5)
    slotted = jnp.concatenate(
        [
            lax.dynamic_index_in_dim(
                queries.reshape(per_model, n_model, -1), (place - k) % n_model, 1, keepdims=False
            )
            for k in range(n_model)
        ],
        axis=0,
    ).reshape(latents, image_heads, HD)
    keyvals = jnp.einsum(
        "ipc,ckd->ipkd", features, kv_weight, preferred_element_type=jnp.float32
    ).astype(jnp.bfloat16)
    image_keys = keyvals[:, :, 0].reshape(images, patches, image_heads, HD)
    image_values = keyvals[:, :, 1].reshape(images, patches, image_heads, HD)
    image_scores = (
        jnp.einsum("lhd,iphd->ihlp", slotted, image_keys, preferred_element_type=jnp.float32)
        * factor
    )
    image_expo = jnp.exp(image_scores - jnp.max(image_scores, axis=-1, keepdims=True))
    image_probs = image_expo / jnp.sum(image_expo, axis=-1, keepdims=True)
    image_low = image_probs.astype(jnp.bfloat16)
    pooled = (
        jnp.einsum("ihlp,iphd->ilhd", image_low, image_values, preferred_element_type=jnp.float32)
        .reshape(images, latents, -1)
        .astype(jnp.bfloat16)
    )
    pooled_late, text_in[0] = lax.optimization_barrier((pooled, text_in[0]))
    embed_part = jnp.einsum(
        "ilc,cd->lid", pooled_late, out_weight, preferred_element_type=jnp.float32
    ).reshape(latents, images * width)
    own_embeds = scatter_slots(embed_part, n_model).astype(jnp.bfloat16)
    slot_embeds = gather_slots(own_embeds, n_model)
    slot_embeds, text_in[1:] = lax.optimization_barrier((slot_embeds, text_in[1:]))
    slot_embeds = slot_embeds.reshape(latents, images, width)
    all_embeds = lax.all_gather(slot_embeds, "dp", axis=0, tiled=False)
    grads_all = lax.all_gather(cotangent[:, :, 0, :], "mp", axis=0, tiled=False)
    ffn_up = gather_rows(ffn_up_weight)
    ffn_down = gather_rows(ffn_down_weight)
    total_images = n_data * images
    all_embeds = all_embeds.transpose(0, 2, 1, 3).reshape(total_images, latents, width)
    embeds_in = (row_norm(all_embeds.astype(jnp.float32))[0] * gain_one).astype(jnp.bfloat16)
    image_index = jnp.arange(total_images, dtype=jnp.int32)
    blocks_row = shard_rows // per_model

    index = jnp.arange(row_length, dtype=jnp.int32)
    position = to_slots(index, place, n_model)
    rows = []
    for r in range(micro):
        row = Row()
        blocks = lax.dynamic_index_in_dim(
            image_blocks, data_index * micro + r, 0, keepdims=False
        )
        selector = (blocks[:, None] == image_index[None, :]).astype(jnp.bfloat16)
        row.selector = selector
        is_text = jnp.repeat(blocks == total_images, per_model)[:, None]
        row.is_text = is_text
        placed = jnp.einsum(
            "bi,isd->bsd",
            selector,
            embeds_in.reshape(total_images, n_model * per_model, width),
            preferred_element_type=jnp.float32,
        ).astype(jnp.bfloat16)
        placed = (
            placed.reshape(blocks_row, n_model, per_model, width)
            .swapaxes(0, 1)
            .reshape(row_length, width)
        )
        own_placed = jnp.einsum(
            "bi,isd->bsd",
            selector,
            all_embeds[:, :per_model],
            preferred_element_type=jnp.float32,
        ).reshape(shard_rows, width)
        start = jnp.where(is_text, text[r].astype(jnp.float32), own_placed)
        row.start = start
        row.input1 = jnp.where(jnp.tile(is_text, (n_model, 1)), text_in[r], placed)
        segments = to_slots(segment_ids[r], place, n_model)
        places = to_slots(doc_positions(segment_ids[r]), place, n_model)
        row.allowed = (position[:, None] >= position[None, :]) & (
            segments[:, None] == segments[None, :]
        )
        cosine, sine, decay = rotary_tables(places, HD)
        row.tables = (cosine, sine, decay[:, None, :])
        rows.append(row)

    local_heads = attn_in.shape[2] // HD
    outputs = []
    for r in range(micro):
        row = rows[r]
        cosine, sine, decay = row.tables
        mixed = jnp.einsum(
            "lc,ckd->lkd", row.input1, attn_in, preferred_element_type=jnp.float32
        )
        row.query = (
            rotate(mixed[:, 0].reshape(row_length, local_heads, HD), cosine, sine) * decay
        ).astype(jnp.bfloat16)
        row.key = (
            rotate(mixed[:, 1].reshape(row_length, local_heads, HD), cosine, sine) / decay
        ).astype(jnp.bfloat16)
        row.value = mixed[:, 2].reshape(row_length, local_heads, HD).astype(jnp.bfloat16)
        attended, row.totals = attend_forward(
            row.query, row.key, row.value, row.allowed
        )
        row.normed_a, row.back_a = split_norm(
            attended.reshape(row_length, -1), D, n_model
        )
        row.sub_attn = (row.normed_a * attn_gain).astype(jnp.bfloat16)
        part = jnp.dot(row.sub_attn, attn_out, preferred_element_type=jnp.float32)
        later = [other.input1 for other in rows[r + 1 :]]
        part, later = lax.optimization_barrier((part, later))
        for other, value in zip(rows[r + 1 :], later):
            other.input1 = value
        if r == micro - 1:
            _, grads_all = lax.optimization_barrier((part, grads_all))
        row.middle = row.start + scatter_slots(part, n_model)
        second = row.middle.astype(jnp.bfloat16).astype(jnp.float32)
        row.normed2, row.back2 = row_norm(second)
        row.input2 = gather_slots(
            (row.normed2 * gain_two).astype(jnp.bfloat16), n_model
        )
    branch = [
        jnp.concatenate(
            [
                lax.dynamic_index_in_dim(grads_all, (place - k) % n_model, 0, keepdims=False)[r]
                for k in range(n_model)
            ],
            axis=0,
        )
        for r in range(micro)
    ]
    ffn_gain_grad = 0.0
    attn_gain_grad = 0.0
    norm2_gain_grad = 0.0
    norm1_gain_grad = 0.0
    for r in range(micro):
        row = rows[r]
        row.hidden = jnp.dot(row.input2, ffn_up, preferred_element_type=jnp.float32)
        row.normed_f, row.back_f = split_norm(
            jax.nn.gelu(row.hidden, approximate=False), FF, n_model
        )
        row.sub_ffn = (row.normed_f * ffn_gain).astype(jnp.bfloat16)
        part = jnp.dot(row.sub_ffn, ffn_down, preferred_element_type=jnp.float32)
        outputs.append((row.middle + scatter_slots(part, n_model)).astype(jnp.bfloat16))
        grad_sub = jnp.einsum(
            "ld,fd->lf", branch[r], ffn_down, preferred_element_type=jnp.float32
        )
        grad_active, gain_part = split_norm_back(
            grad_sub, row.normed_f, row.back_f, ffn_gain, FF, n_model
        )
        ffn_gain_grad = ffn_gain_grad + gain_part
        row.grad_hidden = (grad_active * gelu_slope(row.hidden)).astype(jnp.bfloat16)
        grad_input2 = jnp.einsum(
            "lf,cf->lc", row.grad_hidden, ffn_up, preferred_element_type=jnp.float32
        )
        later = [other.input2 for other in rows[r + 1 :]]
        grad_input2, later = lax.optimization_barrier((grad_input2, later))
        for other, value in zip(rows[r + 1 :], later):
            other.input2 = value
        share, gain_part = row_norm_back(
            scatter_slots(grad_input2, n_model), row.normed2, row.back2, gain_two
        )
        norm2_gain_grad = norm2_gain_grad + gain_part
        row.grad_middle = cotangent[r, :, 0, :].astype(jnp.float32) + share
        row.grad_out = gather_slots(row.grad_middle.astype(jnp.bfloat16), n_model)

    def both(values):
        return jnp.concatenate(values, axis=0)

    down_part = jnp.einsum(
        "lf,ld->fd",
        both([row.sub_ffn for row in rows]),
        jnp.concatenate(branch, axis=0),
        preferred_element_type=jnp.float32,
    ).astype(jnp.bfloat16)
    up_part = jnp.einsum(
        "lc,lf->cf", both([row.input2 for row in rows]), both([row.grad_hidden for row in rows]), preferred_element_type=jnp.float32
    ).astype(jnp.bfloat16)
    _, rows[0].grad_out = lax.optimization_barrier((down_part, rows[0].grad_out))
    _, rows[-1].grad_out = lax.optimization_barrier((up_part, rows[-1].grad_out))
    ffn_down_grad = scatter_rows(down_part)
    ffn_up_grad = scatter_rows(up_part)
    attn_out_part = jnp.einsum(
        "lc,ld->cd", both([row.sub_attn for row in rows]), both([row.grad_out for row in rows]), preferred_element_type=jnp.float32
    ).astype(jnp.bfloat16)
    token_grads = []
    grad_table = jnp.zeros((per_model, total_images, width), jnp.float32)
    for r in range(micro):
        row = rows[r]
        cosine, sine, decay = row.tables
        grad_sub_attn = jnp.einsum(
            "ld,cd->lc", row.grad_out, attn_out, preferred_element_type=jnp.float32
        )
        grad_attended, gain_part = split_norm_back(
            grad_sub_attn, row.normed_a, row.back_a, attn_gain, D, n_model
        )
        attn_gain_grad = attn_gain_grad + gain_part
        grad_query, grad_key, grad_value = attend_backward(
            row.query,
            row.key,
            row.value,
            row.allowed,
            row.totals,
            grad_attended.astype(jnp.bfloat16).reshape(row_length, local_heads, HD),
        )
        row.grad_mixed = (
            jnp.stack(
                [
                    rotate(grad_query * decay, cosine, -sine),
                    rotate(grad_key / decay, cosine, -sine),
                    grad_value,
                ],
                axis=1,
            )
            .reshape(row_length, 3, -1)
            .astype(jnp.bfloat16)
        )
        grad_input1 = jnp.einsum(
            "lkd,ckd->lc", row.grad_mixed, attn_in, preferred_element_type=jnp.float32
        )
        if r < micro - 1:
            later = [other.grad_out for other in rows[r + 1 :]]
            grad_input1, later = lax.optimization_barrier((grad_input1, later))
            for other, value in zip(rows[r + 1 :], later):
                other.grad_out = value
        else:
            grad_input1, _ = lax.optimization_barrier((grad_input1, attn_out_part))
        normed1, back1 = row_norm(row.start)
        share, gain_part = row_norm_back(
            scatter_slots(grad_input1, n_model), normed1, back1, gain_one
        )
        norm1_gain_grad = norm1_gain_grad + gain_part
        grad_start = row.grad_middle + share
        token_grads.append(jnp.where(row.is_text, grad_start, 0.0))
        grad_table = grad_table + jnp.einsum(
            "bi,bsd->sid",
            row.selector,
            grad_start.astype(jnp.bfloat16).reshape(blocks_row, per_model, width),
            preferred_element_type=jnp.float32,
        )
    attn_out_grad = scatter_rows(attn_out_part)
    attn_in_part = jnp.einsum(
        "lc,lkd->ckd",
        both([row.input1 for row in rows]),
        both([row.grad_mixed for row in rows]),
        preferred_element_type=jnp.float32,
    ).astype(jnp.bfloat16)
    attn_in_grad = scatter_rows(attn_in_part)

    share_grad = lax.psum_scatter(
        grad_table.astype(jnp.bfloat16), "dp", scatter_dimension=1, tiled=True
    )
    embed_grad = gather_slots(share_grad.reshape(per_model, images * width), n_model).reshape(
        latents, images, width
    )
    out_grad = jnp.einsum("ilc,lid->cd", pooled, embed_grad, preferred_element_type=jnp.float32)
    grad_pooled = (
        jnp.einsum("lid,cd->ilc", embed_grad, out_weight, preferred_element_type=jnp.float32)
        .astype(jnp.bfloat16)
        .reshape(images, latents, image_heads, HD)
    )
    grad_values = jnp.einsum(
        "ihlp,ilhd->iphd", image_low, grad_pooled, preferred_element_type=jnp.float32
    )
    grad_probs = jnp.einsum(
        "ilhd,iphd->ihlp", grad_pooled, image_values, preferred_element_type=jnp.float32
    )
    delta = jnp.sum(image_probs * grad_probs, axis=-1, keepdims=True)
    grad_scores = (image_probs * (grad_probs - delta)).astype(jnp.bfloat16)
    grad_latent = (
        jnp.einsum("ihlp,iphd->lhd", grad_scores, image_keys, preferred_element_type=jnp.float32)
        * factor
    )
    grad_keys = (
        jnp.einsum("ihlp,lhd->iphd", grad_scores, slotted, preferred_element_type=jnp.float32)
        * factor
    )
    grad_keyvals = jnp.stack(
        [grad_keys.reshape(images, patches, -1), grad_values.reshape(images, patches, -1)], axis=2
    ).astype(jnp.bfloat16)
    kv_grad = jnp.einsum(
        "ipc,ipkd->ckd", features, grad_keyvals, preferred_element_type=jnp.float32
    )
    slot_grad = grad_latent.reshape(n_model, per_model, -1)
    query_grad = jnp.stack(
        [
            lax.dynamic_index_in_dim(slot_grad, (place - m) % n_model, 0, keepdims=False)
            for m in range(n_model)
        ],
        axis=1,
    ).reshape(latents, -1)
    gains = jnp.stack([norm1_gain_grad, norm2_gain_grad]).reshape(2, n_model, -1)
    own = 0.0
    for step in range(n_model):
        chunk = lax.dynamic_index_in_dim(gains, (place + step) % n_model, 1, keepdims=False)
        own = own + (chunk if step == 0 else shift(chunk, step, n_model))
    pieces = [
        piece.astype(jnp.bfloat16).reshape(n_data, -1)
        for piece in (
            kv_grad,
            out_grad,
            query_grad,
            own[0],
            own[1],
            attn_gain_grad,
            ffn_gain_grad,
        )
    ]
    packed = jnp.concatenate(pieces, axis=1)
    packed = jnp.pad(packed, ((0, 0), (0, -packed.shape[1] % 2048))).reshape(n_data, -1, 128)
    packed, outputs = lax.optimization_barrier((packed, outputs))
    packed = lax.psum_scatter(packed, "dp", scatter_dimension=0, tiled=True)
    packed = packed.reshape(-1).astype(jnp.float32)
    split = []
    begin = 0
    for piece in pieces:
        split.append(packed[begin : begin + piece.shape[1]])
        begin += piece.shape[1]
    return (
        jnp.stack(outputs)[:, :, None, :],
        jnp.stack(token_grads)[:, :, None, :],
        split[2].reshape(latent_queries.shape),
        split[0].reshape(image_kv_weight.shape),
        split[1].reshape(image_out_weight.shape),
        split[3],
        attn_in_grad,
        split[5],
        attn_out_grad,
        split[4],
        ffn_up_grad,
        split[6],
        ffn_down_grad,
    )


def solution(mesh):
    placed = (
        P("dp", None, "mp", None),
        P("dp", None),
        P(),
        P("dp", None, None),
        P("dp", "mp"),
        P("dp", None, "mp"),
        P(("mp", "dp"), None),
        P(),
        P("dp", None, "mp"),
        P(("mp", "dp")),
        P(("mp", "dp"), None),
        P(),
        P("dp", "mp"),
        P(("mp", "dp")),
        P(("mp", "dp"), None),
        P("dp", None, "mp", None),
    )

    return jax.shard_map(
        per_device,
        mesh=mesh,
        in_specs=placed,
        out_specs=(
            P("dp", None, "mp", None),
            P("dp", None, "mp", None),
            P("dp", "mp"),
            P("dp", None, "mp"),
            P(("mp", "dp"), None),
            P(("mp", "dp")),
            P("dp", None, "mp"),
            P(("mp", "dp")),
            P(("mp", "dp"), None),
            P(("mp", "dp")),
            P("dp", "mp"),
            P(("mp", "dp")),
            P(("mp", "dp"), None),
        ),
        check_vma=False,
    )
```

```python
import jax
import jax.numpy as jnp
from jax import lax
from jax.sharding import PartitionSpec as P

D = 2048
HD = 64
FF = 8192


EPS = 1e-05
GAMMA = 0.4
SCALE_BASE = 512.0
NEG = -1e30
ROOT_HALF = 0.7071067811865476
INV_ROOT_TAU = 0.3989422804014327


def doc_positions(segments):
    index = jnp.arange(segments.shape[0], dtype=jnp.int32)
    starts = jnp.concatenate([jnp.ones((1,), dtype=bool), segments[1:] != segments[:-1]])
    first = lax.cummax(jnp.where(starts, index, 0), axis=0)
    return (index - first).astype(jnp.float32)


def rotary_tables(places, head_size):
    half = head_size // 2
    steps = jnp.arange(half, dtype=jnp.float32)
    freqs = 10000.0 ** (-2.0 * steps / head_size)
    angles = places[:, None] * freqs[None, :]
    zeta = (2.0 * steps / head_size + GAMMA) / (1.0 + GAMMA)
    decay = jnp.exp(jnp.log(zeta)[None, :] * places[:, None] / SCALE_BASE)
    return (jnp.cos(angles), jnp.sin(angles), jnp.concatenate([decay, decay], axis=-1))


def rotate(values, cosine, sine):
    half = values.shape[-1] // 2
    first = values[..., :half]
    second = values[..., half:]
    cosine = cosine[:, None, :]
    sine = sine[:, None, :]
    return jnp.concatenate(
        [first * cosine - second * sine, second * cosine + first * sine], axis=-1
    )


def gelu_slope(values):
    return (
        0.5 * (1.0 + lax.erf(values * ROOT_HALF))
        + values * jnp.exp(-0.5 * values * values) * INV_ROOT_TAU
    )


def row_norm(values):
    centre = values - jnp.mean(values, axis=-1, keepdims=True)
    scale_back = lax.rsqrt(jnp.mean(centre * centre, axis=-1, keepdims=True) + EPS)
    return (centre * scale_back, scale_back)


def row_norm_back(grad_out, normed, scale_back, gain):
    scaled = grad_out * gain
    gain_grad = jnp.sum(grad_out * normed, axis=0)
    grad_in = scale_back * (
        scaled
        - jnp.mean(scaled, axis=-1, keepdims=True)
        - normed * jnp.mean(scaled * normed, axis=-1, keepdims=True)
    )
    return (grad_in, gain_grad)


def shift(values, step, size):
    return lax.ppermute(values, "mp", [(i, (i + step) % size) for i in range(size)])


def sum_slots(values, size):
    total = values
    for step in range(1, size):
        total = total + jnp.roll(shift(values, step, size), step, axis=-2)
    return total


def gather_slots(shard, size):
    if size != 4:
        return jnp.concatenate(
            [shard] + [shift(shard, step, size) for step in range(1, size)], axis=0
        )
    place = lax.axis_index("mp")
    across = lax.ppermute(shard, "mp", [(0, 2), (1, 3), (2, 0), (3, 1)])
    up = lax.ppermute(shard, "mp", [(0, 1), (1, 2), (2, 3)])
    down = lax.ppermute(shard, "mp", [(1, 0), (2, 1), (3, 2)])
    ends = lax.ppermute(across, "mp", [(2, 3), (1, 0)])
    first = jnp.where(place == 0, ends, up)
    third = jnp.where(place == 3, ends, down)
    return jnp.concatenate([shard, first, across, third], axis=0)


def scatter_slots(partial, size):
    rows = partial.shape[0] // size
    parts = [partial[k * rows : (k + 1) * rows] for k in range(size)]
    low = [part.astype(jnp.bfloat16) for part in parts]
    if size != 4:
        total = parts[0]
        for step in range(1, size):
            total = total + shift(low[step], size - step, size).astype(jnp.float32)
        return total
    place = lax.axis_index("mp")
    ends = lax.ppermute(jnp.where(place == 0, low[1], low[3]), "mp", [(0, 1), (3, 2)])
    down = lax.ppermute(low[1], "mp", [(1, 0), (2, 1), (3, 2)])
    up = lax.ppermute(low[3], "mp", [(0, 1), (1, 2), (2, 3)])
    across = lax.ppermute(
        (parts[2] + ends.astype(jnp.float32)).astype(jnp.bfloat16),
        "mp",
        [(0, 2), (1, 3), (2, 0), (3, 1)],
    )
    return (
        parts[0]
        + down.astype(jnp.float32)
        + up.astype(jnp.float32)
        + across.astype(jnp.float32)
    )


def split_norm(values, width, size):
    rows = values.shape[0]
    sums = jnp.stack([jnp.sum(values, axis=-1), jnp.sum(values * values, axis=-1)])
    sums = sum_slots(sums.reshape(2, size, rows // size), size).reshape(2, rows)
    mean = sums[0] / width
    scale_back = lax.rsqrt(sums[1] / width - mean * mean + EPS)
    return ((values - mean[:, None]) * scale_back[:, None], scale_back[:, None])


def split_norm_back(grad_out, normed, scale_back, gain, width, size):
    rows = grad_out.shape[0]
    scaled = grad_out * gain
    gain_grad = jnp.sum(grad_out * normed, axis=0)
    sums = jnp.stack([jnp.sum(scaled, axis=-1), jnp.sum(scaled * normed, axis=-1)])
    sums = sum_slots(sums.reshape(2, size, rows // size), size).reshape(2, rows) / width
    grad_in = scale_back * (scaled - sums[0][:, None] - normed * sums[1][:, None])
    return (grad_in, gain_grad)


def score_block(query, key, allowed, factor):
    scores = jnp.einsum("qhd,khd->hqk", query, key, preferred_element_type=jnp.float32) * factor
    return jnp.where(allowed[None], scores, NEG)


def attend_forward(query, key, value, allowed):
    factor = query.shape[2] ** (-0.5)
    scores = score_block(query, key, allowed, factor)
    peak = jnp.max(scores, axis=-1, keepdims=True)
    expo = jnp.exp(scores - peak)
    denom = jnp.sum(expo, axis=-1, keepdims=True)
    probs = (expo / denom).astype(jnp.bfloat16)
    outputs = jnp.einsum("hqk,khd->qhd", probs, value, preferred_element_type=jnp.float32)
    return (outputs, peak + jnp.log(denom))


def attend_backward(query, key, value, allowed, totals, grad_out):
    factor = query.shape[2] ** (-0.5)
    scores = score_block(query, key, allowed, factor)
    probs = jnp.where(allowed[None], jnp.exp(scores - totals), 0.0)
    grad_value = jnp.einsum(
        "hqk,qhd->khd", probs.astype(jnp.bfloat16), grad_out, preferred_element_type=jnp.float32
    )
    grad_probs = jnp.einsum("qhd,khd->hqk", grad_out, value, preferred_element_type=jnp.float32)
    delta = jnp.sum(probs * grad_probs, axis=-1, keepdims=True)
    grad_scores = (probs * (grad_probs - delta)).astype(jnp.bfloat16)
    grad_query = (
        jnp.einsum("hqk,khd->qhd", grad_scores, key, preferred_element_type=jnp.float32) * factor
    )
    grad_key = (
        jnp.einsum("hqk,qhd->khd", grad_scores, query, preferred_element_type=jnp.float32) * factor
    )
    return (grad_query, grad_key, grad_value)


def to_slots(values, place, size):
    columns = values.reshape(-1, size).T
    return jnp.concatenate(
        [
            lax.dynamic_index_in_dim(columns, (place - k) % size, 0, keepdims=False)
            for k in range(size)
        ]
    )


def gather_rows(values):
    return lax.all_gather(values, "dp", axis=0, tiled=True)


def scatter_rows(values):
    return lax.psum_scatter(
        values.astype(jnp.bfloat16), "dp", scatter_dimension=0, tiled=True
    ).astype(jnp.float32)


class Row:
    pass


def per_device(
    tokens,
    segment_ids,
    image_blocks,
    features,
    latent_queries,
    image_kv_weight,
    image_out_weight,
    norm1_gain,
    attn_in_weight,
    attn_norm_gain,
    attn_out_weight,
    norm2_gain,
    ffn_up_weight,
    ffn_norm_gain,
    ffn_down_weight,
    cotangent,
):
    n_model = lax.axis_size("mp")
    n_data = lax.axis_size("dp")
    place = lax.axis_index("mp")
    data_index = lax.axis_index("dp")
    micro, shard_rows, _, width = tokens.shape
    row_length = shard_rows * n_model
    gain_one = norm1_gain.astype(jnp.float32)
    gain_two = norm2_gain.astype(jnp.float32)
    n_query = latent_queries.shape[0]

    columns = latent_queries.shape[1]
    query_size = n_query * columns
    small = jnp.concatenate([latent_queries.reshape(-1), attn_norm_gain, ffn_norm_gain])
    small = jnp.pad(small, (0, -small.shape[0] % (16 * columns))).reshape(-1, columns)
    kv_rows = image_kv_weight.size // columns
    out_rows = image_out_weight.size // columns
    pack = lax.all_gather(
        jnp.concatenate(
            [image_kv_weight.reshape(-1, columns), image_out_weight.reshape(-1, columns), small]
        ),
        "dp",
        axis=0,
        tiled=True,
    ).reshape(n_data, -1, columns)
    kv_weight = pack[:, :kv_rows].reshape(-1, 2, columns)
    out_weight = pack[:, kv_rows : kv_rows + out_rows].reshape(-1, width)
    small = pack[:, kv_rows + out_rows :].reshape(n_data, -1)
    queries = small[:, :query_size].reshape(n_data * n_query, -1)
    attn_end = query_size + attn_norm_gain.shape[0]
    attn_gain = small[:, query_size:attn_end].reshape(-1).astype(jnp.float32)
    ffn_gain = small[:, attn_end : attn_end + ffn_norm_gain.shape[0]].reshape(-1)
    ffn_gain = ffn_gain.astype(jnp.float32)
    attn_in = gather_rows(attn_in_weight)
    attn_out = gather_rows(attn_out_weight)

    text = [tokens[r, :, 0, :] for r in range(micro)]
    text_in = [
        gather_slots(
            (row_norm(text[r].astype(jnp.float32))[0] * gain_one).astype(jnp.bfloat16), n_model
        )
        for r in range(micro)
    ]

    latents = queries.shape[0]
    per_model = latents // n_model
    images, patches = features.shape[:2]
    image_heads = queries.shape[1] // HD
    factor = HD ** (-0.5)
    slotted = jnp.concatenate(
        [
            lax.dynamic_index_in_dim(
                queries.reshape(per_model, n_model, -1), (place - k) % n_model, 1, keepdims=False
            )
            for k in range(n_model)
        ],
        axis=0,
    ).reshape(latents, image_heads, HD)
    keyvals = jnp.einsum(
        "ipc,ckd->ipkd", features, kv_weight, preferred_element_type=jnp.float32
    ).astype(jnp.bfloat16)
    image_keys = keyvals[:, :, 0].reshape(images, patches, image_heads, HD)
    image_values = keyvals[:, :, 1].reshape(images, patches, image_heads, HD)
    image_scores = (
        jnp.einsum("lhd,iphd->ihlp", slotted, image_keys, preferred_element_type=jnp.float32)
        * factor
    )
    image_expo = jnp.exp(image_scores - jnp.max(image_scores, axis=-1, keepdims=True))
    image_probs = image_expo / jnp.sum(image_expo, axis=-1, keepdims=True)
    image_low = image_probs.astype(jnp.bfloat16)
    pooled = (
        jnp.einsum("ihlp,iphd->ilhd", image_low, image_values, preferred_element_type=jnp.float32)
        .reshape(images, latents, -1)
        .astype(jnp.bfloat16)
    )
    pooled_late, text_in[0] = lax.optimization_barrier((pooled, text_in[0]))
    embed_part = jnp.einsum(
        "ilc,cd->lid", pooled_late, out_weight, preferred_element_type=jnp.float32
    ).reshape(latents, images * width)
    own_embeds = scatter_slots(embed_part, n_model).astype(jnp.bfloat16)
    slot_embeds = gather_slots(own_embeds, n_model)
    slot_embeds, text_in[1:] = lax.optimization_barrier((slot_embeds, text_in[1:]))
    slot_embeds = slot_embeds.reshape(latents, images, width)
    all_embeds = lax.all_gather(slot_embeds, "dp", axis=0, tiled=False)
    grads_all = lax.all_gather(cotangent[:, :, 0, :], "mp", axis=0, tiled=False)
    ffn_up = gather_rows(ffn_up_weight)
    ffn_down = gather_rows(ffn_down_weight)
    total_images = n_data * images
    all_embeds = all_embeds.transpose(0, 2, 1, 3).reshape(total_images, latents, width)
    embeds_in = (row_norm(all_embeds.astype(jnp.float32))[0] * gain_one).astype(jnp.bfloat16)
    image_index = jnp.arange(total_images, dtype=jnp.int32)
    blocks_row = shard_rows // per_model

    index = jnp.arange(row_length, dtype=jnp.int32)
    position = to_slots(index, place, n_model)
    rows = []
    for r in range(micro):
        row = Row()
        blocks = lax.dynamic_index_in_dim(
            image_blocks, data_index * micro + r, 0, keepdims=False
        )
        selector = (blocks[:, None] == image_index[None, :]).astype(jnp.bfloat16)
        row.selector = selector
        is_text = jnp.repeat(blocks == total_images, per_model)[:, None]
        row.is_text = is_text
        placed = jnp.einsum(
            "bi,isd->bsd",
            selector,
            embeds_in.reshape(total_images, n_model * per_model, width),
            preferred_element_type=jnp.float32,
        ).astype(jnp.bfloat16)
        placed = (
            placed.reshape(blocks_row, n_model, per_model, width)
            .swapaxes(0, 1)
            .reshape(row_length, width)
        )
        own_placed = jnp.einsum(
            "bi,isd->bsd",
            selector,
            all_embeds[:, :per_model],
            preferred_element_type=jnp.float32,
        ).reshape(shard_rows, width)
        start = jnp.where(is_text, text[r].astype(jnp.float32), own_placed)
        row.start = start
        row.input1 = jnp.where(jnp.tile(is_text, (n_model, 1)), text_in[r], placed)
        segments = to_slots(segment_ids[r], place, n_model)
        places = to_slots(doc_positions(segment_ids[r]), place, n_model)
        row.allowed = (position[:, None] >= position[None, :]) & (
            segments[:, None] == segments[None, :]
        )
        cosine, sine, decay = rotary_tables(places, HD)
        row.tables = (cosine, sine, decay[:, None, :])
        rows.append(row)

    local_heads = attn_in.shape[2] // HD
    outputs = []
    for r in range(micro):
        row = rows[r]
        cosine, sine, decay = row.tables
        mixed = jnp.einsum(
            "lc,ckd->lkd", row.input1, attn_in, preferred_element_type=jnp.float32
        )
        row.query = (
            rotate(mixed[:, 0].reshape(row_length, local_heads, HD), cosine, sine) * decay
        ).astype(jnp.bfloat16)
        row.key = (
            rotate(mixed[:, 1].reshape(row_length, local_heads, HD), cosine, sine) / decay
        ).astype(jnp.bfloat16)
        row.value = mixed[:, 2].reshape(row_length, local_heads, HD).astype(jnp.bfloat16)
        attended, row.totals = attend_forward(
            row.query, row.key, row.value, row.allowed
        )
        row.normed_a, row.back_a = split_norm(
            attended.reshape(row_length, -1), D, n_model
        )
        row.sub_attn = (row.normed_a * attn_gain).astype(jnp.bfloat16)
        part = jnp.dot(row.sub_attn, attn_out, preferred_element_type=jnp.float32)
        later = [other.input1 for other in rows[r + 1 :]]
        before = [other.ready for other in rows[:r]]
        part, later, _ = lax.optimization_barrier((part, later, before))
        for other, value in zip(rows[r + 1 :], later):
            other.input1 = value
        if r == micro - 1:
            _, grads_all = lax.optimization_barrier((part, grads_all))
        row.middle = row.start + scatter_slots(part, n_model)
        second = row.middle.astype(jnp.bfloat16).astype(jnp.float32)
        row.normed2, row.back2 = row_norm(second)
        row.ready = (row.normed2 * gain_two).astype(jnp.bfloat16)
        row.input2 = gather_slots(row.ready, n_model)
    branch = [
        jnp.concatenate(
            [
                lax.dynamic_index_in_dim(grads_all, (place - k) % n_model, 0, keepdims=False)[r]
                for k in range(n_model)
            ],
            axis=0,
        )
        for r in range(micro)
    ]
    ffn_gain_grad = 0.0
    attn_gain_grad = 0.0
    norm2_gain_grad = 0.0
    norm1_gain_grad = 0.0
    for r in range(micro):
        row = rows[r]
        row.hidden = jnp.dot(row.input2, ffn_up, preferred_element_type=jnp.float32)
        row.normed_f, row.back_f = split_norm(
            jax.nn.gelu(row.hidden, approximate=False), FF, n_model
        )
        row.sub_ffn = (row.normed_f * ffn_gain).astype(jnp.bfloat16)
        part = jnp.dot(row.sub_ffn, ffn_down, preferred_element_type=jnp.float32)
        outputs.append((row.middle + scatter_slots(part, n_model)).astype(jnp.bfloat16))
        grad_sub = jnp.einsum(
            "ld,fd->lf", branch[r], ffn_down, preferred_element_type=jnp.float32
        )
        grad_active, gain_part = split_norm_back(
            grad_sub, row.normed_f, row.back_f, ffn_gain, FF, n_model
        )
        ffn_gain_grad = ffn_gain_grad + gain_part
        row.grad_hidden = (grad_active * gelu_slope(row.hidden)).astype(jnp.bfloat16)
        grad_input2 = jnp.einsum(
            "lf,cf->lc", row.grad_hidden, ffn_up, preferred_element_type=jnp.float32
        )
        later = [other.input2 for other in rows[r + 1 :]]
        before = [other.landed for other in rows[:r]]
        grad_input2, later, _ = lax.optimization_barrier((grad_input2, later, before))
        for other, value in zip(rows[r + 1 :], later):
            other.input2 = value
        share, gain_part = row_norm_back(
            scatter_slots(grad_input2, n_model), row.normed2, row.back2, gain_two
        )
        norm2_gain_grad = norm2_gain_grad + gain_part
        row.grad_middle = cotangent[r, :, 0, :].astype(jnp.float32) + share
        row.landed = row.grad_middle.astype(jnp.bfloat16)
        row.grad_out = gather_slots(row.landed, n_model)

    def both(values):
        return jnp.concatenate(values, axis=0)

    down_part = jnp.einsum(
        "lf,ld->fd",
        both([row.sub_ffn for row in rows]),
        jnp.concatenate(branch, axis=0),
        preferred_element_type=jnp.float32,
    ).astype(jnp.bfloat16)
    up_part = jnp.einsum(
        "lc,lf->cf", both([row.input2 for row in rows]), both([row.grad_hidden for row in rows]), preferred_element_type=jnp.float32
    ).astype(jnp.bfloat16)
    _, rows[0].grad_out = lax.optimization_barrier((down_part, rows[0].grad_out))
    _, rows[-1].grad_out = lax.optimization_barrier((up_part, rows[-1].grad_out))
    ffn_down_grad = scatter_rows(down_part)
    ffn_up_grad = scatter_rows(up_part)
    attn_out_part = jnp.einsum(
        "lc,ld->cd", both([row.sub_attn for row in rows]), both([row.grad_out for row in rows]), preferred_element_type=jnp.float32
    ).astype(jnp.bfloat16)
    token_grads = []
    grad_table = jnp.zeros((per_model, total_images, width), jnp.float32)
    for r in range(micro):
        row = rows[r]
        cosine, sine, decay = row.tables
        grad_sub_attn = jnp.einsum(
            "ld,cd->lc", row.grad_out, attn_out, preferred_element_type=jnp.float32
        )
        grad_attended, gain_part = split_norm_back(
            grad_sub_attn, row.normed_a, row.back_a, attn_gain, D, n_model
        )
        attn_gain_grad = attn_gain_grad + gain_part
        grad_query, grad_key, grad_value = attend_backward(
            row.query,
            row.key,
            row.value,
            row.allowed,
            row.totals,
            grad_attended.astype(jnp.bfloat16).reshape(row_length, local_heads, HD),
        )
        row.grad_mixed = (
            jnp.stack(
                [
                    rotate(grad_query * decay, cosine, -sine),
                    rotate(grad_key / decay, cosine, -sine),
                    grad_value,
                ],
                axis=1,
            )
            .reshape(row_length, 3, -1)
            .astype(jnp.bfloat16)
        )
        grad_input1 = jnp.einsum(
            "lkd,ckd->lc", row.grad_mixed, attn_in, preferred_element_type=jnp.float32
        )
        if r < micro - 1:
            later = [other.grad_out for other in rows[r + 1 :]]
            grad_input1, later = lax.optimization_barrier((grad_input1, later))
            for other, value in zip(rows[r + 1 :], later):
                other.grad_out = value
        else:
            before = [other.share for other in rows[:r]]
            grad_input1, _, _ = lax.optimization_barrier((grad_input1, attn_out_part, before))
        normed1, back1 = row_norm(row.start)
        share, gain_part = row_norm_back(
            scatter_slots(grad_input1, n_model), normed1, back1, gain_one
        )
        row.share = share
        norm1_gain_grad = norm1_gain_grad + gain_part
        grad_start = row.grad_middle + share
        token_grads.append(jnp.where(row.is_text, grad_start, 0.0))
        grad_table = grad_table + jnp.einsum(
            "bi,bsd->sid",
            row.selector,
            grad_start.astype(jnp.bfloat16).reshape(blocks_row, per_model, width),
            preferred_element_type=jnp.float32,
        )
    attn_out_grad = scatter_rows(attn_out_part)
    attn_in_part = jnp.einsum(
        "lc,lkd->ckd",
        both([row.input1 for row in rows]),
        both([row.grad_mixed for row in rows]),
        preferred_element_type=jnp.float32,
    ).astype(jnp.bfloat16)
    attn_in_grad = scatter_rows(attn_in_part)

    share_grad = lax.psum_scatter(
        grad_table.astype(jnp.bfloat16), "dp", scatter_dimension=1, tiled=True
    )
    embed_grad = gather_slots(share_grad.reshape(per_model, images * width), n_model).reshape(
        latents, images, width
    )
    out_grad = jnp.einsum("ilc,lid->cd", pooled, embed_grad, preferred_element_type=jnp.float32)
    grad_pooled = (
        jnp.einsum("lid,cd->ilc", embed_grad, out_weight, preferred_element_type=jnp.float32)
        .astype(jnp.bfloat16)
        .reshape(images, latents, image_heads, HD)
    )
    grad_values = jnp.einsum(
        "ihlp,ilhd->iphd", image_low, grad_pooled, preferred_element_type=jnp.float32
    )
    grad_probs = jnp.einsum(
        "ilhd,iphd->ihlp", grad_pooled, image_values, preferred_element_type=jnp.float32
    )
    delta = jnp.sum(image_probs * grad_probs, axis=-1, keepdims=True)
    grad_scores = (image_probs * (grad_probs - delta)).astype(jnp.bfloat16)
    grad_latent = (
        jnp.einsum("ihlp,iphd->lhd", grad_scores, image_keys, preferred_element_type=jnp.float32)
        * factor
    )
    grad_keys = (
        jnp.einsum("ihlp,lhd->iphd", grad_scores, slotted, preferred_element_type=jnp.float32)
        * factor
    )
    grad_keyvals = jnp.stack(
        [grad_keys.reshape(images, patches, -1), grad_values.reshape(images, patches, -1)], axis=2
    ).astype(jnp.bfloat16)
    kv_grad = jnp.einsum(
        "ipc,ipkd->ckd", features, grad_keyvals, preferred_element_type=jnp.float32
    )
    slot_grad = grad_latent.reshape(n_model, per_model, -1)
    query_grad = jnp.stack(
        [
            lax.dynamic_index_in_dim(slot_grad, (place - m) % n_model, 0, keepdims=False)
            for m in range(n_model)
        ],
        axis=1,
    ).reshape(latents, -1)
    gains = jnp.stack([norm1_gain_grad, norm2_gain_grad]).reshape(2, n_model, -1)
    own = 0.0
    for step in range(n_model):
        chunk = lax.dynamic_index_in_dim(gains, (place + step) % n_model, 1, keepdims=False)
        own = own + (chunk if step == 0 else shift(chunk, step, n_model))
    pieces = [
        piece.astype(jnp.bfloat16).reshape(n_data, -1)
        for piece in (
            kv_grad,
            out_grad,
            query_grad,
            own[0],
            own[1],
            attn_gain_grad,
            ffn_gain_grad,
        )
    ]
    packed = jnp.concatenate(pieces, axis=1)
    packed = jnp.pad(packed, ((0, 0), (0, -packed.shape[1] % 2048))).reshape(n_data, -1, 128)
    packed, outputs = lax.optimization_barrier((packed, outputs))
    packed = lax.psum_scatter(packed, "dp", scatter_dimension=0, tiled=True)
    packed = packed.reshape(-1).astype(jnp.float32)
    split = []
    begin = 0
    for piece in pieces:
        split.append(packed[begin : begin + piece.shape[1]])
        begin += piece.shape[1]
    return (
        jnp.stack(outputs)[:, :, None, :],
        jnp.stack(token_grads)[:, :, None, :],
        split[2].reshape(latent_queries.shape),
        split[0].reshape(image_kv_weight.shape),
        split[1].reshape(image_out_weight.shape),
        split[3],
        attn_in_grad,
        split[5],
        attn_out_grad,
        split[4],
        ffn_up_grad,
        split[6],
        ffn_down_grad,
    )


def solution(mesh):
    placed = (
        P("dp", None, "mp", None),
        P("dp", None),
        P(),
        P("dp", None, None),
        P("dp", "mp"),
        P("dp", None, "mp"),
        P(("mp", "dp"), None),
        P(),
        P("dp", None, "mp"),
        P(("mp", "dp")),
        P(("mp", "dp"), None),
        P(),
        P("dp", "mp"),
        P(("mp", "dp")),
        P(("mp", "dp"), None),
        P("dp", None, "mp", None),
    )

    return jax.shard_map(
        per_device,
        mesh=mesh,
        in_specs=placed,
        out_specs=(
            P("dp", None, "mp", None),
            P("dp", None, "mp", None),
            P("dp", "mp"),
            P("dp", None, "mp"),
            P(("mp", "dp"), None),
            P(("mp", "dp")),
            P("dp", None, "mp"),
            P(("mp", "dp")),
            P(("mp", "dp"), None),
            P(("mp", "dp")),
            P("dp", "mp"),
            P(("mp", "dp")),
            P(("mp", "dp"), None),
        ),
        check_vma=False,
    )
```

```python
import jax
import jax.numpy as jnp
from jax import lax
from jax.sharding import PartitionSpec as P

D = 2048
HD = 64
FF = 8192


EPS = 1e-05
GAMMA = 0.4
SCALE_BASE = 512.0
NEG = -1e30
ROOT_HALF = 0.7071067811865476
INV_ROOT_TAU = 0.3989422804014327


def doc_positions(segments):
    index = jnp.arange(segments.shape[0], dtype=jnp.int32)
    starts = jnp.concatenate([jnp.ones((1,), dtype=bool), segments[1:] != segments[:-1]])
    first = lax.cummax(jnp.where(starts, index, 0), axis=0)
    return (index - first).astype(jnp.float32)


def rotary_tables(places, head_size):
    half = head_size // 2
    steps = jnp.arange(half, dtype=jnp.float32)
    freqs = 10000.0 ** (-2.0 * steps / head_size)
    angles = places[:, None] * freqs[None, :]
    zeta = (2.0 * steps / head_size + GAMMA) / (1.0 + GAMMA)
    decay = jnp.exp(jnp.log(zeta)[None, :] * places[:, None] / SCALE_BASE)
    return (jnp.cos(angles), jnp.sin(angles), jnp.concatenate([decay, decay], axis=-1))


def rotate(values, cosine, sine):
    half = values.shape[-1] // 2
    first = values[..., :half]
    second = values[..., half:]
    cosine = cosine[:, None, :]
    sine = sine[:, None, :]
    return jnp.concatenate(
        [first * cosine - second * sine, second * cosine + first * sine], axis=-1
    )


def gelu_slope(values):
    return (
        0.5 * (1.0 + lax.erf(values * ROOT_HALF))
        + values * jnp.exp(-0.5 * values * values) * INV_ROOT_TAU
    )


def row_norm(values):
    centre = values - jnp.mean(values, axis=-1, keepdims=True)
    scale_back = lax.rsqrt(jnp.mean(centre * centre, axis=-1, keepdims=True) + EPS)
    return (centre * scale_back, scale_back)


def row_norm_back(grad_out, normed, scale_back, gain):
    scaled = grad_out * gain
    gain_grad = jnp.sum(grad_out * normed, axis=0)
    grad_in = scale_back * (
        scaled
        - jnp.mean(scaled, axis=-1, keepdims=True)
        - normed * jnp.mean(scaled * normed, axis=-1, keepdims=True)
    )
    return (grad_in, gain_grad)


def shift(values, step, size):
    return lax.ppermute(values, "mp", [(i, (i + step) % size) for i in range(size)])


def sum_slots(values, size):
    total = values
    for step in range(1, size):
        total = total + jnp.roll(shift(values, step, size), step, axis=-2)
    return total


def gather_slots(shard, size):
    if size != 4:
        return jnp.concatenate(
            [shard] + [shift(shard, step, size) for step in range(1, size)], axis=0
        )
    place = lax.axis_index("mp")
    across = lax.ppermute(shard, "mp", [(0, 2), (1, 3), (2, 0), (3, 1)])
    up = lax.ppermute(shard, "mp", [(0, 1), (1, 2), (2, 3)])
    down = lax.ppermute(shard, "mp", [(1, 0), (2, 1), (3, 2)])
    ends = lax.ppermute(across, "mp", [(2, 3), (1, 0)])
    first = jnp.where(place == 0, ends, up)
    third = jnp.where(place == 3, ends, down)
    return jnp.concatenate([shard, first, across, third], axis=0)


def scatter_slots(partial, size, after=()):
    rows = partial.shape[0] // size
    parts = [partial[k * rows : (k + 1) * rows] for k in range(size)]
    low = [part.astype(jnp.bfloat16) for part in parts]
    if size != 4:
        total = parts[0]
        for step in range(1, size):
            total = total + shift(low[step], size - step, size).astype(jnp.float32)
        return total
    place = lax.axis_index("mp")
    ends = lax.ppermute(jnp.where(place == 0, low[1], low[3]), "mp", [(0, 1), (3, 2)])
    down = lax.ppermute(low[1], "mp", [(1, 0), (2, 1), (3, 2)])
    up = lax.ppermute(low[3], "mp", [(0, 1), (1, 2), (2, 3)])
    across = lax.ppermute(
        (parts[2] + ends.astype(jnp.float32)).astype(jnp.bfloat16),
        "mp",
        [(0, 2), (1, 3), (2, 0), (3, 1)],
    )
    down, up, across, _ = lax.optimization_barrier((down, up, across, after))
    return (
        parts[0]
        + down.astype(jnp.float32)
        + up.astype(jnp.float32)
        + across.astype(jnp.float32)
    )


def split_norm(values, width, size):
    rows = values.shape[0]
    sums = jnp.stack([jnp.sum(values, axis=-1), jnp.sum(values * values, axis=-1)])
    sums = sum_slots(sums.reshape(2, size, rows // size), size).reshape(2, rows)
    mean = sums[0] / width
    scale_back = lax.rsqrt(sums[1] / width - mean * mean + EPS)
    return ((values - mean[:, None]) * scale_back[:, None], scale_back[:, None])


def split_norm_back(grad_out, normed, scale_back, gain, width, size):
    rows = grad_out.shape[0]
    scaled = grad_out * gain
    gain_grad = jnp.sum(grad_out * normed, axis=0)
    sums = jnp.stack([jnp.sum(scaled, axis=-1), jnp.sum(scaled * normed, axis=-1)])
    sums = sum_slots(sums.reshape(2, size, rows // size), size).reshape(2, rows) / width
    grad_in = scale_back * (scaled - sums[0][:, None] - normed * sums[1][:, None])
    return (grad_in, gain_grad)


def score_block(query, key, allowed, factor):
    scores = jnp.einsum("qhd,khd->hqk", query, key, preferred_element_type=jnp.float32) * factor
    return jnp.where(allowed[None], scores, NEG)


def attend_forward(query, key, value, allowed):
    factor = query.shape[2] ** (-0.5)
    scores = score_block(query, key, allowed, factor)
    peak = jnp.max(scores, axis=-1, keepdims=True)
    expo = jnp.exp(scores - peak)
    denom = jnp.sum(expo, axis=-1, keepdims=True)
    probs = (expo / denom).astype(jnp.bfloat16)
    outputs = jnp.einsum("hqk,khd->qhd", probs, value, preferred_element_type=jnp.float32)
    return (outputs, peak + jnp.log(denom))


def attend_backward(query, key, value, allowed, totals, grad_out):
    factor = query.shape[2] ** (-0.5)
    scores = score_block(query, key, allowed, factor)
    probs = jnp.where(allowed[None], jnp.exp(scores - totals), 0.0)
    grad_value = jnp.einsum(
        "hqk,qhd->khd", probs.astype(jnp.bfloat16), grad_out, preferred_element_type=jnp.float32
    )
    grad_probs = jnp.einsum("qhd,khd->hqk", grad_out, value, preferred_element_type=jnp.float32)
    delta = jnp.sum(probs * grad_probs, axis=-1, keepdims=True)
    grad_scores = (probs * (grad_probs - delta)).astype(jnp.bfloat16)
    grad_query = (
        jnp.einsum("hqk,khd->qhd", grad_scores, key, preferred_element_type=jnp.float32) * factor
    )
    grad_key = (
        jnp.einsum("hqk,qhd->khd", grad_scores, query, preferred_element_type=jnp.float32) * factor
    )
    return (grad_query, grad_key, grad_value)


def to_slots(values, place, size):
    columns = values.reshape(-1, size).T
    return jnp.concatenate(
        [
            lax.dynamic_index_in_dim(columns, (place - k) % size, 0, keepdims=False)
            for k in range(size)
        ]
    )


def gather_rows(values):
    return lax.all_gather(values, "dp", axis=0, tiled=True)


def scatter_rows(values):
    return lax.psum_scatter(
        values.astype(jnp.bfloat16), "dp", scatter_dimension=0, tiled=True
    ).astype(jnp.float32)


class Row:
    pass


def per_device(
    tokens,
    segment_ids,
    image_blocks,
    features,
    latent_queries,
    image_kv_weight,
    image_out_weight,
    norm1_gain,
    attn_in_weight,
    attn_norm_gain,
    attn_out_weight,
    norm2_gain,
    ffn_up_weight,
    ffn_norm_gain,
    ffn_down_weight,
    cotangent,
):
    n_model = lax.axis_size("mp")
    n_data = lax.axis_size("dp")
    place = lax.axis_index("mp")
    data_index = lax.axis_index("dp")
    micro, shard_rows, _, width = tokens.shape
    row_length = shard_rows * n_model
    gain_one = norm1_gain.astype(jnp.float32)
    gain_two = norm2_gain.astype(jnp.float32)
    n_query = latent_queries.shape[0]

    columns = latent_queries.shape[1]
    query_size = n_query * columns
    small = jnp.concatenate([latent_queries.reshape(-1), attn_norm_gain, ffn_norm_gain])
    small = jnp.pad(small, (0, -small.shape[0] % (16 * columns))).reshape(-1, columns)
    kv_rows = image_kv_weight.size // columns
    out_rows = image_out_weight.size // columns
    pack = lax.all_gather(
        jnp.concatenate(
            [image_kv_weight.reshape(-1, columns), image_out_weight.reshape(-1, columns), small]
        ),
        "dp",
        axis=0,
        tiled=True,
    ).reshape(n_data, -1, columns)
    kv_weight = pack[:, :kv_rows].reshape(-1, 2, columns)
    out_weight = pack[:, kv_rows : kv_rows + out_rows].reshape(-1, width)
    small = pack[:, kv_rows + out_rows :].reshape(n_data, -1)
    queries = small[:, :query_size].reshape(n_data * n_query, -1)
    attn_end = query_size + attn_norm_gain.shape[0]
    attn_gain = small[:, query_size:attn_end].reshape(-1).astype(jnp.float32)
    ffn_gain = small[:, attn_end : attn_end + ffn_norm_gain.shape[0]].reshape(-1)
    ffn_gain = ffn_gain.astype(jnp.float32)
    attn_in = gather_rows(attn_in_weight)
    attn_out = gather_rows(attn_out_weight)

    text = [tokens[r, :, 0, :] for r in range(micro)]
    text_in = [
        gather_slots(
            (row_norm(text[r].astype(jnp.float32))[0] * gain_one).astype(jnp.bfloat16), n_model
        )
        for r in range(micro)
    ]

    latents = queries.shape[0]
    per_model = latents // n_model
    images, patches = features.shape[:2]
    image_heads = queries.shape[1] // HD
    factor = HD ** (-0.5)
    slotted = jnp.concatenate(
        [
            lax.dynamic_index_in_dim(
                queries.reshape(per_model, n_model, -1), (place - k) % n_model, 1, keepdims=False
            )
            for k in range(n_model)
        ],
        axis=0,
    ).reshape(latents, image_heads, HD)
    keyvals = jnp.einsum(
        "ipc,ckd->ipkd", features, kv_weight, preferred_element_type=jnp.float32
    ).astype(jnp.bfloat16)
    image_keys = keyvals[:, :, 0].reshape(images, patches, image_heads, HD)
    image_values = keyvals[:, :, 1].reshape(images, patches, image_heads, HD)
    image_scores = (
        jnp.einsum("lhd,iphd->ihlp", slotted, image_keys, preferred_element_type=jnp.float32)
        * factor
    )
    image_expo = jnp.exp(image_scores - jnp.max(image_scores, axis=-1, keepdims=True))
    image_probs = image_expo / jnp.sum(image_expo, axis=-1, keepdims=True)
    image_low = image_probs.astype(jnp.bfloat16)
    pooled = (
        jnp.einsum("ihlp,iphd->ilhd", image_low, image_values, preferred_element_type=jnp.float32)
        .reshape(images, latents, -1)
        .astype(jnp.bfloat16)
    )
    pooled_late, text_in[0] = lax.optimization_barrier((pooled, text_in[0]))
    embed_part = jnp.einsum(
        "ilc,cd->lid", pooled_late, out_weight, preferred_element_type=jnp.float32
    ).reshape(latents, images * width)
    own_embeds = scatter_slots(embed_part, n_model).astype(jnp.bfloat16)
    slot_embeds = gather_slots(own_embeds, n_model)
    slot_embeds, text_in[1:] = lax.optimization_barrier((slot_embeds, text_in[1:]))
    slot_embeds = slot_embeds.reshape(latents, images, width)
    all_embeds = lax.all_gather(slot_embeds, "dp", axis=0, tiled=False)
    grads_all = lax.all_gather(cotangent[:, :, 0, :], "mp", axis=0, tiled=False)
    ffn_up = gather_rows(ffn_up_weight)
    ffn_down = gather_rows(ffn_down_weight)
    total_images = n_data * images
    all_embeds = all_embeds.transpose(0, 2, 1, 3).reshape(total_images, latents, width)
    embeds_in = (row_norm(all_embeds.astype(jnp.float32))[0] * gain_one).astype(jnp.bfloat16)
    image_index = jnp.arange(total_images, dtype=jnp.int32)
    blocks_row = shard_rows // per_model

    index = jnp.arange(row_length, dtype=jnp.int32)
    position = to_slots(index, place, n_model)
    rows = []
    for r in range(micro):
        row = Row()
        blocks = lax.dynamic_index_in_dim(
            image_blocks, data_index * micro + r, 0, keepdims=False
        )
        selector = (blocks[:, None] == image_index[None, :]).astype(jnp.bfloat16)
        row.selector = selector
        is_text = jnp.repeat(blocks == total_images, per_model)[:, None]
        row.is_text = is_text
        placed = jnp.einsum(
            "bi,isd->bsd",
            selector,
            embeds_in.reshape(total_images, n_model * per_model, width),
            preferred_element_type=jnp.float32,
        ).astype(jnp.bfloat16)
        placed = (
            placed.reshape(blocks_row, n_model, per_model, width)
            .swapaxes(0, 1)
            .reshape(row_length, width)
        )
        own_placed = jnp.einsum(
            "bi,isd->bsd",
            selector,
            all_embeds[:, :per_model],
            preferred_element_type=jnp.float32,
        ).reshape(shard_rows, width)
        start = jnp.where(is_text, text[r].astype(jnp.float32), own_placed)
        row.start = start
        row.input1 = jnp.where(jnp.tile(is_text, (n_model, 1)), text_in[r], placed)
        segments = to_slots(segment_ids[r], place, n_model)
        places = to_slots(doc_positions(segment_ids[r]), place, n_model)
        row.allowed = (position[:, None] >= position[None, :]) & (
            segments[:, None] == segments[None, :]
        )
        cosine, sine, decay = rotary_tables(places, HD)
        row.tables = (cosine, sine, decay[:, None, :])
        rows.append(row)

    local_heads = attn_in.shape[2] // HD
    outputs = []
    for r in range(micro):
        row = rows[r]
        cosine, sine, decay = row.tables
        mixed = jnp.einsum(
            "lc,ckd->lkd", row.input1, attn_in, preferred_element_type=jnp.float32
        )
        row.query = (
            rotate(mixed[:, 0].reshape(row_length, local_heads, HD), cosine, sine) * decay
        ).astype(jnp.bfloat16)
        row.key = (
            rotate(mixed[:, 1].reshape(row_length, local_heads, HD), cosine, sine) / decay
        ).astype(jnp.bfloat16)
        row.value = mixed[:, 2].reshape(row_length, local_heads, HD).astype(jnp.bfloat16)
        attended, row.totals = attend_forward(
            row.query, row.key, row.value, row.allowed
        )
        row.normed_a, row.back_a = split_norm(
            attended.reshape(row_length, -1), D, n_model
        )
        row.sub_attn = (row.normed_a * attn_gain).astype(jnp.bfloat16)
        part = jnp.dot(row.sub_attn, attn_out, preferred_element_type=jnp.float32)
        later = [other.input1 for other in rows[r + 1 :]]
        before = [other.ready for other in rows[:r]]
        part, later, _ = lax.optimization_barrier((part, later, before))
        for other, value in zip(rows[r + 1 :], later):
            other.input1 = value
        if r == micro - 1:
            _, grads_all = lax.optimization_barrier((part, grads_all))
        earlier = [other.hidden for other in rows[: min(r, 1)]]
        row.middle = row.start + scatter_slots(part, n_model, earlier)
        second = row.middle.astype(jnp.bfloat16).astype(jnp.float32)
        row.normed2, row.back2 = row_norm(second)
        row.ready = (row.normed2 * gain_two).astype(jnp.bfloat16)
        row.input2 = gather_slots(row.ready, n_model)
        if r == 0:
            row.hidden = jnp.dot(row.input2, ffn_up, preferred_element_type=jnp.float32)
    branch = [
        jnp.concatenate(
            [
                lax.dynamic_index_in_dim(grads_all, (place - k) % n_model, 0, keepdims=False)[r]
                for k in range(n_model)
            ],
            axis=0,
        )
        for r in range(micro)
    ]
    ffn_gain_grad = 0.0
    attn_gain_grad = 0.0
    norm2_gain_grad = 0.0
    norm1_gain_grad = 0.0
    for r in range(micro):
        row = rows[r]
        if r > 0:
            row.hidden = jnp.dot(row.input2, ffn_up, preferred_element_type=jnp.float32)
        row.normed_f, row.back_f = split_norm(
            jax.nn.gelu(row.hidden, approximate=False), FF, n_model
        )
        row.sub_ffn = (row.normed_f * ffn_gain).astype(jnp.bfloat16)
        grad_sub = jnp.einsum(
            "ld,fd->lf", branch[r], ffn_down, preferred_element_type=jnp.float32
        )
        grad_active, gain_part = split_norm_back(
            grad_sub, row.normed_f, row.back_f, ffn_gain, FF, n_model
        )
        ffn_gain_grad = ffn_gain_grad + gain_part
        row.grad_hidden = (grad_active * gelu_slope(row.hidden)).astype(jnp.bfloat16)
        grad_input2 = jnp.einsum(
            "lf,cf->lc", row.grad_hidden, ffn_up, preferred_element_type=jnp.float32
        )
        later = [other.input2 for other in rows[r + 1 :]]
        before = [other.landed for other in rows[:r]]
        grad_input2, later, _ = lax.optimization_barrier((grad_input2, later, before))
        for other, value in zip(rows[r + 1 :], later):
            other.input2 = value
        share, gain_part = row_norm_back(
            scatter_slots(grad_input2, n_model), row.normed2, row.back2, gain_two
        )
        norm2_gain_grad = norm2_gain_grad + gain_part
        row.grad_middle = cotangent[r, :, 0, :].astype(jnp.float32) + share
        row.landed = row.grad_middle.astype(jnp.bfloat16)
        row.grad_out = gather_slots(row.landed, n_model)

    def both(values):
        return jnp.concatenate(values, axis=0)

    down_part = jnp.einsum(
        "lf,ld->fd",
        both([row.sub_ffn for row in rows]),
        jnp.concatenate(branch, axis=0),
        preferred_element_type=jnp.float32,
    ).astype(jnp.bfloat16)
    up_part = jnp.einsum(
        "lc,lf->cf", both([row.input2 for row in rows]), both([row.grad_hidden for row in rows]), preferred_element_type=jnp.float32
    ).astype(jnp.bfloat16)
    _, rows[0].grad_out = lax.optimization_barrier((down_part, rows[0].grad_out))
    _, rows[-1].grad_out = lax.optimization_barrier((up_part, rows[-1].grad_out))
    ffn_down_grad = scatter_rows(down_part)
    ffn_up_grad = scatter_rows(up_part)
    attn_out_part = jnp.einsum(
        "lc,ld->cd", both([row.sub_attn for row in rows]), both([row.grad_out for row in rows]), preferred_element_type=jnp.float32
    ).astype(jnp.bfloat16)
    token_grads = []
    grad_table = jnp.zeros((per_model, total_images, width), jnp.float32)
    for r in range(micro):
        row = rows[r]
        cosine, sine, decay = row.tables
        grad_sub_attn = jnp.einsum(
            "ld,cd->lc", row.grad_out, attn_out, preferred_element_type=jnp.float32
        )
        grad_attended, gain_part = split_norm_back(
            grad_sub_attn, row.normed_a, row.back_a, attn_gain, D, n_model
        )
        attn_gain_grad = attn_gain_grad + gain_part
        grad_query, grad_key, grad_value = attend_backward(
            row.query,
            row.key,
            row.value,
            row.allowed,
            row.totals,
            grad_attended.astype(jnp.bfloat16).reshape(row_length, local_heads, HD),
        )
        row.grad_mixed = (
            jnp.stack(
                [
                    rotate(grad_query * decay, cosine, -sine),
                    rotate(grad_key / decay, cosine, -sine),
                    grad_value,
                ],
                axis=1,
            )
            .reshape(row_length, 3, -1)
            .astype(jnp.bfloat16)
        )
        before = [other.share for other in rows[:r]]
        mixed_late, _ = lax.optimization_barrier((row.grad_mixed, before))
        grad_input1 = jnp.einsum(
            "lkd,ckd->lc", mixed_late, attn_in, preferred_element_type=jnp.float32
        )
        if r < micro - 1:
            later = [other.grad_out for other in rows[r + 1 :]]
            grad_input1, later = lax.optimization_barrier((grad_input1, later))
            for other, value in zip(rows[r + 1 :], later):
                other.grad_out = value
        else:
            grad_input1, _ = lax.optimization_barrier((grad_input1, attn_out_part))
        normed1, back1 = row_norm(row.start)
        share, gain_part = row_norm_back(
            scatter_slots(grad_input1, n_model), normed1, back1, gain_one
        )
        row.share = share
        norm1_gain_grad = norm1_gain_grad + gain_part
        grad_start = row.grad_middle + share
        token_grads.append(jnp.where(row.is_text, grad_start, 0.0))
        grad_table = grad_table + jnp.einsum(
            "bi,bsd->sid",
            row.selector,
            grad_start.astype(jnp.bfloat16).reshape(blocks_row, per_model, width),
            preferred_element_type=jnp.float32,
        )
    attn_out_grad = scatter_rows(attn_out_part)
    attn_in_part = jnp.einsum(
        "lc,lkd->ckd",
        both([row.input1 for row in rows]),
        both([row.grad_mixed for row in rows]),
        preferred_element_type=jnp.float32,
    ).astype(jnp.bfloat16)
    attn_in_grad = scatter_rows(attn_in_part)

    for row in rows:
        late, _ = lax.optimization_barrier((row.sub_ffn, grad_table))
        part = jnp.dot(late, ffn_down, preferred_element_type=jnp.float32)
        outputs.append((row.middle + scatter_slots(part, n_model)).astype(jnp.bfloat16))

    share_grad = lax.psum_scatter(
        grad_table.astype(jnp.bfloat16), "dp", scatter_dimension=1, tiled=True
    )
    embed_grad = gather_slots(share_grad.reshape(per_model, images * width), n_model).reshape(
        latents, images, width
    )
    out_grad = jnp.einsum("ilc,lid->cd", pooled, embed_grad, preferred_element_type=jnp.float32)
    grad_pooled = (
        jnp.einsum("lid,cd->ilc", embed_grad, out_weight, preferred_element_type=jnp.float32)
        .astype(jnp.bfloat16)
        .reshape(images, latents, image_heads, HD)
    )
    grad_values = jnp.einsum(
        "ihlp,ilhd->iphd", image_low, grad_pooled, preferred_element_type=jnp.float32
    )
    grad_probs = jnp.einsum(
        "ilhd,iphd->ihlp", grad_pooled, image_values, preferred_element_type=jnp.float32
    )
    delta = jnp.sum(image_probs * grad_probs, axis=-1, keepdims=True)
    grad_scores = (image_probs * (grad_probs - delta)).astype(jnp.bfloat16)
    grad_latent = (
        jnp.einsum("ihlp,iphd->lhd", grad_scores, image_keys, preferred_element_type=jnp.float32)
        * factor
    )
    grad_keys = (
        jnp.einsum("ihlp,lhd->iphd", grad_scores, slotted, preferred_element_type=jnp.float32)
        * factor
    )
    grad_keyvals = jnp.stack(
        [grad_keys.reshape(images, patches, -1), grad_values.reshape(images, patches, -1)], axis=2
    ).astype(jnp.bfloat16)
    kv_grad = jnp.einsum(
        "ipc,ipkd->ckd", features, grad_keyvals, preferred_element_type=jnp.float32
    )
    slot_grad = grad_latent.reshape(n_model, per_model, -1)
    query_grad = jnp.stack(
        [
            lax.dynamic_index_in_dim(slot_grad, (place - m) % n_model, 0, keepdims=False)
            for m in range(n_model)
        ],
        axis=1,
    ).reshape(latents, -1)
    gains = jnp.stack([norm1_gain_grad, norm2_gain_grad]).reshape(2, n_model, -1)
    own = 0.0
    for step in range(n_model):
        chunk = lax.dynamic_index_in_dim(gains, (place + step) % n_model, 1, keepdims=False)
        own = own + (chunk if step == 0 else shift(chunk, step, n_model))
    pieces = [
        piece.astype(jnp.bfloat16).reshape(n_data, -1)
        for piece in (
            kv_grad,
            out_grad,
            query_grad,
            own[0],
            own[1],
            attn_gain_grad,
            ffn_gain_grad,
        )
    ]
    packed = jnp.concatenate(pieces, axis=1)
    packed = jnp.pad(packed, ((0, 0), (0, -packed.shape[1] % 2048))).reshape(n_data, -1, 128)
    packed, outputs = lax.optimization_barrier((packed, outputs))
    packed = lax.psum_scatter(packed, "dp", scatter_dimension=0, tiled=True)
    packed = packed.reshape(-1).astype(jnp.float32)
    split = []
    begin = 0
    for piece in pieces:
        split.append(packed[begin : begin + piece.shape[1]])
        begin += piece.shape[1]
    return (
        jnp.stack(outputs)[:, :, None, :],
        jnp.stack(token_grads)[:, :, None, :],
        split[2].reshape(latent_queries.shape),
        split[0].reshape(image_kv_weight.shape),
        split[1].reshape(image_out_weight.shape),
        split[3],
        attn_in_grad,
        split[5],
        attn_out_grad,
        split[4],
        ffn_up_grad,
        split[6],
        ffn_down_grad,
    )


def solution(mesh):
    placed = (
        P("dp", None, "mp", None),
        P("dp", None),
        P(),
        P("dp", None, None),
        P("dp", "mp"),
        P("dp", None, "mp"),
        P(("mp", "dp"), None),
        P(),
        P("dp", None, "mp"),
        P(("mp", "dp")),
        P(("mp", "dp"), None),
        P(),
        P("dp", "mp"),
        P(("mp", "dp")),
        P(("mp", "dp"), None),
        P("dp", None, "mp", None),
    )

    return jax.shard_map(
        per_device,
        mesh=mesh,
        in_specs=placed,
        out_specs=(
            P("dp", None, "mp", None),
            P("dp", None, "mp", None),
            P("dp", "mp"),
            P("dp", None, "mp"),
            P(("mp", "dp"), None),
            P(("mp", "dp")),
            P("dp", None, "mp"),
            P(("mp", "dp")),
            P(("mp", "dp"), None),
            P(("mp", "dp")),
            P("dp", "mp"),
            P(("mp", "dp")),
            P(("mp", "dp"), None),
        ),
        check_vma=False,
    )
```

```python
import jax
import jax.numpy as jnp
from jax import lax
from jax.sharding import PartitionSpec as P

D = 2048
HD = 64
FF = 8192


EPS = 1e-05
GAMMA = 0.4
SCALE_BASE = 512.0
NEG = -1e30
ROOT_HALF = 0.7071067811865476
INV_ROOT_TAU = 0.3989422804014327


def doc_positions(segments):
    index = jnp.arange(segments.shape[0], dtype=jnp.int32)
    starts = jnp.concatenate([jnp.ones((1,), dtype=bool), segments[1:] != segments[:-1]])
    first = lax.cummax(jnp.where(starts, index, 0), axis=0)
    return (index - first).astype(jnp.float32)


def rotary_tables(places, head_size):
    half = head_size // 2
    steps = jnp.arange(half, dtype=jnp.float32)
    freqs = 10000.0 ** (-2.0 * steps / head_size)
    angles = places[:, None] * freqs[None, :]
    zeta = (2.0 * steps / head_size + GAMMA) / (1.0 + GAMMA)
    decay = jnp.exp(jnp.log(zeta)[None, :] * places[:, None] / SCALE_BASE)
    return (jnp.cos(angles), jnp.sin(angles), jnp.concatenate([decay, decay], axis=-1))


def rotate(values, cosine, sine):
    half = values.shape[-1] // 2
    first = values[..., :half]
    second = values[..., half:]
    cosine = cosine[:, None, :]
    sine = sine[:, None, :]
    return jnp.concatenate(
        [first * cosine - second * sine, second * cosine + first * sine], axis=-1
    )


def gelu_slope(values):
    return (
        0.5 * (1.0 + lax.erf(values * ROOT_HALF))
        + values * jnp.exp(-0.5 * values * values) * INV_ROOT_TAU
    )


def row_norm(values):
    centre = values - jnp.mean(values, axis=-1, keepdims=True)
    scale_back = lax.rsqrt(jnp.mean(centre * centre, axis=-1, keepdims=True) + EPS)
    return (centre * scale_back, scale_back)


def row_norm_back(grad_out, normed, scale_back, gain):
    scaled = grad_out * gain
    gain_grad = jnp.sum(grad_out * normed, axis=0)
    grad_in = scale_back * (
        scaled
        - jnp.mean(scaled, axis=-1, keepdims=True)
        - normed * jnp.mean(scaled * normed, axis=-1, keepdims=True)
    )
    return (grad_in, gain_grad)


def shift(values, step, size):
    return lax.ppermute(values, "mp", [(i, (i + step) % size) for i in range(size)])


def sum_slots(values, size):
    total = values
    for step in range(1, size):
        total = total + jnp.roll(shift(values, step, size), step, axis=-2)
    return total


def gather_slots(shard, size):
    if size != 4:
        return jnp.concatenate(
            [shard] + [shift(shard, step, size) for step in range(1, size)], axis=0
        )
    place = lax.axis_index("mp")
    across = lax.ppermute(shard, "mp", [(0, 2), (1, 3), (2, 0), (3, 1)])
    up = lax.ppermute(shard, "mp", [(0, 1), (1, 2), (2, 3)])
    down = lax.ppermute(shard, "mp", [(1, 0), (2, 1), (3, 2)])
    ends = lax.ppermute(across, "mp", [(2, 3), (1, 0)])
    first = jnp.where(place == 0, ends, up)
    third = jnp.where(place == 3, ends, down)
    return jnp.concatenate([shard, first, across, third], axis=0)


def scatter_slots(partial, size, after=()):
    rows = partial.shape[0] // size
    parts = [partial[k * rows : (k + 1) * rows] for k in range(size)]
    low = [part.astype(jnp.bfloat16) for part in parts]
    if size != 4:
        total = parts[0]
        for step in range(1, size):
            total = total + shift(low[step], size - step, size).astype(jnp.float32)
        return total
    place = lax.axis_index("mp")
    ends = lax.ppermute(jnp.where(place == 0, low[1], low[3]), "mp", [(0, 1), (3, 2)])
    down = lax.ppermute(low[1], "mp", [(1, 0), (2, 1), (3, 2)])
    up = lax.ppermute(low[3], "mp", [(0, 1), (1, 2), (2, 3)])
    across = lax.ppermute(
        (parts[2] + ends.astype(jnp.float32)).astype(jnp.bfloat16),
        "mp",
        [(0, 2), (1, 3), (2, 0), (3, 1)],
    )
    down, up, across, _ = lax.optimization_barrier((down, up, across, after))
    return (
        parts[0]
        + down.astype(jnp.float32)
        + up.astype(jnp.float32)
        + across.astype(jnp.float32)
    )


def split_norm(values, width, size):
    rows = values.shape[0]
    sums = jnp.stack([jnp.sum(values, axis=-1), jnp.sum(values * values, axis=-1)])
    sums = sum_slots(sums.reshape(2, size, rows // size), size).reshape(2, rows)
    mean = sums[0] / width
    scale_back = lax.rsqrt(sums[1] / width - mean * mean + EPS)
    return ((values - mean[:, None]) * scale_back[:, None], scale_back[:, None])


def split_norm_back(grad_out, normed, scale_back, gain, width, size):
    rows = grad_out.shape[0]
    scaled = grad_out * gain
    gain_grad = jnp.sum(grad_out * normed, axis=0)
    sums = jnp.stack([jnp.sum(scaled, axis=-1), jnp.sum(scaled * normed, axis=-1)])
    sums = sum_slots(sums.reshape(2, size, rows // size), size).reshape(2, rows) / width
    grad_in = scale_back * (scaled - sums[0][:, None] - normed * sums[1][:, None])
    return (grad_in, gain_grad)


def score_block(query, key, allowed, factor):
    scores = jnp.einsum("qhd,khd->hqk", query, key, preferred_element_type=jnp.float32) * factor
    return jnp.where(allowed[None], scores, NEG)


def attend_forward(query, key, value, allowed):
    factor = query.shape[2] ** (-0.5)
    scores = score_block(query, key, allowed, factor)
    peak = jnp.max(scores, axis=-1, keepdims=True)
    expo = jnp.exp(scores - peak)
    denom = jnp.sum(expo, axis=-1, keepdims=True)
    probs = (expo / denom).astype(jnp.bfloat16)
    outputs = jnp.einsum("hqk,khd->qhd", probs, value, preferred_element_type=jnp.float32)
    return (outputs, peak + jnp.log(denom))


def attend_backward(query, key, value, allowed, totals, grad_out):
    factor = query.shape[2] ** (-0.5)
    scores = score_block(query, key, allowed, factor)
    probs = jnp.where(allowed[None], jnp.exp(scores - totals), 0.0)
    grad_value = jnp.einsum(
        "hqk,qhd->khd", probs.astype(jnp.bfloat16), grad_out, preferred_element_type=jnp.float32
    )
    grad_probs = jnp.einsum("qhd,khd->hqk", grad_out, value, preferred_element_type=jnp.float32)
    delta = jnp.sum(probs * grad_probs, axis=-1, keepdims=True)
    grad_scores = (probs * (grad_probs - delta)).astype(jnp.bfloat16)
    grad_query = (
        jnp.einsum("hqk,khd->qhd", grad_scores, key, preferred_element_type=jnp.float32) * factor
    )
    grad_key = (
        jnp.einsum("hqk,qhd->khd", grad_scores, query, preferred_element_type=jnp.float32) * factor
    )
    return (grad_query, grad_key, grad_value)


def to_slots(values, place, size):
    columns = values.reshape(-1, size).T
    return jnp.concatenate(
        [
            lax.dynamic_index_in_dim(columns, (place - k) % size, 0, keepdims=False)
            for k in range(size)
        ]
    )


def gather_rows(values):
    return lax.all_gather(values, "dp", axis=0, tiled=True)


def scatter_rows(values):
    return lax.psum_scatter(
        values.astype(jnp.bfloat16), "dp", scatter_dimension=0, tiled=True
    ).astype(jnp.float32)


class Row:
    pass


def per_device(
    tokens,
    segment_ids,
    image_blocks,
    features,
    latent_queries,
    image_kv_weight,
    image_out_weight,
    norm1_gain,
    attn_in_weight,
    attn_norm_gain,
    attn_out_weight,
    norm2_gain,
    ffn_up_weight,
    ffn_norm_gain,
    ffn_down_weight,
    cotangent,
):
    n_model = lax.axis_size("mp")
    n_data = lax.axis_size("dp")
    place = lax.axis_index("mp")
    data_index = lax.axis_index("dp")
    micro, shard_rows, _, width = tokens.shape
    row_length = shard_rows * n_model
    gain_one = norm1_gain.astype(jnp.float32)
    gain_two = norm2_gain.astype(jnp.float32)
    n_query = latent_queries.shape[0]

    columns = latent_queries.shape[1]
    query_size = n_query * columns
    small = jnp.concatenate([latent_queries.reshape(-1), attn_norm_gain, ffn_norm_gain])
    small = jnp.pad(small, (0, -small.shape[0] % (16 * columns))).reshape(-1, columns)
    kv_rows = image_kv_weight.size // columns
    out_rows = image_out_weight.size // columns
    pack = lax.all_gather(
        jnp.concatenate(
            [image_kv_weight.reshape(-1, columns), image_out_weight.reshape(-1, columns), small]
        ),
        "dp",
        axis=0,
        tiled=True,
    ).reshape(n_data, -1, columns)
    kv_weight = pack[:, :kv_rows].reshape(-1, 2, columns)
    out_weight = pack[:, kv_rows : kv_rows + out_rows].reshape(-1, width)
    small = pack[:, kv_rows + out_rows :].reshape(n_data, -1)
    queries = small[:, :query_size].reshape(n_data * n_query, -1)
    attn_end = query_size + attn_norm_gain.shape[0]
    attn_gain = small[:, query_size:attn_end].reshape(-1).astype(jnp.float32)
    ffn_gain = small[:, attn_end : attn_end + ffn_norm_gain.shape[0]].reshape(-1)
    ffn_gain = ffn_gain.astype(jnp.float32)
    attn_in = gather_rows(attn_in_weight)
    attn_out = gather_rows(attn_out_weight)

    text = [tokens[r, :, 0, :] for r in range(micro)]
    text_in = [
        gather_slots(
            (row_norm(text[r].astype(jnp.float32))[0] * gain_one).astype(jnp.bfloat16), n_model
        )
        for r in range(micro)
    ]

    latents = queries.shape[0]
    per_model = latents // n_model
    images, patches = features.shape[:2]
    image_heads = queries.shape[1] // HD
    factor = HD ** (-0.5)
    slotted = jnp.concatenate(
        [
            lax.dynamic_index_in_dim(
                queries.reshape(per_model, n_model, -1), (place - k) % n_model, 1, keepdims=False
            )
            for k in range(n_model)
        ],
        axis=0,
    ).reshape(latents, image_heads, HD)
    keyvals = jnp.einsum(
        "ipc,ckd->ipkd", features, kv_weight, preferred_element_type=jnp.float32
    ).astype(jnp.bfloat16)
    image_keys = keyvals[:, :, 0].reshape(images, patches, image_heads, HD)
    image_values = keyvals[:, :, 1].reshape(images, patches, image_heads, HD)
    image_scores = (
        jnp.einsum("lhd,iphd->ihlp", slotted, image_keys, preferred_element_type=jnp.float32)
        * factor
    )
    image_expo = jnp.exp(image_scores - jnp.max(image_scores, axis=-1, keepdims=True))
    image_probs = image_expo / jnp.sum(image_expo, axis=-1, keepdims=True)
    image_low = image_probs.astype(jnp.bfloat16)
    pooled = (
        jnp.einsum("ihlp,iphd->ilhd", image_low, image_values, preferred_element_type=jnp.float32)
        .reshape(images, latents, -1)
        .astype(jnp.bfloat16)
    )
    pooled_late, text_in[0] = lax.optimization_barrier((pooled, text_in[0]))
    embed_part = jnp.einsum(
        "ilc,cd->lid", pooled_late, out_weight, preferred_element_type=jnp.float32
    ).reshape(latents, images * width)
    own_embeds = scatter_slots(embed_part, n_model).astype(jnp.bfloat16)
    slot_embeds = gather_slots(own_embeds, n_model)
    slot_embeds, text_in[1:] = lax.optimization_barrier((slot_embeds, text_in[1:]))
    slot_embeds = slot_embeds.reshape(latents, images, width)
    all_embeds = lax.all_gather(slot_embeds, "dp", axis=0, tiled=False)
    grads_all = lax.all_gather(cotangent[:, :, 0, :], "mp", axis=0, tiled=False)
    ffn_up = gather_rows(ffn_up_weight)
    ffn_down = gather_rows(ffn_down_weight)
    total_images = n_data * images
    all_embeds = all_embeds.transpose(0, 2, 1, 3).reshape(total_images, latents, width)
    embeds_in = (row_norm(all_embeds.astype(jnp.float32))[0] * gain_one).astype(jnp.bfloat16)
    image_index = jnp.arange(total_images, dtype=jnp.int32)
    blocks_row = shard_rows // per_model

    index = jnp.arange(row_length, dtype=jnp.int32)
    position = to_slots(index, place, n_model)
    rows = []
    for r in range(micro):
        row = Row()
        blocks = lax.dynamic_index_in_dim(
            image_blocks, data_index * micro + r, 0, keepdims=False
        )
        selector = (blocks[:, None] == image_index[None, :]).astype(jnp.bfloat16)
        row.selector = selector
        is_text = jnp.repeat(blocks == total_images, per_model)[:, None]
        row.is_text = is_text
        placed = jnp.einsum(
            "bi,isd->bsd",
            selector,
            embeds_in.reshape(total_images, n_model * per_model, width),
            preferred_element_type=jnp.float32,
        ).astype(jnp.bfloat16)
        placed = (
            placed.reshape(blocks_row, n_model, per_model, width)
            .swapaxes(0, 1)
            .reshape(row_length, width)
        )
        own_placed = jnp.einsum(
            "bi,isd->bsd",
            selector,
            all_embeds[:, :per_model],
            preferred_element_type=jnp.float32,
        ).reshape(shard_rows, width)
        start = jnp.where(is_text, text[r].astype(jnp.float32), own_placed)
        row.start = start
        row.input1 = jnp.where(jnp.tile(is_text, (n_model, 1)), text_in[r], placed)
        segments = to_slots(segment_ids[r], place, n_model)
        places = to_slots(doc_positions(segment_ids[r]), place, n_model)
        row.allowed = (position[:, None] >= position[None, :]) & (
            segments[:, None] == segments[None, :]
        )
        cosine, sine, decay = rotary_tables(places, HD)
        row.tables = (cosine, sine, decay[:, None, :])
        rows.append(row)

    local_heads = attn_in.shape[2] // HD
    outputs = []
    for r in range(micro):
        row = rows[r]
        cosine, sine, decay = row.tables
        mixed = jnp.einsum(
            "lc,ckd->lkd", row.input1, attn_in, preferred_element_type=jnp.float32
        )
        row.query = (
            rotate(mixed[:, 0].reshape(row_length, local_heads, HD), cosine, sine) * decay
        ).astype(jnp.bfloat16)
        row.key = (
            rotate(mixed[:, 1].reshape(row_length, local_heads, HD), cosine, sine) / decay
        ).astype(jnp.bfloat16)
        row.value = mixed[:, 2].reshape(row_length, local_heads, HD).astype(jnp.bfloat16)
        attended, row.totals = attend_forward(
            row.query, row.key, row.value, row.allowed
        )
        row.normed_a, row.back_a = split_norm(
            attended.reshape(row_length, -1), D, n_model
        )
        row.sub_attn = (row.normed_a * attn_gain).astype(jnp.bfloat16)
        part = jnp.dot(row.sub_attn, attn_out, preferred_element_type=jnp.float32)
        later = [other.input1 for other in rows[r + 1 :]]
        before = [other.ready for other in rows[:r]]
        part, later, _ = lax.optimization_barrier((part, later, before))
        for other, value in zip(rows[r + 1 :], later):
            other.input1 = value
        if r == micro - 1:
            _, grads_all = lax.optimization_barrier((part, grads_all))
        earlier = [other.hidden for other in rows[: min(r, 1)]]
        row.middle = row.start + scatter_slots(part, n_model, earlier)
        second = row.middle.astype(jnp.bfloat16).astype(jnp.float32)
        row.normed2, row.back2 = row_norm(second)
        row.ready = (row.normed2 * gain_two).astype(jnp.bfloat16)
        row.input2 = gather_slots(row.ready, n_model)
        if r == 0:
            row.hidden = jnp.dot(row.input2, ffn_up, preferred_element_type=jnp.float32)
    branch = [
        jnp.concatenate(
            [
                lax.dynamic_index_in_dim(grads_all, (place - k) % n_model, 0, keepdims=False)[r]
                for k in range(n_model)
            ],
            axis=0,
        )
        for r in range(micro)
    ]
    ffn_gain_grad = 0.0
    attn_gain_grad = 0.0
    norm2_gain_grad = 0.0
    norm1_gain_grad = 0.0
    for r in range(micro):
        row = rows[r]
        if r > 0:
            row.hidden = jnp.dot(row.input2, ffn_up, preferred_element_type=jnp.float32)
        row.normed_f, row.back_f = split_norm(
            jax.nn.gelu(row.hidden, approximate=False), FF, n_model
        )
        row.sub_ffn = (row.normed_f * ffn_gain).astype(jnp.bfloat16)
        before = [other.landed for other in rows[:r]]
        branch_late, _ = lax.optimization_barrier((branch[r], before))
        grad_sub = jnp.einsum(
            "ld,fd->lf", branch_late, ffn_down, preferred_element_type=jnp.float32
        )
        grad_active, gain_part = split_norm_back(
            grad_sub, row.normed_f, row.back_f, ffn_gain, FF, n_model
        )
        ffn_gain_grad = ffn_gain_grad + gain_part
        row.grad_hidden = (grad_active * gelu_slope(row.hidden)).astype(jnp.bfloat16)
        grad_input2 = jnp.einsum(
            "lf,cf->lc", row.grad_hidden, ffn_up, preferred_element_type=jnp.float32
        )
        later = [other.input2 for other in rows[r + 1 :]]
        before = [other.landed for other in rows[:r]]
        grad_input2, later, _ = lax.optimization_barrier((grad_input2, later, before))
        for other, value in zip(rows[r + 1 :], later):
            other.input2 = value
        share, gain_part = row_norm_back(
            scatter_slots(grad_input2, n_model), row.normed2, row.back2, gain_two
        )
        norm2_gain_grad = norm2_gain_grad + gain_part
        row.grad_middle = cotangent[r, :, 0, :].astype(jnp.float32) + share
        row.landed = row.grad_middle.astype(jnp.bfloat16)
        row.grad_out = gather_slots(row.landed, n_model)

    def both(values):
        return jnp.concatenate(values, axis=0)

    down_part = jnp.einsum(
        "lf,ld->fd",
        both([row.sub_ffn for row in rows]),
        jnp.concatenate(branch, axis=0),
        preferred_element_type=jnp.float32,
    ).astype(jnp.bfloat16)
    up_part = jnp.einsum(
        "lc,lf->cf", both([row.input2 for row in rows]), both([row.grad_hidden for row in rows]), preferred_element_type=jnp.float32
    ).astype(jnp.bfloat16)
    _, rows[0].grad_out = lax.optimization_barrier((down_part, rows[0].grad_out))
    _, rows[-1].grad_out = lax.optimization_barrier((up_part, rows[-1].grad_out))
    ffn_down_grad = scatter_rows(down_part)
    ffn_up_grad = scatter_rows(up_part)
    attn_out_part = jnp.einsum(
        "lc,ld->cd", both([row.sub_attn for row in rows]), both([row.grad_out for row in rows]), preferred_element_type=jnp.float32
    ).astype(jnp.bfloat16)
    token_grads = []
    grad_table = jnp.zeros((per_model, total_images, width), jnp.float32)
    for r in range(micro):
        row = rows[r]
        cosine, sine, decay = row.tables
        grad_sub_attn = jnp.einsum(
            "ld,cd->lc", row.grad_out, attn_out, preferred_element_type=jnp.float32
        )
        grad_attended, gain_part = split_norm_back(
            grad_sub_attn, row.normed_a, row.back_a, attn_gain, D, n_model
        )
        attn_gain_grad = attn_gain_grad + gain_part
        grad_query, grad_key, grad_value = attend_backward(
            row.query,
            row.key,
            row.value,
            row.allowed,
            row.totals,
            grad_attended.astype(jnp.bfloat16).reshape(row_length, local_heads, HD),
        )
        row.grad_mixed = (
            jnp.stack(
                [
                    rotate(grad_query * decay, cosine, -sine),
                    rotate(grad_key / decay, cosine, -sine),
                    grad_value,
                ],
                axis=1,
            )
            .reshape(row_length, 3, -1)
            .astype(jnp.bfloat16)
        )
        before = [other.share for other in rows[:r]]
        mixed_late, _ = lax.optimization_barrier((row.grad_mixed, before))
        grad_input1 = jnp.einsum(
            "lkd,ckd->lc", mixed_late, attn_in, preferred_element_type=jnp.float32
        )
        if r < micro - 1:
            later = [other.grad_out for other in rows[r + 1 :]]
            grad_input1, later = lax.optimization_barrier((grad_input1, later))
            for other, value in zip(rows[r + 1 :], later):
                other.grad_out = value
        else:
            grad_input1, _ = lax.optimization_barrier((grad_input1, attn_out_part))
        normed1, back1 = row_norm(row.start)
        share, gain_part = row_norm_back(
            scatter_slots(grad_input1, n_model), normed1, back1, gain_one
        )
        row.share = share
        norm1_gain_grad = norm1_gain_grad + gain_part
        grad_start = row.grad_middle + share
        token_grads.append(jnp.where(row.is_text, grad_start, 0.0))
        grad_table = grad_table + jnp.einsum(
            "bi,bsd->sid",
            row.selector,
            grad_start.astype(jnp.bfloat16).reshape(blocks_row, per_model, width),
            preferred_element_type=jnp.float32,
        )
    attn_out_grad = scatter_rows(attn_out_part)
    attn_in_part = jnp.einsum(
        "lc,lkd->ckd",
        both([row.input1 for row in rows]),
        both([row.grad_mixed for row in rows]),
        preferred_element_type=jnp.float32,
    ).astype(jnp.bfloat16)
    attn_in_grad = scatter_rows(attn_in_part)

    for row in rows:
        late, _ = lax.optimization_barrier((row.sub_ffn, row.share))
        part = jnp.dot(late, ffn_down, preferred_element_type=jnp.float32)
        outputs.append((row.middle + scatter_slots(part, n_model)).astype(jnp.bfloat16))

    share_grad = lax.psum_scatter(
        grad_table.astype(jnp.bfloat16), "dp", scatter_dimension=1, tiled=True
    )
    embed_grad = gather_slots(share_grad.reshape(per_model, images * width), n_model).reshape(
        latents, images, width
    )
    out_grad = jnp.einsum("ilc,lid->cd", pooled, embed_grad, preferred_element_type=jnp.float32)
    grad_pooled = (
        jnp.einsum("lid,cd->ilc", embed_grad, out_weight, preferred_element_type=jnp.float32)
        .astype(jnp.bfloat16)
        .reshape(images, latents, image_heads, HD)
    )
    grad_values = jnp.einsum(
        "ihlp,ilhd->iphd", image_low, grad_pooled, preferred_element_type=jnp.float32
    )
    grad_probs = jnp.einsum(
        "ilhd,iphd->ihlp", grad_pooled, image_values, preferred_element_type=jnp.float32
    )
    delta = jnp.sum(image_probs * grad_probs, axis=-1, keepdims=True)
    grad_scores = (image_probs * (grad_probs - delta)).astype(jnp.bfloat16)
    grad_latent = (
        jnp.einsum("ihlp,iphd->lhd", grad_scores, image_keys, preferred_element_type=jnp.float32)
        * factor
    )
    grad_keys = (
        jnp.einsum("ihlp,lhd->iphd", grad_scores, slotted, preferred_element_type=jnp.float32)
        * factor
    )
    grad_keyvals = jnp.stack(
        [grad_keys.reshape(images, patches, -1), grad_values.reshape(images, patches, -1)], axis=2
    ).astype(jnp.bfloat16)
    kv_grad = jnp.einsum(
        "ipc,ipkd->ckd", features, grad_keyvals, preferred_element_type=jnp.float32
    )
    slot_grad = grad_latent.reshape(n_model, per_model, -1)
    query_grad = jnp.stack(
        [
            lax.dynamic_index_in_dim(slot_grad, (place - m) % n_model, 0, keepdims=False)
            for m in range(n_model)
        ],
        axis=1,
    ).reshape(latents, -1)
    gains = jnp.stack([norm1_gain_grad, norm2_gain_grad]).reshape(2, n_model, -1)
    own = 0.0
    for step in range(n_model):
        chunk = lax.dynamic_index_in_dim(gains, (place + step) % n_model, 1, keepdims=False)
        own = own + (chunk if step == 0 else shift(chunk, step, n_model))
    pieces = [
        piece.astype(jnp.bfloat16).reshape(n_data, -1)
        for piece in (
            kv_grad,
            out_grad,
            query_grad,
            own[0],
            own[1],
            attn_gain_grad,
            ffn_gain_grad,
        )
    ]
    packed = jnp.concatenate(pieces, axis=1)
    packed = jnp.pad(packed, ((0, 0), (0, -packed.shape[1] % 2048))).reshape(n_data, -1, 128)
    packed, outputs = lax.optimization_barrier((packed, outputs))
    packed = lax.psum_scatter(packed, "dp", scatter_dimension=0, tiled=True)
    packed = packed.reshape(-1).astype(jnp.float32)
    split = []
    begin = 0
    for piece in pieces:
        split.append(packed[begin : begin + piece.shape[1]])
        begin += piece.shape[1]
    return (
        jnp.stack(outputs)[:, :, None, :],
        jnp.stack(token_grads)[:, :, None, :],
        split[2].reshape(latent_queries.shape),
        split[0].reshape(image_kv_weight.shape),
        split[1].reshape(image_out_weight.shape),
        split[3],
        attn_in_grad,
        split[5],
        attn_out_grad,
        split[4],
        ffn_up_grad,
        split[6],
        ffn_down_grad,
    )


def solution(mesh):
    placed = (
        P("dp", None, "mp", None),
        P("dp", None),
        P(),
        P("dp", None, None),
        P("dp", "mp"),
        P("dp", None, "mp"),
        P(("mp", "dp"), None),
        P(),
        P("dp", None, "mp"),
        P(("mp", "dp")),
        P(("mp", "dp"), None),
        P(),
        P("dp", "mp"),
        P(("mp", "dp")),
        P(("mp", "dp"), None),
        P("dp", None, "mp", None),
    )

    return jax.shard_map(
        per_device,
        mesh=mesh,
        in_specs=placed,
        out_specs=(
            P("dp", None, "mp", None),
            P("dp", None, "mp", None),
            P("dp", "mp"),
            P("dp", None, "mp"),
            P(("mp", "dp"), None),
            P(("mp", "dp")),
            P("dp", None, "mp"),
            P(("mp", "dp")),
            P(("mp", "dp"), None),
            P(("mp", "dp")),
            P("dp", "mp"),
            P(("mp", "dp")),
            P(("mp", "dp"), None),
        ),
        check_vma=False,
    )
```

```python
import jax
import jax.numpy as jnp
from jax import lax
from jax.sharding import PartitionSpec as P

D = 2048
HD = 64
FF = 8192


EPS = 1e-05
GAMMA = 0.4
SCALE_BASE = 512.0
NEG = -1e30
ROOT_HALF = 0.7071067811865476
INV_ROOT_TAU = 0.3989422804014327


def doc_positions(segments):
    index = jnp.arange(segments.shape[0], dtype=jnp.int32)
    starts = jnp.concatenate([jnp.ones((1,), dtype=bool), segments[1:] != segments[:-1]])
    first = lax.cummax(jnp.where(starts, index, 0), axis=0)
    return (index - first).astype(jnp.float32)


def rotary_tables(places, head_size):
    half = head_size // 2
    steps = jnp.arange(half, dtype=jnp.float32)
    freqs = 10000.0 ** (-2.0 * steps / head_size)
    angles = places[:, None] * freqs[None, :]
    zeta = (2.0 * steps / head_size + GAMMA) / (1.0 + GAMMA)
    decay = jnp.exp(jnp.log(zeta)[None, :] * places[:, None] / SCALE_BASE)
    return (jnp.cos(angles), jnp.sin(angles), jnp.concatenate([decay, decay], axis=-1))


def rotate(values, cosine, sine):
    half = values.shape[-1] // 2
    first = values[..., :half]
    second = values[..., half:]
    cosine = cosine[:, None, :]
    sine = sine[:, None, :]
    return jnp.concatenate(
        [first * cosine - second * sine, second * cosine + first * sine], axis=-1
    )


def gelu_slope(values):
    return (
        0.5 * (1.0 + lax.erf(values * ROOT_HALF))
        + values * jnp.exp(-0.5 * values * values) * INV_ROOT_TAU
    )


def row_norm(values):
    centre = values - jnp.mean(values, axis=-1, keepdims=True)
    scale_back = lax.rsqrt(jnp.mean(centre * centre, axis=-1, keepdims=True) + EPS)
    return (centre * scale_back, scale_back)


def row_norm_back(grad_out, normed, scale_back, gain):
    scaled = grad_out * gain
    gain_grad = jnp.sum(grad_out * normed, axis=0)
    grad_in = scale_back * (
        scaled
        - jnp.mean(scaled, axis=-1, keepdims=True)
        - normed * jnp.mean(scaled * normed, axis=-1, keepdims=True)
    )
    return (grad_in, gain_grad)


def shift(values, step, size):
    return lax.ppermute(values, "mp", [(i, (i + step) % size) for i in range(size)])


def sum_slots(values, size):
    total = values
    for step in range(1, size):
        total = total + jnp.roll(shift(values, step, size), step, axis=-2)
    return total


def gather_slots(shard, size):
    if size != 4:
        return jnp.concatenate(
            [shard] + [shift(shard, step, size) for step in range(1, size)], axis=0
        )
    place = lax.axis_index("mp")
    across = lax.ppermute(shard, "mp", [(0, 2), (1, 3), (2, 0), (3, 1)])
    up = lax.ppermute(shard, "mp", [(0, 1), (1, 2), (2, 3)])
    down = lax.ppermute(shard, "mp", [(1, 0), (2, 1), (3, 2)])
    ends = lax.ppermute(across, "mp", [(2, 3), (1, 0)])
    first = jnp.where(place == 0, ends, up)
    third = jnp.where(place == 3, ends, down)
    return jnp.concatenate([shard, first, across, third], axis=0)


def scatter_slots(partial, size, after=()):
    rows = partial.shape[0] // size
    parts = [partial[k * rows : (k + 1) * rows] for k in range(size)]
    low = [part.astype(jnp.bfloat16) for part in parts]
    if size != 4:
        total = parts[0]
        for step in range(1, size):
            total = total + shift(low[step], size - step, size).astype(jnp.float32)
        return total
    place = lax.axis_index("mp")
    ends = lax.ppermute(jnp.where(place == 0, low[1], low[3]), "mp", [(0, 1), (3, 2)])
    down = lax.ppermute(low[1], "mp", [(1, 0), (2, 1), (3, 2)])
    up = lax.ppermute(low[3], "mp", [(0, 1), (1, 2), (2, 3)])
    across = lax.ppermute(
        (parts[2] + ends.astype(jnp.float32)).astype(jnp.bfloat16),
        "mp",
        [(0, 2), (1, 3), (2, 0), (3, 1)],
    )
    down, up, across, _ = lax.optimization_barrier((down, up, across, after))
    return (
        parts[0]
        + down.astype(jnp.float32)
        + up.astype(jnp.float32)
        + across.astype(jnp.float32)
    )


def split_norm(values, width, size):
    rows = values.shape[0]
    sums = jnp.stack([jnp.sum(values, axis=-1), jnp.sum(values * values, axis=-1)])
    sums = sum_slots(sums.reshape(2, size, rows // size), size).reshape(2, rows)
    mean = sums[0] / width
    scale_back = lax.rsqrt(sums[1] / width - mean * mean + EPS)
    return ((values - mean[:, None]) * scale_back[:, None], scale_back[:, None])


def split_norm_back(grad_out, normed, scale_back, gain, width, size):
    rows = grad_out.shape[0]
    scaled = grad_out * gain
    gain_grad = jnp.sum(grad_out * normed, axis=0)
    sums = jnp.stack([jnp.sum(scaled, axis=-1), jnp.sum(scaled * normed, axis=-1)])
    sums = sum_slots(sums.reshape(2, size, rows // size), size).reshape(2, rows) / width
    grad_in = scale_back * (scaled - sums[0][:, None] - normed * sums[1][:, None])
    return (grad_in, gain_grad)


def score_block(query, key, allowed, factor):
    scores = jnp.einsum("qhd,khd->hqk", query, key, preferred_element_type=jnp.float32) * factor
    return jnp.where(allowed[None], scores, NEG)


def attend_forward(query, key, value, allowed):
    factor = query.shape[2] ** (-0.5)
    scores = score_block(query, key, allowed, factor)
    peak = jnp.max(scores, axis=-1, keepdims=True)
    expo = jnp.exp(scores - peak)
    denom = jnp.sum(expo, axis=-1, keepdims=True)
    probs = (expo / denom).astype(jnp.bfloat16)
    outputs = jnp.einsum("hqk,khd->qhd", probs, value, preferred_element_type=jnp.float32)
    return (outputs, peak + jnp.log(denom))


def attend_backward(query, key, value, allowed, totals, grad_out):
    factor = query.shape[2] ** (-0.5)
    scores = score_block(query, key, allowed, factor)
    probs = jnp.where(allowed[None], jnp.exp(scores - totals), 0.0)
    grad_value = jnp.einsum(
        "hqk,qhd->khd", probs.astype(jnp.bfloat16), grad_out, preferred_element_type=jnp.float32
    )
    grad_probs = jnp.einsum("qhd,khd->hqk", grad_out, value, preferred_element_type=jnp.float32)
    delta = jnp.sum(probs * grad_probs, axis=-1, keepdims=True)
    grad_scores = (probs * (grad_probs - delta)).astype(jnp.bfloat16)
    grad_query = (
        jnp.einsum("hqk,khd->qhd", grad_scores, key, preferred_element_type=jnp.float32) * factor
    )
    grad_key = (
        jnp.einsum("hqk,qhd->khd", grad_scores, query, preferred_element_type=jnp.float32) * factor
    )
    return (grad_query, grad_key, grad_value)


def to_slots(values, place, size):
    columns = values.reshape(-1, size).T
    return jnp.concatenate(
        [
            lax.dynamic_index_in_dim(columns, (place - k) % size, 0, keepdims=False)
            for k in range(size)
        ]
    )


def gather_rows(values):
    return lax.all_gather(values, "dp", axis=0, tiled=True)


def scatter_rows(values):
    return lax.psum_scatter(
        values.astype(jnp.bfloat16), "dp", scatter_dimension=0, tiled=True
    ).astype(jnp.float32)


class Row:
    pass


def per_device(
    tokens,
    segment_ids,
    image_blocks,
    features,
    latent_queries,
    image_kv_weight,
    image_out_weight,
    norm1_gain,
    attn_in_weight,
    attn_norm_gain,
    attn_out_weight,
    norm2_gain,
    ffn_up_weight,
    ffn_norm_gain,
    ffn_down_weight,
    cotangent,
):
    n_model = lax.axis_size("mp")
    n_data = lax.axis_size("dp")
    place = lax.axis_index("mp")
    data_index = lax.axis_index("dp")
    micro, shard_rows, _, width = tokens.shape
    row_length = shard_rows * n_model
    gain_one = norm1_gain.astype(jnp.float32)
    gain_two = norm2_gain.astype(jnp.float32)
    n_query = latent_queries.shape[0]

    columns = latent_queries.shape[1]
    query_size = n_query * columns
    small = jnp.concatenate([latent_queries.reshape(-1), attn_norm_gain, ffn_norm_gain])
    small = jnp.pad(small, (0, -small.shape[0] % (16 * columns))).reshape(-1, columns)
    kv_rows = image_kv_weight.size // columns
    out_rows = image_out_weight.size // columns
    pack = lax.all_gather(
        jnp.concatenate(
            [image_kv_weight.reshape(-1, columns), image_out_weight.reshape(-1, columns), small]
        ),
        "dp",
        axis=0,
        tiled=True,
    ).reshape(n_data, -1, columns)
    kv_weight = pack[:, :kv_rows].reshape(-1, 2, columns)
    out_weight = pack[:, kv_rows : kv_rows + out_rows].reshape(-1, width)
    small = pack[:, kv_rows + out_rows :].reshape(n_data, -1)
    queries = small[:, :query_size].reshape(n_data * n_query, -1)
    attn_end = query_size + attn_norm_gain.shape[0]
    attn_gain = small[:, query_size:attn_end].reshape(-1).astype(jnp.float32)
    ffn_gain = small[:, attn_end : attn_end + ffn_norm_gain.shape[0]].reshape(-1)
    ffn_gain = ffn_gain.astype(jnp.float32)
    attn_in = gather_rows(attn_in_weight)
    attn_out = gather_rows(attn_out_weight)

    text = [tokens[r, :, 0, :] for r in range(micro)]
    text_in = [
        gather_slots(
            (row_norm(text[r].astype(jnp.float32))[0] * gain_one).astype(jnp.bfloat16), n_model
        )
        for r in range(micro)
    ]

    latents = queries.shape[0]
    per_model = latents // n_model
    images, patches = features.shape[:2]
    image_heads = queries.shape[1] // HD
    factor = HD ** (-0.5)
    slotted = jnp.concatenate(
        [
            lax.dynamic_index_in_dim(
                queries.reshape(per_model, n_model, -1), (place - k) % n_model, 1, keepdims=False
            )
            for k in range(n_model)
        ],
        axis=0,
    ).reshape(latents, image_heads, HD)
    keyvals = jnp.einsum(
        "ipc,ckd->ipkd", features, kv_weight, preferred_element_type=jnp.float32
    ).astype(jnp.bfloat16)
    image_keys = keyvals[:, :, 0].reshape(images, patches, image_heads, HD)
    image_values = keyvals[:, :, 1].reshape(images, patches, image_heads, HD)
    image_scores = (
        jnp.einsum("lhd,iphd->ihlp", slotted, image_keys, preferred_element_type=jnp.float32)
        * factor
    )
    image_expo = jnp.exp(image_scores - jnp.max(image_scores, axis=-1, keepdims=True))
    image_probs = image_expo / jnp.sum(image_expo, axis=-1, keepdims=True)
    image_low = image_probs.astype(jnp.bfloat16)
    pooled = (
        jnp.einsum("ihlp,iphd->ilhd", image_low, image_values, preferred_element_type=jnp.float32)
        .reshape(images, latents, -1)
        .astype(jnp.bfloat16)
    )
    pooled_late, text_in[0] = lax.optimization_barrier((pooled, text_in[0]))
    embed_part = jnp.einsum(
        "ilc,cd->lid", pooled_late, out_weight, preferred_element_type=jnp.float32
    ).reshape(latents, images * width)
    own_embeds = scatter_slots(embed_part, n_model).astype(jnp.bfloat16)
    slot_embeds = gather_slots(own_embeds, n_model)
    slot_embeds, text_in[1:] = lax.optimization_barrier((slot_embeds, text_in[1:]))
    slot_embeds = slot_embeds.reshape(latents, images, width)
    all_embeds = lax.all_gather(slot_embeds, "dp", axis=0, tiled=False)
    grads_all = lax.all_gather(cotangent[:, :, 0, :], "mp", axis=0, tiled=False)
    ffn_up = gather_rows(ffn_up_weight)
    ffn_down = gather_rows(ffn_down_weight)
    total_images = n_data * images
    all_embeds = all_embeds.transpose(0, 2, 1, 3).reshape(total_images, latents, width)
    embeds_in = (row_norm(all_embeds.astype(jnp.float32))[0] * gain_one).astype(jnp.bfloat16)
    image_index = jnp.arange(total_images, dtype=jnp.int32)
    blocks_row = shard_rows // per_model

    index = jnp.arange(row_length, dtype=jnp.int32)
    position = to_slots(index, place, n_model)
    rows = []
    for r in range(micro):
        row = Row()
        blocks = lax.dynamic_index_in_dim(
            image_blocks, data_index * micro + r, 0, keepdims=False
        )
        selector = (blocks[:, None] == image_index[None, :]).astype(jnp.bfloat16)
        row.selector = selector
        is_text = jnp.repeat(blocks == total_images, per_model)[:, None]
        row.is_text = is_text
        placed = jnp.einsum(
            "bi,isd->bsd",
            selector,
            embeds_in.reshape(total_images, n_model * per_model, width),
            preferred_element_type=jnp.float32,
        ).astype(jnp.bfloat16)
        placed = (
            placed.reshape(blocks_row, n_model, per_model, width)
            .swapaxes(0, 1)
            .reshape(row_length, width)
        )
        own_placed = jnp.einsum(
            "bi,isd->bsd",
            selector,
            all_embeds[:, :per_model],
            preferred_element_type=jnp.float32,
        ).reshape(shard_rows, width)
        start = jnp.where(is_text, text[r].astype(jnp.float32), own_placed)
        row.start = start
        row.input1 = jnp.where(jnp.tile(is_text, (n_model, 1)), text_in[r], placed)
        segments = to_slots(segment_ids[r], place, n_model)
        places = to_slots(doc_positions(segment_ids[r]), place, n_model)
        row.allowed = (position[:, None] >= position[None, :]) & (
            segments[:, None] == segments[None, :]
        )
        cosine, sine, decay = rotary_tables(places, HD)
        row.tables = (cosine, sine, decay[:, None, :])
        rows.append(row)

    local_heads = attn_in.shape[2] // HD
    outputs = []
    for r in range(micro):
        row = rows[r]
        cosine, sine, decay = row.tables
        mixed = jnp.einsum(
            "lc,ckd->lkd", row.input1, attn_in, preferred_element_type=jnp.float32
        )
        row.query = (
            rotate(mixed[:, 0].reshape(row_length, local_heads, HD), cosine, sine) * decay
        ).astype(jnp.bfloat16)
        row.key = (
            rotate(mixed[:, 1].reshape(row_length, local_heads, HD), cosine, sine) / decay
        ).astype(jnp.bfloat16)
        row.value = mixed[:, 2].reshape(row_length, local_heads, HD).astype(jnp.bfloat16)
        attended, row.totals = attend_forward(
            row.query, row.key, row.value, row.allowed
        )
        row.normed_a, row.back_a = split_norm(
            attended.reshape(row_length, -1), D, n_model
        )
        row.sub_attn = (row.normed_a * attn_gain).astype(jnp.bfloat16)
        part = jnp.dot(row.sub_attn, attn_out, preferred_element_type=jnp.float32)
        later = [other.input1 for other in rows[r + 1 :]]
        before = [other.ready for other in rows[:r]]
        part, later, _ = lax.optimization_barrier((part, later, before))
        for other, value in zip(rows[r + 1 :], later):
            other.input1 = value
        if r == micro - 1:
            _, grads_all = lax.optimization_barrier((part, grads_all))
        earlier = [other.hidden for other in rows[:r]]
        row.middle = row.start + scatter_slots(part, n_model, earlier)
        second = row.middle.astype(jnp.bfloat16).astype(jnp.float32)
        row.normed2, row.back2 = row_norm(second)
        row.ready = (row.normed2 * gain_two).astype(jnp.bfloat16)
        row.input2 = gather_slots(row.ready, n_model)
        row.hidden = jnp.dot(row.input2, ffn_up, preferred_element_type=jnp.float32)
    branch = [
        jnp.concatenate(
            [
                lax.dynamic_index_in_dim(grads_all, (place - k) % n_model, 0, keepdims=False)[r]
                for k in range(n_model)
            ],
            axis=0,
        )
        for r in range(micro)
    ]
    ffn_gain_grad = 0.0
    attn_gain_grad = 0.0
    norm2_gain_grad = 0.0
    norm1_gain_grad = 0.0
    for r in range(micro):
        row = rows[r]
        row.normed_f, row.back_f = split_norm(
            jax.nn.gelu(row.hidden, approximate=False), FF, n_model
        )
        row.sub_ffn = (row.normed_f * ffn_gain).astype(jnp.bfloat16)
        grad_sub = jnp.einsum(
            "ld,fd->lf", branch[r], ffn_down, preferred_element_type=jnp.float32
        )
        grad_active, gain_part = split_norm_back(
            grad_sub, row.normed_f, row.back_f, ffn_gain, FF, n_model
        )
        ffn_gain_grad = ffn_gain_grad + gain_part
        row.grad_hidden = (grad_active * gelu_slope(row.hidden)).astype(jnp.bfloat16)
        grad_input2 = jnp.einsum(
            "lf,cf->lc", row.grad_hidden, ffn_up, preferred_element_type=jnp.float32
        )
        later = [other.input2 for other in rows[r + 1 :]]
        before = [other.landed for other in rows[:r]]
        grad_input2, later, _ = lax.optimization_barrier((grad_input2, later, before))
        for other, value in zip(rows[r + 1 :], later):
            other.input2 = value
        share, gain_part = row_norm_back(
            scatter_slots(grad_input2, n_model), row.normed2, row.back2, gain_two
        )
        norm2_gain_grad = norm2_gain_grad + gain_part
        row.grad_middle = cotangent[r, :, 0, :].astype(jnp.float32) + share
        row.landed = row.grad_middle.astype(jnp.bfloat16)
        row.grad_out = gather_slots(row.landed, n_model)

    def both(values):
        return jnp.concatenate(values, axis=0)

    down_part = jnp.einsum(
        "lf,ld->fd",
        both([row.sub_ffn for row in rows]),
        jnp.concatenate(branch, axis=0),
        preferred_element_type=jnp.float32,
    ).astype(jnp.bfloat16)
    up_part = jnp.einsum(
        "lc,lf->cf", both([row.input2 for row in rows]), both([row.grad_hidden for row in rows]), preferred_element_type=jnp.float32
    ).astype(jnp.bfloat16)
    _, rows[0].grad_out = lax.optimization_barrier((down_part, rows[0].grad_out))
    _, rows[-1].grad_out = lax.optimization_barrier((up_part, rows[-1].grad_out))
    ffn_down_grad = scatter_rows(down_part)
    ffn_up_grad = scatter_rows(up_part)
    attn_out_part = jnp.einsum(
        "lc,ld->cd", both([row.sub_attn for row in rows]), both([row.grad_out for row in rows]), preferred_element_type=jnp.float32
    ).astype(jnp.bfloat16)
    token_grads = []
    grad_table = jnp.zeros((per_model, total_images, width), jnp.float32)
    for r in range(micro):
        row = rows[r]
        cosine, sine, decay = row.tables
        grad_sub_attn = jnp.einsum(
            "ld,cd->lc", row.grad_out, attn_out, preferred_element_type=jnp.float32
        )
        grad_attended, gain_part = split_norm_back(
            grad_sub_attn, row.normed_a, row.back_a, attn_gain, D, n_model
        )
        attn_gain_grad = attn_gain_grad + gain_part
        grad_query, grad_key, grad_value = attend_backward(
            row.query,
            row.key,
            row.value,
            row.allowed,
            row.totals,
            grad_attended.astype(jnp.bfloat16).reshape(row_length, local_heads, HD),
        )
        row.grad_mixed = (
            jnp.stack(
                [
                    rotate(grad_query * decay, cosine, -sine),
                    rotate(grad_key / decay, cosine, -sine),
                    grad_value,
                ],
                axis=1,
            )
            .reshape(row_length, 3, -1)
            .astype(jnp.bfloat16)
        )
        before = [other.share for other in rows[:r]]
        mixed_late, _ = lax.optimization_barrier((row.grad_mixed, before))
        grad_input1 = jnp.einsum(
            "lkd,ckd->lc", mixed_late, attn_in, preferred_element_type=jnp.float32
        )
        if r < micro - 1:
            later = [other.grad_out for other in rows[r + 1 :]]
            grad_input1, later = lax.optimization_barrier((grad_input1, later))
            for other, value in zip(rows[r + 1 :], later):
                other.grad_out = value
        else:
            grad_input1, _ = lax.optimization_barrier((grad_input1, attn_out_part))
        normed1, back1 = row_norm(row.start)
        share, gain_part = row_norm_back(
            scatter_slots(grad_input1, n_model), normed1, back1, gain_one
        )
        row.share = share
        norm1_gain_grad = norm1_gain_grad + gain_part
        grad_start = row.grad_middle + share
        token_grads.append(jnp.where(row.is_text, grad_start, 0.0))
        grad_table = grad_table + jnp.einsum(
            "bi,bsd->sid",
            row.selector,
            grad_start.astype(jnp.bfloat16).reshape(blocks_row, per_model, width),
            preferred_element_type=jnp.float32,
        )
    attn_out_grad = scatter_rows(attn_out_part)
    attn_in_part = jnp.einsum(
        "lc,lkd->ckd",
        both([row.input1 for row in rows]),
        both([row.grad_mixed for row in rows]),
        preferred_element_type=jnp.float32,
    ).astype(jnp.bfloat16)
    attn_in_grad = scatter_rows(attn_in_part)

    for row in rows:
        late, _ = lax.optimization_barrier((row.sub_ffn, row.share))
        part = jnp.dot(late, ffn_down, preferred_element_type=jnp.float32)
        outputs.append((row.middle + scatter_slots(part, n_model)).astype(jnp.bfloat16))

    share_grad = lax.psum_scatter(
        grad_table.astype(jnp.bfloat16), "dp", scatter_dimension=1, tiled=True
    )
    embed_grad = gather_slots(share_grad.reshape(per_model, images * width), n_model).reshape(
        latents, images, width
    )
    out_grad = jnp.einsum("ilc,lid->cd", pooled, embed_grad, preferred_element_type=jnp.float32)
    grad_pooled = (
        jnp.einsum("lid,cd->ilc", embed_grad, out_weight, preferred_element_type=jnp.float32)
        .astype(jnp.bfloat16)
        .reshape(images, latents, image_heads, HD)
    )
    grad_values = jnp.einsum(
        "ihlp,ilhd->iphd", image_low, grad_pooled, preferred_element_type=jnp.float32
    )
    grad_probs = jnp.einsum(
        "ilhd,iphd->ihlp", grad_pooled, image_values, preferred_element_type=jnp.float32
    )
    delta = jnp.sum(image_probs * grad_probs, axis=-1, keepdims=True)
    grad_scores = (image_probs * (grad_probs - delta)).astype(jnp.bfloat16)
    grad_latent = (
        jnp.einsum("ihlp,iphd->lhd", grad_scores, image_keys, preferred_element_type=jnp.float32)
        * factor
    )
    grad_keys = (
        jnp.einsum("ihlp,lhd->iphd", grad_scores, slotted, preferred_element_type=jnp.float32)
        * factor
    )
    grad_keyvals = jnp.stack(
        [grad_keys.reshape(images, patches, -1), grad_values.reshape(images, patches, -1)], axis=2
    ).astype(jnp.bfloat16)
    kv_grad = jnp.einsum(
        "ipc,ipkd->ckd", features, grad_keyvals, preferred_element_type=jnp.float32
    )
    slot_grad = grad_latent.reshape(n_model, per_model, -1)
    query_grad = jnp.stack(
        [
            lax.dynamic_index_in_dim(slot_grad, (place - m) % n_model, 0, keepdims=False)
            for m in range(n_model)
        ],
        axis=1,
    ).reshape(latents, -1)
    gains = jnp.stack([norm1_gain_grad, norm2_gain_grad]).reshape(2, n_model, -1)
    own = 0.0
    for step in range(n_model):
        chunk = lax.dynamic_index_in_dim(gains, (place + step) % n_model, 1, keepdims=False)
        own = own + (chunk if step == 0 else shift(chunk, step, n_model))
    pieces = [
        piece.astype(jnp.bfloat16).reshape(n_data, -1)
        for piece in (
            kv_grad,
            out_grad,
            query_grad,
            own[0],
            own[1],
            attn_gain_grad,
            ffn_gain_grad,
        )
    ]
    packed = jnp.concatenate(pieces, axis=1)
    packed = jnp.pad(packed, ((0, 0), (0, -packed.shape[1] % 2048))).reshape(n_data, -1, 128)
    packed, outputs = lax.optimization_barrier((packed, outputs))
    packed = lax.psum_scatter(packed, "dp", scatter_dimension=0, tiled=True)
    packed = packed.reshape(-1).astype(jnp.float32)
    split = []
    begin = 0
    for piece in pieces:
        split.append(packed[begin : begin + piece.shape[1]])
        begin += piece.shape[1]
    return (
        jnp.stack(outputs)[:, :, None, :],
        jnp.stack(token_grads)[:, :, None, :],
        split[2].reshape(latent_queries.shape),
        split[0].reshape(image_kv_weight.shape),
        split[1].reshape(image_out_weight.shape),
        split[3],
        attn_in_grad,
        split[5],
        attn_out_grad,
        split[4],
        ffn_up_grad,
        split[6],
        ffn_down_grad,
    )


def solution(mesh):
    placed = (
        P("dp", None, "mp", None),
        P("dp", None),
        P(),
        P("dp", None, None),
        P("dp", "mp"),
        P("dp", None, "mp"),
        P(("mp", "dp"), None),
        P(),
        P("dp", None, "mp"),
        P(("mp", "dp")),
        P(("mp", "dp"), None),
        P(),
        P("dp", "mp"),
        P(("mp", "dp")),
        P(("mp", "dp"), None),
        P("dp", None, "mp", None),
    )

    return jax.shard_map(
        per_device,
        mesh=mesh,
        in_specs=placed,
        out_specs=(
            P("dp", None, "mp", None),
            P("dp", None, "mp", None),
            P("dp", "mp"),
            P("dp", None, "mp"),
            P(("mp", "dp"), None),
            P(("mp", "dp")),
            P("dp", None, "mp"),
            P(("mp", "dp")),
            P(("mp", "dp"), None),
            P(("mp", "dp")),
            P("dp", "mp"),
            P(("mp", "dp")),
            P(("mp", "dp"), None),
        ),
        check_vma=False,
    )
```

```python
import jax
import jax.numpy as jnp
from jax import lax
from jax.sharding import PartitionSpec as P

D = 2048
HD = 64
FF = 8192


EPS = 1e-05
GAMMA = 0.4
SCALE_BASE = 512.0
NEG = -1e30
ROOT_HALF = 0.7071067811865476
INV_ROOT_TAU = 0.3989422804014327


def doc_positions(segments):
    index = jnp.arange(segments.shape[0], dtype=jnp.int32)
    starts = jnp.concatenate([jnp.ones((1,), dtype=bool), segments[1:] != segments[:-1]])
    first = lax.cummax(jnp.where(starts, index, 0), axis=0)
    return (index - first).astype(jnp.float32)


def rotary_tables(places, head_size):
    half = head_size // 2
    steps = jnp.arange(half, dtype=jnp.float32)
    freqs = 10000.0 ** (-2.0 * steps / head_size)
    angles = places[:, None] * freqs[None, :]
    zeta = (2.0 * steps / head_size + GAMMA) / (1.0 + GAMMA)
    decay = jnp.exp(jnp.log(zeta)[None, :] * places[:, None] / SCALE_BASE)
    return (jnp.cos(angles), jnp.sin(angles), jnp.concatenate([decay, decay], axis=-1))


def rotate(values, cosine, sine):
    half = values.shape[-1] // 2
    first = values[..., :half]
    second = values[..., half:]
    cosine = cosine[:, None, :]
    sine = sine[:, None, :]
    return jnp.concatenate(
        [first * cosine - second * sine, second * cosine + first * sine], axis=-1
    )


def gelu_slope(values):
    return (
        0.5 * (1.0 + lax.erf(values * ROOT_HALF))
        + values * jnp.exp(-0.5 * values * values) * INV_ROOT_TAU
    )


def row_norm(values):
    centre = values - jnp.mean(values, axis=-1, keepdims=True)
    scale_back = lax.rsqrt(jnp.mean(centre * centre, axis=-1, keepdims=True) + EPS)
    return (centre * scale_back, scale_back)


def row_norm_back(grad_out, normed, scale_back, gain):
    scaled = grad_out * gain
    gain_grad = jnp.sum(grad_out * normed, axis=0)
    grad_in = scale_back * (
        scaled
        - jnp.mean(scaled, axis=-1, keepdims=True)
        - normed * jnp.mean(scaled * normed, axis=-1, keepdims=True)
    )
    return (grad_in, gain_grad)


def shift(values, step, size):
    return lax.ppermute(values, "mp", [(i, (i + step) % size) for i in range(size)])


def sum_slots(values, size):
    total = values
    for step in range(1, size):
        total = total + jnp.roll(shift(values, step, size), step, axis=-2)
    return total


def gather_slots(shard, size):
    if size != 4:
        return jnp.concatenate(
            [shard] + [shift(shard, step, size) for step in range(1, size)], axis=0
        )
    place = lax.axis_index("mp")
    across = lax.ppermute(shard, "mp", [(0, 2), (1, 3), (2, 0), (3, 1)])
    up = lax.ppermute(shard, "mp", [(0, 1), (1, 2), (2, 3)])
    down = lax.ppermute(shard, "mp", [(1, 0), (2, 1), (3, 2)])
    ends = lax.ppermute(across, "mp", [(2, 3), (1, 0)])
    first = jnp.where(place == 0, ends, up)
    third = jnp.where(place == 3, ends, down)
    return jnp.concatenate([shard, first, across, third], axis=0)


def scatter_slots(partial, size, after=()):
    rows = partial.shape[0] // size
    parts = [partial[k * rows : (k + 1) * rows] for k in range(size)]
    low = [part.astype(jnp.bfloat16) for part in parts]
    if size != 4:
        total = parts[0]
        for step in range(1, size):
            total = total + shift(low[step], size - step, size).astype(jnp.float32)
        return total
    place = lax.axis_index("mp")
    ends = lax.ppermute(jnp.where(place == 0, low[1], low[3]), "mp", [(0, 1), (3, 2)])
    down = lax.ppermute(low[1], "mp", [(1, 0), (2, 1), (3, 2)])
    up = lax.ppermute(low[3], "mp", [(0, 1), (1, 2), (2, 3)])
    across = lax.ppermute(
        (parts[2] + ends.astype(jnp.float32)).astype(jnp.bfloat16),
        "mp",
        [(0, 2), (1, 3), (2, 0), (3, 1)],
    )
    down, up, across, _ = lax.optimization_barrier((down, up, across, after))
    return (
        parts[0]
        + down.astype(jnp.float32)
        + up.astype(jnp.float32)
        + across.astype(jnp.float32)
    )


def split_norm(values, width, size):
    rows = values.shape[0]
    sums = jnp.stack([jnp.sum(values, axis=-1), jnp.sum(values * values, axis=-1)])
    sums = sum_slots(sums.reshape(2, size, rows // size), size).reshape(2, rows)
    mean = sums[0] / width
    scale_back = lax.rsqrt(sums[1] / width - mean * mean + EPS)
    return ((values - mean[:, None]) * scale_back[:, None], scale_back[:, None])


def split_norm_back(grad_out, normed, scale_back, gain, width, size):
    rows = grad_out.shape[0]
    scaled = grad_out * gain
    gain_grad = jnp.sum(grad_out * normed, axis=0)
    sums = jnp.stack([jnp.sum(scaled, axis=-1), jnp.sum(scaled * normed, axis=-1)])
    sums = sum_slots(sums.reshape(2, size, rows // size), size).reshape(2, rows) / width
    grad_in = scale_back * (scaled - sums[0][:, None] - normed * sums[1][:, None])
    return (grad_in, gain_grad)


def score_block(query, key, allowed, factor):
    scores = jnp.einsum("qhd,khd->hqk", query, key, preferred_element_type=jnp.float32) * factor
    return jnp.where(allowed[None], scores, NEG)


def attend_forward(query, key, value, allowed):
    factor = query.shape[2] ** (-0.5)
    scores = score_block(query, key, allowed, factor)
    peak = jnp.max(scores, axis=-1, keepdims=True)
    expo = jnp.exp(scores - peak)
    denom = jnp.sum(expo, axis=-1, keepdims=True)
    probs = (expo / denom).astype(jnp.bfloat16)
    outputs = jnp.einsum("hqk,khd->qhd", probs, value, preferred_element_type=jnp.float32)
    return (outputs, peak + jnp.log(denom))


def attend_backward(query, key, value, allowed, totals, grad_out):
    factor = query.shape[2] ** (-0.5)
    scores = score_block(query, key, allowed, factor)
    probs = jnp.where(allowed[None], jnp.exp(scores - totals), 0.0)
    grad_value = jnp.einsum(
        "hqk,qhd->khd", probs.astype(jnp.bfloat16), grad_out, preferred_element_type=jnp.float32
    )
    grad_probs = jnp.einsum("qhd,khd->hqk", grad_out, value, preferred_element_type=jnp.float32)
    delta = jnp.sum(probs * grad_probs, axis=-1, keepdims=True)
    grad_scores = (probs * (grad_probs - delta)).astype(jnp.bfloat16)
    grad_query = (
        jnp.einsum("hqk,khd->qhd", grad_scores, key, preferred_element_type=jnp.float32) * factor
    )
    grad_key = (
        jnp.einsum("hqk,qhd->khd", grad_scores, query, preferred_element_type=jnp.float32) * factor
    )
    return (grad_query, grad_key, grad_value)


def to_slots(values, place, size):
    columns = values.reshape(-1, size).T
    return jnp.concatenate(
        [
            lax.dynamic_index_in_dim(columns, (place - k) % size, 0, keepdims=False)
            for k in range(size)
        ]
    )


def gather_rows(values):
    return lax.all_gather(values, "dp", axis=0, tiled=True)


def scatter_rows(values):
    return lax.psum_scatter(
        values.astype(jnp.bfloat16), "dp", scatter_dimension=0, tiled=True
    ).astype(jnp.float32)


class Row:
    pass


def per_device(
    tokens,
    segment_ids,
    image_blocks,
    features,
    latent_queries,
    image_kv_weight,
    image_out_weight,
    norm1_gain,
    attn_in_weight,
    attn_norm_gain,
    attn_out_weight,
    norm2_gain,
    ffn_up_weight,
    ffn_norm_gain,
    ffn_down_weight,
    cotangent,
):
    n_model = lax.axis_size("mp")
    n_data = lax.axis_size("dp")
    place = lax.axis_index("mp")
    data_index = lax.axis_index("dp")
    micro, shard_rows, _, width = tokens.shape
    row_length = shard_rows * n_model
    gain_one = norm1_gain.astype(jnp.float32)
    gain_two = norm2_gain.astype(jnp.float32)
    n_query = latent_queries.shape[0]

    columns = latent_queries.shape[1]
    query_size = n_query * columns
    small = jnp.concatenate([latent_queries.reshape(-1), attn_norm_gain, ffn_norm_gain])
    small = jnp.pad(small, (0, -small.shape[0] % (16 * columns))).reshape(-1, columns)
    kv_rows = image_kv_weight.size // columns
    out_rows = image_out_weight.size // columns
    pack = lax.all_gather(
        jnp.concatenate(
            [image_kv_weight.reshape(-1, columns), image_out_weight.reshape(-1, columns), small]
        ),
        "dp",
        axis=0,
        tiled=True,
    ).reshape(n_data, -1, columns)
    kv_weight = pack[:, :kv_rows].reshape(-1, 2, columns)
    out_weight = pack[:, kv_rows : kv_rows + out_rows].reshape(-1, width)
    small = pack[:, kv_rows + out_rows :].reshape(n_data, -1)
    queries = small[:, :query_size].reshape(n_data * n_query, -1)
    attn_end = query_size + attn_norm_gain.shape[0]
    attn_gain = small[:, query_size:attn_end].reshape(-1).astype(jnp.float32)
    ffn_gain = small[:, attn_end : attn_end + ffn_norm_gain.shape[0]].reshape(-1)
    ffn_gain = ffn_gain.astype(jnp.float32)
    attn_in = gather_rows(attn_in_weight)
    attn_out = gather_rows(attn_out_weight)

    text = [tokens[r, :, 0, :] for r in range(micro)]
    text_in = [
        gather_slots(
            (row_norm(text[r].astype(jnp.float32))[0] * gain_one).astype(jnp.bfloat16), n_model
        )
        for r in range(micro)
    ]

    latents = queries.shape[0]
    per_model = latents // n_model
    images, patches = features.shape[:2]
    image_heads = queries.shape[1] // HD
    factor = HD ** (-0.5)
    slotted = jnp.concatenate(
        [
            lax.dynamic_index_in_dim(
                queries.reshape(per_model, n_model, -1), (place - k) % n_model, 1, keepdims=False
            )
            for k in range(n_model)
        ],
        axis=0,
    ).reshape(latents, image_heads, HD)
    keyvals = jnp.einsum(
        "ipc,ckd->ipkd", features, kv_weight, preferred_element_type=jnp.float32
    ).astype(jnp.bfloat16)
    image_keys = keyvals[:, :, 0].reshape(images, patches, image_heads, HD)
    image_values = keyvals[:, :, 1].reshape(images, patches, image_heads, HD)
    image_scores = (
        jnp.einsum("lhd,iphd->ihlp", slotted, image_keys, preferred_element_type=jnp.float32)
        * factor
    )
    image_expo = jnp.exp(image_scores - jnp.max(image_scores, axis=-1, keepdims=True))
    image_probs = image_expo / jnp.sum(image_expo, axis=-1, keepdims=True)
    image_low = image_probs.astype(jnp.bfloat16)
    pooled = (
        jnp.einsum("ihlp,iphd->ilhd", image_low, image_values, preferred_element_type=jnp.float32)
        .reshape(images, latents, -1)
        .astype(jnp.bfloat16)
    )
    embed_part = jnp.einsum(
        "ilc,cd->lid", pooled, out_weight, preferred_element_type=jnp.float32
    ).reshape(latents, images * width)
    own_embeds = scatter_slots(embed_part, n_model).astype(jnp.bfloat16)
    slot_embeds = gather_slots(own_embeds, n_model)
    slot_embeds, text_in = lax.optimization_barrier((slot_embeds, text_in))
    slot_embeds = slot_embeds.reshape(latents, images, width)
    all_embeds = lax.all_gather(slot_embeds, "dp", axis=0, tiled=False)
    grads_all = lax.all_gather(cotangent[:, :, 0, :], "mp", axis=0, tiled=False)
    ffn_up = gather_rows(ffn_up_weight)
    ffn_down = gather_rows(ffn_down_weight)
    total_images = n_data * images
    all_embeds = all_embeds.transpose(0, 2, 1, 3).reshape(total_images, latents, width)
    embeds_in = (row_norm(all_embeds.astype(jnp.float32))[0] * gain_one).astype(jnp.bfloat16)
    image_index = jnp.arange(total_images, dtype=jnp.int32)
    blocks_row = shard_rows // per_model

    index = jnp.arange(row_length, dtype=jnp.int32)
    position = to_slots(index, place, n_model)
    rows = []
    for r in range(micro):
        row = Row()
        blocks = lax.dynamic_index_in_dim(
            image_blocks, data_index * micro + r, 0, keepdims=False
        )
        selector = (blocks[:, None] == image_index[None, :]).astype(jnp.bfloat16)
        row.selector = selector
        is_text = jnp.repeat(blocks == total_images, per_model)[:, None]
        row.is_text = is_text
        placed = jnp.einsum(
            "bi,isd->bsd",
            selector,
            embeds_in.reshape(total_images, n_model * per_model, width),
            preferred_element_type=jnp.float32,
        ).astype(jnp.bfloat16)
        placed = (
            placed.reshape(blocks_row, n_model, per_model, width)
            .swapaxes(0, 1)
            .reshape(row_length, width)
        )
        own_placed = jnp.einsum(
            "bi,isd->bsd",
            selector,
            all_embeds[:, :per_model],
            preferred_element_type=jnp.float32,
        ).reshape(shard_rows, width)
        start = jnp.where(is_text, text[r].astype(jnp.float32), own_placed)
        row.start = start
        row.input1 = jnp.where(jnp.tile(is_text, (n_model, 1)), text_in[r], placed)
        segments = to_slots(segment_ids[r], place, n_model)
        places = to_slots(doc_positions(segment_ids[r]), place, n_model)
        row.allowed = (position[:, None] >= position[None, :]) & (
            segments[:, None] == segments[None, :]
        )
        cosine, sine, decay = rotary_tables(places, HD)
        row.tables = (cosine, sine, decay[:, None, :])
        rows.append(row)

    local_heads = attn_in.shape[2] // HD
    outputs = []
    for r in range(micro):
        row = rows[r]
        cosine, sine, decay = row.tables
        mixed = jnp.einsum(
            "lc,ckd->lkd", row.input1, attn_in, preferred_element_type=jnp.float32
        )
        row.query = (
            rotate(mixed[:, 0].reshape(row_length, local_heads, HD), cosine, sine) * decay
        ).astype(jnp.bfloat16)
        row.key = (
            rotate(mixed[:, 1].reshape(row_length, local_heads, HD), cosine, sine) / decay
        ).astype(jnp.bfloat16)
        row.value = mixed[:, 2].reshape(row_length, local_heads, HD).astype(jnp.bfloat16)
        attended, row.totals = attend_forward(
            row.query, row.key, row.value, row.allowed
        )
        row.normed_a, row.back_a = split_norm(
            attended.reshape(row_length, -1), D, n_model
        )
        row.sub_attn = (row.normed_a * attn_gain).astype(jnp.bfloat16)
        part = jnp.dot(row.sub_attn, attn_out, preferred_element_type=jnp.float32)
        later = [other.input1 for other in rows[r + 1 :]]
        before = [other.ready for other in rows[:r]]
        part, later, _ = lax.optimization_barrier((part, later, before))
        for other, value in zip(rows[r + 1 :], later):
            other.input1 = value
        if r == micro - 1:
            _, grads_all = lax.optimization_barrier((part, grads_all))
        earlier = [other.hidden for other in rows[:r]]
        row.middle = row.start + scatter_slots(part, n_model, earlier)
        second = row.middle.astype(jnp.bfloat16).astype(jnp.float32)
        row.normed2, row.back2 = row_norm(second)
        row.ready = (row.normed2 * gain_two).astype(jnp.bfloat16)
        row.input2 = gather_slots(row.ready, n_model)
        row.hidden = jnp.dot(row.input2, ffn_up, preferred_element_type=jnp.float32)
    branch = [
        jnp.concatenate(
            [
                lax.dynamic_index_in_dim(grads_all, (place - k) % n_model, 0, keepdims=False)[r]
                for k in range(n_model)
            ],
            axis=0,
        )
        for r in range(micro)
    ]
    ffn_gain_grad = 0.0
    attn_gain_grad = 0.0
    norm2_gain_grad = 0.0
    norm1_gain_grad = 0.0
    for r in range(micro):
        row = rows[r]
        row.normed_f, row.back_f = split_norm(
            jax.nn.gelu(row.hidden, approximate=False), FF, n_model
        )
        row.sub_ffn = (row.normed_f * ffn_gain).astype(jnp.bfloat16)
        grad_sub = jnp.einsum(
            "ld,fd->lf", branch[r], ffn_down, preferred_element_type=jnp.float32
        )
        grad_active, gain_part = split_norm_back(
            grad_sub, row.normed_f, row.back_f, ffn_gain, FF, n_model
        )
        ffn_gain_grad = ffn_gain_grad + gain_part
        row.grad_hidden = (grad_active * gelu_slope(row.hidden)).astype(jnp.bfloat16)
        grad_input2 = jnp.einsum(
            "lf,cf->lc", row.grad_hidden, ffn_up, preferred_element_type=jnp.float32
        )
        later = [other.input2 for other in rows[r + 1 :]]
        before = [other.landed for other in rows[:r]]
        grad_input2, later, _ = lax.optimization_barrier((grad_input2, later, before))
        for other, value in zip(rows[r + 1 :], later):
            other.input2 = value
        share, gain_part = row_norm_back(
            scatter_slots(grad_input2, n_model), row.normed2, row.back2, gain_two
        )
        norm2_gain_grad = norm2_gain_grad + gain_part
        row.grad_middle = cotangent[r, :, 0, :].astype(jnp.float32) + share
        row.landed = row.grad_middle.astype(jnp.bfloat16)
        row.grad_out = gather_slots(row.landed, n_model)

    def both(values):
        return jnp.concatenate(values, axis=0)

    down_part = jnp.einsum(
        "lf,ld->fd",
        both([row.sub_ffn for row in rows]),
        jnp.concatenate(branch, axis=0),
        preferred_element_type=jnp.float32,
    ).astype(jnp.bfloat16)
    up_part = jnp.einsum(
        "lc,lf->cf", both([row.input2 for row in rows]), both([row.grad_hidden for row in rows]), preferred_element_type=jnp.float32
    ).astype(jnp.bfloat16)
    _, rows[0].grad_out = lax.optimization_barrier((down_part, rows[0].grad_out))
    _, rows[-1].grad_out = lax.optimization_barrier((up_part, rows[-1].grad_out))
    ffn_down_grad = scatter_rows(down_part)
    ffn_up_grad = scatter_rows(up_part)
    attn_out_part = jnp.einsum(
        "lc,ld->cd", both([row.sub_attn for row in rows]), both([row.grad_out for row in rows]), preferred_element_type=jnp.float32
    ).astype(jnp.bfloat16)
    token_grads = []
    grad_table = jnp.zeros((per_model, total_images, width), jnp.float32)
    for r in range(micro):
        row = rows[r]
        cosine, sine, decay = row.tables
        grad_sub_attn = jnp.einsum(
            "ld,cd->lc", row.grad_out, attn_out, preferred_element_type=jnp.float32
        )
        grad_attended, gain_part = split_norm_back(
            grad_sub_attn, row.normed_a, row.back_a, attn_gain, D, n_model
        )
        attn_gain_grad = attn_gain_grad + gain_part
        grad_query, grad_key, grad_value = attend_backward(
            row.query,
            row.key,
            row.value,
            row.allowed,
            row.totals,
            grad_attended.astype(jnp.bfloat16).reshape(row_length, local_heads, HD),
        )
        row.grad_mixed = (
            jnp.stack(
                [
                    rotate(grad_query * decay, cosine, -sine),
                    rotate(grad_key / decay, cosine, -sine),
                    grad_value,
                ],
                axis=1,
            )
            .reshape(row_length, 3, -1)
            .astype(jnp.bfloat16)
        )
        before = [other.share for other in rows[:r]]
        mixed_late, _ = lax.optimization_barrier((row.grad_mixed, before))
        grad_input1 = jnp.einsum(
            "lkd,ckd->lc", mixed_late, attn_in, preferred_element_type=jnp.float32
        )
        if r < micro - 1:
            later = [other.grad_out for other in rows[r + 1 :]]
            grad_input1, later = lax.optimization_barrier((grad_input1, later))
            for other, value in zip(rows[r + 1 :], later):
                other.grad_out = value
        else:
            grad_input1, _ = lax.optimization_barrier((grad_input1, attn_out_part))
        normed1, back1 = row_norm(row.start)
        share, gain_part = row_norm_back(
            scatter_slots(grad_input1, n_model), normed1, back1, gain_one
        )
        row.share = share
        norm1_gain_grad = norm1_gain_grad + gain_part
        grad_start = row.grad_middle + share
        token_grads.append(jnp.where(row.is_text, grad_start, 0.0))
        grad_table = grad_table + jnp.einsum(
            "bi,bsd->sid",
            row.selector,
            grad_start.astype(jnp.bfloat16).reshape(blocks_row, per_model, width),
            preferred_element_type=jnp.float32,
        )
    attn_out_grad = scatter_rows(attn_out_part)
    attn_in_part = jnp.einsum(
        "lc,lkd->ckd",
        both([row.input1 for row in rows]),
        both([row.grad_mixed for row in rows]),
        preferred_element_type=jnp.float32,
    ).astype(jnp.bfloat16)
    attn_in_grad = scatter_rows(attn_in_part)

    for row in rows:
        late, _ = lax.optimization_barrier((row.sub_ffn, row.share))
        part = jnp.dot(late, ffn_down, preferred_element_type=jnp.float32)
        outputs.append((row.middle + scatter_slots(part, n_model)).astype(jnp.bfloat16))

    share_grad = lax.psum_scatter(
        grad_table.astype(jnp.bfloat16), "dp", scatter_dimension=1, tiled=True
    )
    embed_grad = gather_slots(share_grad.reshape(per_model, images * width), n_model).reshape(
        latents, images, width
    )
    out_grad = jnp.einsum("ilc,lid->cd", pooled, embed_grad, preferred_element_type=jnp.float32)
    grad_pooled = (
        jnp.einsum("lid,cd->ilc", embed_grad, out_weight, preferred_element_type=jnp.float32)
        .astype(jnp.bfloat16)
        .reshape(images, latents, image_heads, HD)
    )
    grad_values = jnp.einsum(
        "ihlp,ilhd->iphd", image_low, grad_pooled, preferred_element_type=jnp.float32
    )
    grad_probs = jnp.einsum(
        "ilhd,iphd->ihlp", grad_pooled, image_values, preferred_element_type=jnp.float32
    )
    delta = jnp.sum(image_probs * grad_probs, axis=-1, keepdims=True)
    grad_scores = (image_probs * (grad_probs - delta)).astype(jnp.bfloat16)
    grad_latent = (
        jnp.einsum("ihlp,iphd->lhd", grad_scores, image_keys, preferred_element_type=jnp.float32)
        * factor
    )
    grad_keys = (
        jnp.einsum("ihlp,lhd->iphd", grad_scores, slotted, preferred_element_type=jnp.float32)
        * factor
    )
    grad_keyvals = jnp.stack(
        [grad_keys.reshape(images, patches, -1), grad_values.reshape(images, patches, -1)], axis=2
    ).astype(jnp.bfloat16)
    kv_grad = jnp.einsum(
        "ipc,ipkd->ckd", features, grad_keyvals, preferred_element_type=jnp.float32
    )
    slot_grad = grad_latent.reshape(n_model, per_model, -1)
    query_grad = jnp.stack(
        [
            lax.dynamic_index_in_dim(slot_grad, (place - m) % n_model, 0, keepdims=False)
            for m in range(n_model)
        ],
        axis=1,
    ).reshape(latents, -1)
    gains = jnp.stack([norm1_gain_grad, norm2_gain_grad]).reshape(2, n_model, -1)
    own = 0.0
    for step in range(n_model):
        chunk = lax.dynamic_index_in_dim(gains, (place + step) % n_model, 1, keepdims=False)
        own = own + (chunk if step == 0 else shift(chunk, step, n_model))
    pieces = [
        piece.astype(jnp.bfloat16).reshape(n_data, -1)
        for piece in (
            kv_grad,
            out_grad,
            query_grad,
            own[0],
            own[1],
            attn_gain_grad,
            ffn_gain_grad,
        )
    ]
    packed = jnp.concatenate(pieces, axis=1)
    packed = jnp.pad(packed, ((0, 0), (0, -packed.shape[1] % 2048))).reshape(n_data, -1, 128)
    packed, outputs = lax.optimization_barrier((packed, outputs))
    packed = lax.psum_scatter(packed, "dp", scatter_dimension=0, tiled=True)
    packed = packed.reshape(-1).astype(jnp.float32)
    split = []
    begin = 0
    for piece in pieces:
        split.append(packed[begin : begin + piece.shape[1]])
        begin += piece.shape[1]
    return (
        jnp.stack(outputs)[:, :, None, :],
        jnp.stack(token_grads)[:, :, None, :],
        split[2].reshape(latent_queries.shape),
        split[0].reshape(image_kv_weight.shape),
        split[1].reshape(image_out_weight.shape),
        split[3],
        attn_in_grad,
        split[5],
        attn_out_grad,
        split[4],
        ffn_up_grad,
        split[6],
        ffn_down_grad,
    )


def solution(mesh):
    placed = (
        P("dp", None, "mp", None),
        P("dp", None),
        P(),
        P("dp", None, None),
        P("dp", "mp"),
        P("dp", None, "mp"),
        P(("mp", "dp"), None),
        P(),
        P("dp", None, "mp"),
        P(("mp", "dp")),
        P(("mp", "dp"), None),
        P(),
        P("dp", "mp"),
        P(("mp", "dp")),
        P(("mp", "dp"), None),
        P("dp", None, "mp", None),
    )

    return jax.shard_map(
        per_device,
        mesh=mesh,
        in_specs=placed,
        out_specs=(
            P("dp", None, "mp", None),
            P("dp", None, "mp", None),
            P("dp", "mp"),
            P("dp", None, "mp"),
            P(("mp", "dp"), None),
            P(("mp", "dp")),
            P("dp", None, "mp"),
            P(("mp", "dp")),
            P(("mp", "dp"), None),
            P(("mp", "dp")),
            P("dp", "mp"),
            P(("mp", "dp")),
            P(("mp", "dp"), None),
        ),
        check_vma=False,
    )
```
